32 devices in a mesh: dp: 4 (over x, core), section: 4 (over z), expert: 2 (over y).
Axes of the slice: x: 2, y: 2, z: 4, core: 2. Of those that a mesh axis runs over, the one named last changes fastest.
Arguments:
- tokens: bfloat16 [8192, 4096], P(('dp', 'section')), may hold values from -90 to 90
- w_query: bfloat16 [4096, 2048], P(None, 'expert'), may hold values from -0.09375 to 0.09375
- w_key: bfloat16 [4096, 1024], P(None, 'expert'), may hold values from -0.09375 to 0.09375
- w_value: bfloat16 [4096, 1024], P(None, 'expert'), may hold values from -0.09375 to 0.09375
- w_out: bfloat16 [2048, 4096], P('expert'), may hold values from -0.125 to 0.125
- w_gate: bfloat16 [2, 7168, 4096], P('expert', ('dp', 'section')), may hold values from -0.09375 to 0.09375
- w_up: bfloat16 [2, 7168, 4096], P('expert', ('dp', 'section')), may hold values from -0.09375 to 0.09375
- w_down: bfloat16 [2, 7168, 4096], P('expert', ('dp', 'section')), may hold values from -0.0625 to 0.0625
- route: int32 [128, 1], P(('dp', 'section')), may hold values from 0 to 1; in each aligned block of 8 rows (0 to 7, 8 to 15, ...) at most 5 rows name the same one
- old_out: bfloat16 [128, 64, 4096], P(('dp', 'section'), 'expert'), may hold values from -6 to 6
- cotangent: bfloat16 [8192, 4096], P(('dp', 'section')), may hold values from -6 to 6
Outputs:
- joined: bfloat16 [128, 64, 4096], P(('dp', 'section'), 'expert')
- divergence: float32 [128, 64], P(('dp', 'section'), 'expert')
- grad_out_t: float32 [4096, 2048], P(('dp', 'section'), 'expert')
The draws below stay inside these ranges and needn't reach their ends.
Inputs may be any that keep to these rules, and one draw needn't show every extreme that they name: `route`: blocks routed to experts 1 and above go to new experts. Among the 8 blocks of one replica no expert is named more than 5 times, and some replica names one expert exactly 5 times in every draw.
All inputs are finite; a program needn't handle non-finite values.
Results may differ from the reference program's by a relative error of at most 0.025.
Values may be sent and summed in bfloat16 or wider, within the bound.
A program may use at most 192 MiB of HBM per device.

```python
import math
import jax
import jax.numpy as jnp
import numpy as np
from jax import lax

D = 4096
HEADS = 16
KV_HEADS = 8
HEAD_DIM = 128
FFW = 7168
BLOCK = 64
SEQ = 512
EXPERTS = 2
OLD = 1
NB = 8
NBT = 128
TOKENS = 8192
CAP = 5
N_DP = 4
N_SECTION = 4


def draw_tokens(key, part):
    noise = jax.random.truncated_normal(jax.random.fold_in(key, 11), -6.0, 6.0, (TOKENS, D), jnp.float32)
    return noise.astype(jnp.bfloat16)


def strengthened(values, stream_key, source, target, blocks, factor):
    def block_of(axis_at):
        return (jnp.arange(values.shape[axis_at]) // (values.shape[axis_at] // blocks)).reshape((-1,) + (1,) * (values.ndim - 1 - axis_at))

    one_side = jax.random.permutation(stream_key, blocks)[block_of(target)]
    other_side = (block_of(target) + blocks // 2) % blocks
    return jnp.where((block_of(source) == one_side) | (block_of(source) == other_side), factor * values, values)


def levels(stream_key, shape, shards, low, largest):
    gain, own = 1.0, jax.random.fold_in(stream_key, 6)
    for position, shards_of in shards:
        heights = jnp.exp(jax.random.uniform(jax.random.fold_in(own, position), (shards_of,), jnp.float32, low / len(shards), largest / len(shards)))
        gain = gain * jnp.repeat(heights, shape[position] // shards_of).reshape([-1 if axis == position else 1 for axis in range(len(shape))])
    return gain


def deal_out(key, own, number, rows, count, top, reach, lean):
    order = jax.random.permutation(key, count)
    packed, ordinary = portions_of(count, rows * top, reach, lean, True), portions_of(count, rows * top, reach, lean, False)
    places = jnp.arange(count)

    def named(lengths, turn):
        used = int((lengths > 0).sum())
        fixed = max(1, used // 4)
        passed = fixed + (places - fixed + turn * (used - fixed)) % max(1, count - fixed)
        return jnp.zeros((count,), jnp.int32).at[order[jnp.where(places < fixed, places, passed)]].set(jnp.asarray(lengths, jnp.int32))

    lengths = jnp.where(number % 4 == 0, named(packed, number // 4), named(ordinary, number - number // 4 - 1))
    mixed = jax.random.permutation(jax.random.fold_in(own, 3), count)
    source_of, taker = mixed[0:count // 2 * 2:2], mixed[1:count // 2 * 2:2]
    margin = jnp.minimum(lengths[source_of] - 1, reach - lengths[taker]) // 2
    margin = jnp.where((source_of == order[0]) | (taker == order[0]) | (lengths[taker] == 0), 0, jnp.maximum(margin, 0))
    passed = jax.random.randint(jax.random.fold_in(own, 4), (count // 2,), 0, 1 << 20) % (margin + 1)
    lengths = lengths.at[source_of].add(-passed).at[taker].add(passed)
    items = jnp.searchsorted(jnp.cumsum(lengths), jnp.arange(rows * top), side="right").astype(jnp.int32)
    listing = items.reshape(top, rows).T
    listing = listing[jax.random.permutation(jax.random.fold_in(own, 1), rows)]
    turn = jax.random.randint(jax.random.fold_in(own, 2), (rows, 1), 0, top)
    return jnp.take_along_axis(listing, (jnp.arange(top)[None, :] + turn) % top, axis=1)


def portions_of(amount, total, reach, lean, full):
    weights = [(1 << 20) // math.isqrt(grade ** lean) + 1 for grade in range(1, amount + 1)]
    largest = reach if full else min(reach, max(-(-total // amount), total * weights[0] // sum(weights)))
    least = 1 if total - largest >= amount - 1 else 0
    given, rest = [largest] + [least] * (amount - 1), total - largest - least * (amount - 1)
    while rest > 0:
        movable = [i for i in range(1, amount) if given[i] < largest] or [i for i in range(1, amount) if given[i] < reach]
        whole, left = sum([weights[i] for i in movable]), rest
        for i in movable:
            extra = min(reach - given[i], max(1, left * weights[i] // whole), rest)
            given[i] = given[i] + extra
            rest = rest - extra
    return np.array(given)


def gaussian(own_key, shape, deviation, limit, cuts=(), held_as=jnp.bfloat16):
    array = deviation * jax.random.normal(own_key, shape, jnp.float32)
    if cuts:
        array = array * levels(own_key, shape, cuts, -0.22, 0.18)
    return jnp.clip(array, -limit, limit).astype(held_as)


def bell_draw_with(key, extent, spread, reach, split, heavy, dtype=jnp.bfloat16):
    entries = spread * jax.random.normal(key, extent, jnp.float32)
    if split:
        entries = entries * levels(key, extent, split, -0.22, 0.18)
    return jnp.clip(strengthened(entries, jax.random.fold_in(key, 3), *heavy), -reach, reach).astype(dtype)


def setup_inputs(seed: int = 0) -> dict:
    splits = jax.random.split(jax.random.key(seed), 12)
    tokens = draw_tokens(jax.random.fold_in(splits[11], 71), 0)
    w_query = gaussian(splits[1], (D, HEADS * HEAD_DIM), D ** -0.5, 0.09375, ((1, 2),))
    w_key = gaussian(splits[2], (D, KV_HEADS * HEAD_DIM), D ** -0.5, 0.09375, ((1, 2),))
    w_value = gaussian(splits[3], (D, KV_HEADS * HEAD_DIM), D ** -0.5, 0.09375, ((1, 2),))
    w_out = gaussian(splits[4], (HEADS * HEAD_DIM, D), (HEADS * HEAD_DIM) ** -0.5, 0.125, ((0, 2),))
    w_gate = gaussian(splits[5], (EXPERTS, FFW, D), D ** -0.5, 0.09375, ((0, 2), (1, 16)))
    w_up = gaussian(splits[6], (EXPERTS, FFW, D), D ** -0.5, 0.09375, ((0, 2), (1, 16)))
    w_down = gaussian(splits[7], (EXPERTS, FFW, D), FFW ** -0.5, 0.0625, ((0, 2), (1, 16)))
    route_keys = jax.random.split(jax.random.fold_in(splits[8], 1), NBT // NB)
    route_turns = jax.random.permutation(jax.random.fold_in(splits[8], 3), NBT // NB)
    route = jax.vmap(lambda own, number: deal_out(jax.random.fold_in(splits[8], 2), own, number, NB, EXPERTS, 1, CAP, 2))(route_keys, route_turns).reshape((NBT, 1))
    old_out = gaussian(splits[9], (NBT, BLOCK, D), 1.0, 6.0, ((0, 16), (1, 2)))
    cotangent = bell_draw_with(splits[10], (TOKENS, D), 1.0, 6.0, ((0, 16),), (0, 1, 16, 2.0))
    return {"tokens": tokens, "w_query": w_query, "w_key": w_key, "w_value": w_value, "w_out": w_out, "w_gate": w_gate, "w_up": w_up, "w_down": w_down, "route": route, "old_out": old_out, "cotangent": cotangent}


def attend_all(sequence, w_query, w_key, w_value):
    length = sequence.shape[0]
    group = HEADS // KV_HEADS
    queries = jnp.dot(sequence, w_query, preferred_element_type=jnp.float32).astype(jnp.bfloat16)
    keys = jnp.dot(sequence, w_key, preferred_element_type=jnp.float32).astype(jnp.bfloat16)
    values = jnp.dot(sequence, w_value, preferred_element_type=jnp.float32).astype(jnp.bfloat16)
    queries = queries.astype(jnp.float32).reshape(length, KV_HEADS, group, HEAD_DIM)
    keys = keys.astype(jnp.float32).reshape(length, KV_HEADS, HEAD_DIM)
    values = values.astype(jnp.float32).reshape(length, KV_HEADS, HEAD_DIM)
    scores = jnp.einsum('qkgd,skd->kgqs', queries, keys) * (1.0 / math.sqrt(HEAD_DIM))
    causal = jnp.arange(length)[:, None] >= jnp.arange(length)[None, :]
    scores = jnp.where(causal, scores, -jnp.inf)
    top = lax.optimization_barrier(jnp.max(scores, axis=-1, keepdims=True))
    weights = jnp.exp(scores - top)
    probs = (weights / lax.optimization_barrier(jnp.sum(weights, axis=-1, keepdims=True))).astype(jnp.bfloat16)
    mixed = jnp.einsum('kgqs,skd->qkgd', probs.astype(jnp.float32), values)
    return mixed.reshape(length, HEADS * HEAD_DIM).astype(jnp.bfloat16)

def expert_block(block_rows, expert, w_gate, w_up, w_down):
    slices = N_DP * N_SECTION
    width = FFW // slices
    gate_rows = lax.dynamic_index_in_dim(w_gate, expert, 0, keepdims=False)
    up_rows = lax.dynamic_index_in_dim(w_up, expert, 0, keepdims=False)
    down_rows = lax.dynamic_index_in_dim(w_down, expert, 0, keepdims=False)
    contract = (((1,), (1,)), ((), ()))
    gate = lax.dot_general(block_rows, gate_rows, contract, preferred_element_type=jnp.float32)
    lifted = lax.dot_general(block_rows, up_rows, contract, preferred_element_type=jnp.float32)
    active = (jax.nn.silu(gate) * lifted).astype(jnp.bfloat16)
    active = active.astype(jnp.float32).reshape(BLOCK, slices, width)
    down = down_rows.astype(jnp.float32).reshape(slices, width, D)
    partial_value = jnp.einsum('tsh,shd->std', active, down)
    partial_value = lax.optimization_barrier(partial_value.astype(jnp.bfloat16)).astype(jnp.float32)
    return lax.optimization_barrier(jnp.sum(partial_value, axis=0)).astype(jnp.bfloat16)

def reference(tokens, w_query, w_key, w_value, w_out, w_gate, w_up, w_down, route, old_out, cotangent):
    replicas = N_DP * N_SECTION
    sequences = tokens.reshape(replicas, SEQ, D)
    routes = route.reshape(replicas, NB)
    olds = old_out.reshape(replicas, NB, BLOCK, D)
    cotangents = cotangent.reshape(replicas, SEQ, D)

    def one_replica(total, item):
        sequence, seq_routes, seq_old, seq_cot = item
        heads_out = attend_all(sequence, w_query, w_key, w_value)
        attention = jnp.dot(heads_out, w_out, preferred_element_type=jnp.float32)
        hidden_in = (sequence.astype(jnp.float32) + attention).astype(jnp.bfloat16)
        blocks_in = hidden_in.reshape(NB, BLOCK, D)
        expert_out = lax.map(lambda pair: expert_block(pair[0], pair[1], w_gate, w_up, w_down), (blocks_in, seq_routes))
        joined = (blocks_in.astype(jnp.float32) + expert_out.astype(jnp.float32)).astype(jnp.bfloat16)
        gap = joined.astype(jnp.float32) - seq_old.astype(jnp.float32)
        fresh = (seq_routes >= OLD).astype(jnp.float32)
        divergence = 0.5 * lax.optimization_barrier(jnp.mean(gap * gap, axis=-1)) * fresh[:, None]
        term = jnp.dot(seq_cot.T, heads_out, preferred_element_type=jnp.float32)
        term = lax.optimization_barrier(term.astype(jnp.bfloat16)).astype(jnp.float32)
        return (total + term, (joined, divergence))
    start = jnp.zeros((D, HEADS * HEAD_DIM), jnp.float32)
    grad, (joined, divergence) = lax.scan(one_replica, start, (sequences, routes, olds, cotangents))
    return (joined.reshape(NBT, BLOCK, D), divergence.reshape(NBT, BLOCK), grad)
```

```python
import math

import jax
import jax.numpy as jnp
from jax import lax
from jax.sharding import Mesh
from jax.sharding import PartitionSpec as P

HEAD_DIM = 128
BLOCK = 64
GROUP = ("outer", "section")


def attend_local(tokens, w_query, w_key, w_value):
    length = tokens.shape[0]
    key_heads = w_key.shape[1] // HEAD_DIM
    group = w_query.shape[1] // w_key.shape[1]
    queries = jnp.dot(tokens, w_query, preferred_element_type=jnp.float32).astype(jnp.bfloat16)
    queries = queries.reshape(length, key_heads, group, HEAD_DIM)
    keys = jnp.dot(tokens, w_key, preferred_element_type=jnp.float32).astype(jnp.bfloat16)
    keys = keys.reshape(length, key_heads, HEAD_DIM)
    values = jnp.dot(tokens, w_value, preferred_element_type=jnp.float32).astype(jnp.bfloat16)
    values = values.reshape(length, key_heads, HEAD_DIM)
    scores = jnp.einsum("qkgd,skd->kgqs", queries, keys, preferred_element_type=jnp.float32)
    scores = scores * (1.0 / math.sqrt(HEAD_DIM))
    query_pos = lax.broadcasted_iota(jnp.int32, (length, length), 0)
    key_pos = lax.broadcasted_iota(jnp.int32, (length, length), 1)
    scores = jnp.where(query_pos >= key_pos, scores, -jnp.inf)
    top = jnp.max(scores, axis=-1, keepdims=True)
    weights = jnp.exp(scores - top)
    probs = (weights / jnp.sum(weights, axis=-1, keepdims=True)).astype(jnp.bfloat16)
    mixed = jnp.einsum("kgqs,skd->qkgd", probs, values, preferred_element_type=jnp.float32)
    return mixed.astype(jnp.bfloat16).reshape(length, key_heads * group * HEAD_DIM)


def routing_table(routes, experts, capacity):
    number = routes.shape[0]
    same = routes[:, None] == routes[None, :]
    earlier = lax.broadcasted_iota(jnp.int32, (number, number), 1) < lax.broadcasted_iota(
        jnp.int32, (number, number), 0
    )
    slot = jnp.sum((same & earlier).astype(jnp.int32), axis=1)
    expert_hit = routes[None, :] == lax.broadcasted_iota(jnp.int32, (experts, number), 0)
    slot_hit = slot[None, :] == lax.broadcasted_iota(jnp.int32, (capacity, number), 0)
    return (expert_hit[:, None, :] & slot_hit[None, :, :]).astype(jnp.bfloat16)


def swap(value, axis):
    return lax.ppermute(value, axis, [(0, 1), (1, 0)])


def both(value, axis=0):
    if lax.axis_size("pair") == 1:
        return value
    return jnp.concatenate([value, swap(value, "pair")], axis=axis)


def pick(blocks, table):
    rows = jnp.einsum("cb,brd->crd", table, blocks, preferred_element_type=jnp.float32)
    return rows.astype(jnp.bfloat16)


def wo_gradient(cotangent, heads_out):
    length, width = cotangent.shape
    outer, pair = lax.axis_size("outer"), lax.axis_size("pair")
    parts = cotangent.reshape(length, outer, pair, width // (outer * pair))
    mine = lax.axis_index("pair")

    def part(number):
        return lax.dynamic_index_in_dim(parts, number, 2, keepdims=False).reshape(length, width // pair)

    left = part(mine)
    if pair == 2:
        left = jnp.concatenate([left, swap(part(1 - mine), "pair")], axis=0)
    term = lax.dot_general(
        left, both(heads_out), (((0,), (0,)), ((), ())), preferred_element_type=jnp.float32
    ).astype(jnp.bfloat16)
    return lax.psum_scatter(term, GROUP, scatter_dimension=0, tiled=True).astype(jnp.float32)


def per_device(
    tokens, w_query, w_key, w_value, w_out, w_gate, w_up, w_down, route, old_out, cotangent
):
    experts = lax.axis_size("expert")
    own = lax.axis_index("expert")
    length, width = tokens.shape
    blocks = length // BLOCK
    piece_rows = BLOCK // experts
    capacity = max(2, blocks // experts + 1)
    old_count = experts - max(1, experts // 4)
    routes = route[:, 0]
    table = routing_table(routes, experts, capacity)
    own_table = lax.dynamic_index_in_dim(table, own, 0, keepdims=False)
    token_rows = pick(tokens.reshape(blocks, BLOCK, width), own_table)

    heads_out = attend_local(tokens, w_query, w_key, w_value)
    head_blocks = heads_out.reshape(blocks, BLOCK, heads_out.shape[1])

    def project(rows):
        return jnp.dot(
            rows.reshape(-1, rows.shape[-1]), w_out, preferred_element_type=jnp.float32
        ).reshape(rows.shape[:-1] + (width,))

    if experts == 2:
        half = capacity * BLOCK // 2
        peer_table = lax.dynamic_index_in_dim(table, 1 - own, 0, keepdims=False)
        outgoing = project(pick(head_blocks, peer_table)).astype(jnp.bfloat16).reshape(-1, width)
        kept = project(pick(head_blocks, own_table)).reshape(-1, width)
        kept = kept + token_rows.reshape(-1, width).astype(jnp.float32)
        first = (kept[:half] + swap(outgoing[:half], "expert").astype(jnp.float32)).astype(jnp.bfloat16)
        second = (kept[half:] + swap(outgoing[half:], "expert").astype(jnp.float32)).astype(jnp.bfloat16)
    else:
        half = capacity * BLOCK // 2
        rows = jnp.einsum("jcb,brd->jcrd", table, head_blocks, preferred_element_type=jnp.float32)
        outgoing = project(rows.astype(jnp.bfloat16)).astype(jnp.bfloat16)
        total = lax.psum_scatter(outgoing, "expert", scatter_dimension=0, tiled=True)[0]
        total = (token_rows.astype(jnp.float32) + total.astype(jnp.float32)).astype(jnp.bfloat16)
        total = total.reshape(-1, width)
        first, second = total[:half], total[half:]

    gradient = wo_gradient(cotangent, heads_out)
    gate_rows, up_rows, down_rows = both(w_gate[0]), both(w_up[0]), both(w_down[0])
    contract = (((1,), (1,)), ((), ()))

    def expert(top, bottom):
        rows = jnp.concatenate([top, bottom], axis=0)
        gate = lax.dot_general(rows, gate_rows, contract, preferred_element_type=jnp.float32)
        lifted = lax.dot_general(rows, up_rows, contract, preferred_element_type=jnp.float32)
        active = (jax.nn.silu(gate) * lifted).astype(jnp.bfloat16)
        return jnp.dot(active, down_rows, preferred_element_type=jnp.float32)

    outer, section = lax.axis_size("outer"), lax.axis_size("section")
    ring = []
    for line in range(outer):
        places = [line * section + place for place in range(section)]
        ring += places if line % 2 == 0 else places[::-1]
    count = len(ring)
    onward = [(ring[i], ring[(i + 1) % count]) for i in range(count)]
    backward = [(target, source) for source, target in onward]
    front, back = first, second
    sums = None
    for _ in range(count - 1):
        front = lax.ppermute(front, GROUP, onward)
        back = lax.ppermute(back, GROUP, backward)
        terms = expert(front, back)
        upper, lower = terms[:half], terms[half:]
        if sums is not None:
            upper = upper + lax.ppermute(sums[0], GROUP, onward).astype(jnp.float32)
            lower = lower + lax.ppermute(sums[1], GROUP, backward).astype(jnp.float32)
        sums = (upper.astype(jnp.bfloat16), lower.astype(jnp.bfloat16))
    terms = expert(first, second)
    upper = terms[:half] + lax.ppermute(sums[0], GROUP, onward).astype(jnp.float32)
    lower = terms[half:] + lax.ppermute(sums[1], GROUP, backward).astype(jnp.float32)
    expert_sum = jnp.concatenate([upper, lower], axis=0)
    hidden = jnp.concatenate([first, second], axis=0).astype(jnp.float32)
    whole = (hidden + expert_sum.astype(jnp.bfloat16).astype(jnp.float32)).astype(jnp.bfloat16)
    whole = whole.reshape(capacity, experts, piece_rows, width)
    if experts == 2:
        mine = lax.dynamic_index_in_dim(whole, own, 1, keepdims=False)
        theirs = swap(lax.dynamic_index_in_dim(whole, 1 - own, 1, keepdims=False), "expert")
        joined = jnp.einsum("cb,crd->brd", own_table, mine, preferred_element_type=jnp.float32)
        joined = joined + jnp.einsum("cb,crd->brd", peer_table, theirs, preferred_element_type=jnp.float32)
    else:
        returned = lax.all_to_all(
            whole.transpose(1, 0, 2, 3), "expert", split_axis=0, concat_axis=0, tiled=True
        )
        joined = jnp.einsum("jcb,jcrd->brd", table, returned, preferred_element_type=jnp.float32)
    joined = joined.astype(jnp.bfloat16)
    fresh = (routes >= old_count).astype(jnp.float32)
    gap = joined.astype(jnp.float32) - old_out.astype(jnp.float32)
    divergence = 0.5 * jnp.mean(gap * gap, axis=-1) * fresh[:, None]
    return (joined, divergence, gradient)


def order_of(routes, experts_first, capacity):
    number = routes.shape[0]
    certain = number - capacity
    same = routes[:, None] == routes[None, :]
    earlier = lax.broadcasted_iota(jnp.int32, (number, number), 1) < lax.broadcasted_iota(
        jnp.int32, (number, number), 0
    )
    slot = jnp.sum((same & earlier).astype(jnp.int32), axis=1)
    loose = slot >= certain
    rank = jnp.sum((loose[None, :] & earlier).astype(jnp.int32), axis=1)
    fixed = jnp.where(routes == experts_first, slot, capacity + slot)
    place = jnp.where(loose, certain + rank, fixed)
    hit = place[None, :] == lax.broadcasted_iota(jnp.int32, (number, number), 0)
    return hit


def gated(rows, gate, up):
    contract = (((1,), (1,)), ((), ()))
    pre = lax.dot_general(rows, gate, contract, preferred_element_type=jnp.float32)
    lifted = lax.dot_general(rows, up, contract, preferred_element_type=jnp.float32)
    return (jax.nn.silu(pre) * lifted).astype(jnp.bfloat16)


def lowered(actives, downs):
    total = None
    for active, down in zip(actives, downs):
        term = jnp.dot(active, down, preferred_element_type=jnp.float32)
        total = term if total is None else total + term
    return total


def two_experts(
    tokens, w_query, w_key, w_value, w_out, w_gate, w_up, w_down, route, old_out, cotangent
):
    own = lax.axis_index("expert")
    length, width = tokens.shape
    blocks = length // BLOCK
    piece = BLOCK // 2
    strip = piece // 2
    capacity = max(2, blocks // 2 + 1)
    certain = blocks - capacity
    free = blocks - 2 * certain
    routes = route[:, 0]
    outer, section = lax.axis_size("outer"), lax.axis_size("section")
    ring = []
    for line in range(outer):
        places = [line * section + place for place in range(section)]
        ring += places if line % 2 == 0 else places[::-1]
    count = len(ring)
    onward = [(ring[i], ring[(i + 1) % count]) for i in range(count)]
    backward = [(target, source) for source, target in onward]
    logical = lax.axis_index("outer") * section + lax.axis_index("section")
    ring_array = jnp.asarray(ring, jnp.int32)
    spot_of = [ring.index(i) for i in range(count)]
    spot = jnp.asarray(spot_of, jnp.int32)[logical]

    own_hit = order_of(routes, own, capacity)
    peer_hit = order_of(routes, 1 - own, capacity)
    own_table, peer_table = own_hit.astype(jnp.bfloat16), peer_hit.astype(jnp.bfloat16)
    sorted_routes = jnp.sum(jnp.where(own_hit, routes[None, :], 0), axis=1)
    loose_own = (sorted_routes[certain:capacity] == own).astype(jnp.float32)
    flags = jnp.broadcast_to(loose_own[None, :, None], (1, free, 128))
    shift = 1
    while shift < count:
        moved = lax.ppermute(flags, GROUP, [(ring[i], ring[(i + shift) % count]) for i in range(count)])
        flags = jnp.concatenate([flags, moved], axis=0)
        shift *= 2

    heads_out = attend_local(tokens, w_query, w_key, w_value)

    def mine_of(value, side):
        cut = value.reshape(blocks, 2, 2, strip, value.shape[-1])
        return lax.dynamic_index_in_dim(cut, side, 1, keepdims=False)

    def arranged(value, table):
        rows = jnp.einsum("pb,bfrd->fprd", table, value, preferred_element_type=jnp.float32)
        return rows.astype(jnp.bfloat16).reshape(2, blocks * strip, value.shape[-1])

    theirs = arranged(mine_of(heads_out, 1 - own), peer_table)
    parcel = [jnp.dot(theirs[i], w_out, preferred_element_type=jnp.float32).astype(jnp.bfloat16) for i in range(2)]
    got = [swap(parcel[i], "expert") for i in range(2)]
    kept = arranged(mine_of(heads_out, own), own_table)
    base = arranged(mine_of(tokens, own), own_table)
    hidden = []
    for i in range(2):
        value = jnp.dot(kept[i], w_out, preferred_element_type=jnp.float32)
        value = value + base[i].astype(jnp.float32) + got[i].astype(jnp.float32)
        hidden.append(value.astype(jnp.bfloat16))

    own_gate, own_up, own_down = w_gate[0], w_up[0], w_down[0]
    gates = [own_gate, swap(own_gate, "pair")]
    ups = [own_up, swap(own_up, "pair")]
    downs = [own_down, swap(own_down, "pair")]
    gate_away, up_away, down_away, parcel = lax.optimization_barrier((own_gate, own_up, own_down, parcel))
    gate_away, up_away, down_away = swap(gate_away, "expert"), swap(up_away, "expert"), swap(down_away, "expert")
    far_gates = [gate_away, swap(gate_away, "pair")]
    far_ups = [up_away, swap(up_away, "pair")]
    far_downs = [down_away, swap(down_away, "pair")]

    parts = cotangent.reshape(length, outer, 2, width // (outer * 2))
    core = lax.axis_index("pair")

    def part(number):
        return lax.dynamic_index_in_dim(parts, number, 2, keepdims=False).reshape(length, width // 2)

    left = jnp.concatenate([part(core), swap(part(1 - core), "pair")], axis=0)
    term = lax.dot_general(
        left, both(heads_out), (((0,), (0,)), ((), ())), preferred_element_type=jnp.float32
    ).astype(jnp.bfloat16)
    term = term.reshape(count, width // (2 * count), term.shape[1])
    middle = term.shape[2] // 2

    def share(away, side):
        place = ring_array[(spot + away) % count]
        block = lax.dynamic_index_in_dim(term, place, 0, keepdims=False)
        return block[:, :middle] if side == 0 else block[:, middle:]

    grads = [share(-1, 0), share(1, 1)]

    sure = certain * strip
    fronts, backs = [hidden[0]], [hidden[1]]
    sums = None

    def first_terms(top, bottom):
        rows = jnp.concatenate([top[:sure], bottom[:sure]], axis=0)
        return lowered([gated(rows, g, u) for g, u in zip(gates, ups)], downs)

    for step in range(1, count):
        fronts.append(lax.ppermute(fronts[-1], GROUP, onward))
        backs.append(lax.ppermute(backs[-1], GROUP, backward))
        moved = [lax.ppermute(grads[0], GROUP, onward), lax.ppermute(grads[1], GROUP, backward)]
        mine = [share(-1 - step, 0), share(1 + step, 1)]
        grads = [moved[i].astype(jnp.float32) + mine[i].astype(jnp.float32) for i in range(2)]
        if step < count - 1:
            grads = [value.astype(jnp.bfloat16) for value in grads]
        terms = first_terms(fronts[-1], backs[-1])
        upper, lower = terms[:sure], terms[sure:]
        if sums is not None:
            upper = upper + lax.ppermute(sums[0], GROUP, onward).astype(jnp.float32)
            lower = lower + lax.ppermute(sums[1], GROUP, backward).astype(jnp.float32)
        sums = (upper.astype(jnp.bfloat16), lower.astype(jnp.bfloat16))
    gradient = jnp.concatenate(grads, axis=1)
    terms = first_terms(hidden[0], hidden[1])
    sure_upper = terms[:sure] + lax.ppermute(sums[0], GROUP, onward).astype(jnp.float32)
    sure_lower = terms[sure:] + lax.ppermute(sums[1], GROUP, backward).astype(jnp.float32)

    rest = capacity * strip
    actives = {}
    own_masks = []
    for step in range(count):
        marks = [flags[step], flags[(count - step) % count]]
        for mark in marks:
            own_masks.append(jnp.concatenate([jnp.repeat(mark[:, :1], strip, axis=0), jnp.zeros((sure, 1), jnp.float32)], axis=0))

    def rest_actives(steps):
        pieces, masks = [], []
        for step in steps:
            pieces += [fronts[step][sure:], backs[step][sure:]]
            masks += own_masks[2 * step : 2 * step + 2]
        rows = jnp.concatenate(pieces, axis=0)
        mask = jnp.concatenate(masks, axis=0) > 0
        near = [jnp.where(mask, gated(rows, g, u), 0) for g, u in zip(gates, ups)]
        far = [jnp.where(mask, 0, gated(rows, g, u)) for g, u in zip(far_gates, far_ups)]
        for place, step in enumerate(steps):
            span = slice(2 * rest * place, 2 * rest * (place + 1))
            actives[step] = [value[span] for value in near + far]

    groups = [[1, 2, 3, 4], [5, 6], [7, 0]] if count == 8 else [[(i + 1) % count] for i in range(count)]
    for group in groups:
        rest_actives(group)
    every = downs + far_downs
    sums = None
    for step in list(range(1, count)) + [0]:
        terms = lowered(actives[step], every)
        upper, lower = terms[:rest], terms[rest:]
        if sums is not None:
            upper = upper + lax.ppermute(sums[0], GROUP, onward).astype(jnp.float32)
            lower = lower + lax.ppermute(sums[1], GROUP, backward).astype(jnp.float32)
        if step != 0:
            sums = (upper.astype(jnp.bfloat16), lower.astype(jnp.bfloat16))

    def finish(sides):
        value = jnp.stack(
            [jnp.concatenate([a, b], axis=0) for a, b in sides], axis=0
        )
        start = jnp.stack(hidden, axis=0).astype(jnp.float32)
        whole = (start + value.astype(jnp.bfloat16).astype(jnp.float32)).astype(jnp.bfloat16)
        return whole.reshape(2, blocks, strip, width)

    whole = finish([(sure_upper, upper), (sure_lower, lower)])
    joined = jnp.einsum("pb,fprd->bfrd", own_table, whole, preferred_element_type=jnp.float32)
    joined = joined.astype(jnp.bfloat16).reshape(blocks, piece, width)
    fresh = (routes >= 1).astype(jnp.float32)
    gap = joined.astype(jnp.float32) - old_out.astype(jnp.float32)
    divergence = 0.5 * jnp.mean(gap * gap, axis=-1) * fresh[:, None]
    return (joined, divergence, gradient)


def solution(mesh):
    sizes = mesh.shape
    pair = 2 if sizes["dp"] % 2 == 0 else 1
    body = two_experts if sizes["expert"] == 2 and pair == 2 else per_device
    split = Mesh(
        mesh.devices.reshape(sizes["dp"] // pair, pair, sizes["section"], sizes["expert"]),
        ("outer", "pair", "section", "expert"),
    )
    replicas = ("outer", "pair", "section")
    return jax.shard_map(
        body,
        mesh=split,
        in_specs=(
            P(replicas, None),
            P(None, "expert"),
            P(None, "expert"),
            P(None, "expert"),
            P("expert", None),
            P("expert", replicas, None),
            P("expert", replicas, None),
            P("expert", replicas, None),
            P(replicas, None),
            P(replicas, "expert", None),
            P(replicas, None),
        ),
        out_specs=(
            P(replicas, "expert", None),
            P(replicas, "expert"),
            P(replicas, "expert"),
        ),
        check_vma=False,
    )
```

```python
import functools
import math

import jax
import jax.numpy as jnp
from jax import lax
from jax.experimental import pallas as pl
from jax.experimental.pallas import tpu as pltpu
from jax.sharding import Mesh
from jax.sharding import PartitionSpec as P

HEAD_DIM = 128
BLOCK = 64
GROUP = ("outer", "section")


def attend_local(tokens, w_query, w_key, w_value):
    length = tokens.shape[0]
    key_heads = w_key.shape[1] // HEAD_DIM
    group = w_query.shape[1] // w_key.shape[1]
    queries = jnp.dot(tokens, w_query, preferred_element_type=jnp.float32).astype(jnp.bfloat16)
    queries = queries.reshape(length, key_heads, group, HEAD_DIM)
    keys = jnp.dot(tokens, w_key, preferred_element_type=jnp.float32).astype(jnp.bfloat16)
    keys = keys.reshape(length, key_heads, HEAD_DIM)
    values = jnp.dot(tokens, w_value, preferred_element_type=jnp.float32).astype(jnp.bfloat16)
    values = values.reshape(length, key_heads, HEAD_DIM)
    scores = jnp.einsum("qkgd,skd->kgqs", queries, keys, preferred_element_type=jnp.float32)
    scores = scores * (1.0 / math.sqrt(HEAD_DIM))
    query_pos = lax.broadcasted_iota(jnp.int32, (length, length), 0)
    key_pos = lax.broadcasted_iota(jnp.int32, (length, length), 1)
    scores = jnp.where(query_pos >= key_pos, scores, -jnp.inf)
    top = jnp.max(scores, axis=-1, keepdims=True)
    weights = jnp.exp(scores - top)
    probs = (weights / jnp.sum(weights, axis=-1, keepdims=True)).astype(jnp.bfloat16)
    mixed = jnp.einsum("kgqs,skd->qkgd", probs, values, preferred_element_type=jnp.float32)
    return mixed.astype(jnp.bfloat16).reshape(length, key_heads * group * HEAD_DIM)


def routing_table(routes, experts, capacity):
    number = routes.shape[0]
    same = routes[:, None] == routes[None, :]
    earlier = lax.broadcasted_iota(jnp.int32, (number, number), 1) < lax.broadcasted_iota(
        jnp.int32, (number, number), 0
    )
    slot = jnp.sum((same & earlier).astype(jnp.int32), axis=1)
    expert_hit = routes[None, :] == lax.broadcasted_iota(jnp.int32, (experts, number), 0)
    slot_hit = slot[None, :] == lax.broadcasted_iota(jnp.int32, (capacity, number), 0)
    return (expert_hit[:, None, :] & slot_hit[None, :, :]).astype(jnp.bfloat16)


def swap(value, axis):
    return lax.ppermute(value, axis, [(0, 1), (1, 0)])


def both(value, axis=0):
    if lax.axis_size("pair") == 1:
        return value
    return jnp.concatenate([value, swap(value, "pair")], axis=axis)


def pick(blocks, table):
    rows = jnp.einsum("cb,brd->crd", table, blocks, preferred_element_type=jnp.float32)
    return rows.astype(jnp.bfloat16)


def wo_gradient(cotangent, heads_out):
    length, width = cotangent.shape
    outer, pair = lax.axis_size("outer"), lax.axis_size("pair")
    parts = cotangent.reshape(length, outer, pair, width // (outer * pair))
    mine = lax.axis_index("pair")

    def part(number):
        return lax.dynamic_index_in_dim(parts, number, 2, keepdims=False).reshape(length, width // pair)

    left = part(mine)
    if pair == 2:
        left = jnp.concatenate([left, swap(part(1 - mine), "pair")], axis=0)
    term = lax.dot_general(
        left, both(heads_out), (((0,), (0,)), ((), ())), preferred_element_type=jnp.float32
    ).astype(jnp.bfloat16)
    return lax.psum_scatter(term, GROUP, scatter_dimension=0, tiled=True).astype(jnp.float32)


def per_device(
    tokens, w_query, w_key, w_value, w_out, w_gate, w_up, w_down, route, old_out, cotangent
):
    experts = lax.axis_size("expert")
    own = lax.axis_index("expert")
    length, width = tokens.shape
    blocks = length // BLOCK
    piece_rows = BLOCK // experts
    capacity = max(2, blocks // experts + 1)
    old_count = experts - max(1, experts // 4)
    routes = route[:, 0]
    table = routing_table(routes, experts, capacity)
    own_table = lax.dynamic_index_in_dim(table, own, 0, keepdims=False)
    token_rows = pick(tokens.reshape(blocks, BLOCK, width), own_table)

    heads_out = attend_local(tokens, w_query, w_key, w_value)
    head_blocks = heads_out.reshape(blocks, BLOCK, heads_out.shape[1])

    def project(rows):
        return jnp.dot(
            rows.reshape(-1, rows.shape[-1]), w_out, preferred_element_type=jnp.float32
        ).reshape(rows.shape[:-1] + (width,))

    if experts == 2:
        half = capacity * BLOCK // 2
        peer_table = lax.dynamic_index_in_dim(table, 1 - own, 0, keepdims=False)
        outgoing = project(pick(head_blocks, peer_table)).astype(jnp.bfloat16).reshape(-1, width)
        kept = project(pick(head_blocks, own_table)).reshape(-1, width)
        kept = kept + token_rows.reshape(-1, width).astype(jnp.float32)
        first = (kept[:half] + swap(outgoing[:half], "expert").astype(jnp.float32)).astype(jnp.bfloat16)
        second = (kept[half:] + swap(outgoing[half:], "expert").astype(jnp.float32)).astype(jnp.bfloat16)
    else:
        half = capacity * BLOCK // 2
        rows = jnp.einsum("jcb,brd->jcrd", table, head_blocks, preferred_element_type=jnp.float32)
        outgoing = project(rows.astype(jnp.bfloat16)).astype(jnp.bfloat16)
        total = lax.psum_scatter(outgoing, "expert", scatter_dimension=0, tiled=True)[0]
        total = (token_rows.astype(jnp.float32) + total.astype(jnp.float32)).astype(jnp.bfloat16)
        total = total.reshape(-1, width)
        first, second = total[:half], total[half:]

    gradient = wo_gradient(cotangent, heads_out)
    gate_rows, up_rows, down_rows = both(w_gate[0]), both(w_up[0]), both(w_down[0])
    contract = (((1,), (1,)), ((), ()))

    def expert(top, bottom):
        rows = jnp.concatenate([top, bottom], axis=0)
        gate = lax.dot_general(rows, gate_rows, contract, preferred_element_type=jnp.float32)
        lifted = lax.dot_general(rows, up_rows, contract, preferred_element_type=jnp.float32)
        active = (jax.nn.silu(gate) * lifted).astype(jnp.bfloat16)
        return jnp.dot(active, down_rows, preferred_element_type=jnp.float32)

    outer, section = lax.axis_size("outer"), lax.axis_size("section")
    ring = []
    for line in range(outer):
        places = [line * section + place for place in range(section)]
        ring += places if line % 2 == 0 else places[::-1]
    count = len(ring)
    onward = [(ring[i], ring[(i + 1) % count]) for i in range(count)]
    backward = [(target, source) for source, target in onward]
    front, back = first, second
    sums = None
    for _ in range(count - 1):
        front = lax.ppermute(front, GROUP, onward)
        back = lax.ppermute(back, GROUP, backward)
        terms = expert(front, back)
        upper, lower = terms[:half], terms[half:]
        if sums is not None:
            upper = upper + lax.ppermute(sums[0], GROUP, onward).astype(jnp.float32)
            lower = lower + lax.ppermute(sums[1], GROUP, backward).astype(jnp.float32)
        sums = (upper.astype(jnp.bfloat16), lower.astype(jnp.bfloat16))
    terms = expert(first, second)
    upper = terms[:half] + lax.ppermute(sums[0], GROUP, onward).astype(jnp.float32)
    lower = terms[half:] + lax.ppermute(sums[1], GROUP, backward).astype(jnp.float32)
    expert_sum = jnp.concatenate([upper, lower], axis=0)
    hidden = jnp.concatenate([first, second], axis=0).astype(jnp.float32)
    whole = (hidden + expert_sum.astype(jnp.bfloat16).astype(jnp.float32)).astype(jnp.bfloat16)
    whole = whole.reshape(capacity, experts, piece_rows, width)
    if experts == 2:
        mine = lax.dynamic_index_in_dim(whole, own, 1, keepdims=False)
        theirs = swap(lax.dynamic_index_in_dim(whole, 1 - own, 1, keepdims=False), "expert")
        joined = jnp.einsum("cb,crd->brd", own_table, mine, preferred_element_type=jnp.float32)
        joined = joined + jnp.einsum("cb,crd->brd", peer_table, theirs, preferred_element_type=jnp.float32)
    else:
        returned = lax.all_to_all(
            whole.transpose(1, 0, 2, 3), "expert", split_axis=0, concat_axis=0, tiled=True
        )
        joined = jnp.einsum("jcb,jcrd->brd", table, returned, preferred_element_type=jnp.float32)
    joined = joined.astype(jnp.bfloat16)
    fresh = (routes >= old_count).astype(jnp.float32)
    gap = joined.astype(jnp.float32) - old_out.astype(jnp.float32)
    divergence = 0.5 * jnp.mean(gap * gap, axis=-1) * fresh[:, None]
    return (joined, divergence, gradient)


MESH_ID = pl.DeviceIdType.MESH
NT = (((1,), (1,)), ((), ()))


def order_of(routes, first, capacity):
    number = routes.shape[0]
    certain = number - capacity
    same = routes[:, None] == routes[None, :]
    earlier = lax.broadcasted_iota(jnp.int32, (number, number), 1) < lax.broadcasted_iota(
        jnp.int32, (number, number), 0
    )
    slot = jnp.sum((same & earlier).astype(jnp.int32), axis=1)
    loose = slot >= certain
    rank = jnp.sum((loose[None, :] & earlier).astype(jnp.int32), axis=1)
    fixed = jnp.where(routes == first, slot, capacity + slot)
    place = jnp.where(loose, certain + rank, fixed)
    return place[None, :] == lax.broadcasted_iota(jnp.int32, (number, number), 0)


def moe_kernel(
    sure, loose, half,
    hidden_ref, gate_ref, up_ref, down_ref, term_ref, near_ref, keep_ref,
    out_ref, grad_ref, far_ref, slot_ref,
    near_w, rows, sums, stage, stage_rest, part, far_act, act, gate_tile, up_tile, grad_in, term_in, grad_out, total_grad,
    row_send, row_recv, sum_send, sum_recv, grad_send, grad_recv, rest_send, rest_recv,
    pair_send, pair_recv, far_send, far_recv, fwd_send, fwd_recv, local_sem, free_sem,
):
    outer, section = lax.axis_size("outer"), lax.axis_size("section")
    count = outer * section
    x, z = lax.axis_index("outer"), lax.axis_index("section")
    spot = x * (count - 1) + z * (1 - 2 * x)

    def at(place):
        line = place // section
        within = place % section
        return {"outer": line, "section": within * (1 - 2 * line) + (section - 1) * line}

    onward, backward = at((spot + 1) % count), at((spot + count - 1) % count)
    partner = {"pair": 1 - lax.axis_index("pair")}
    peer = {"expert": 1 - lax.axis_index("expert")}
    ways = (onward, backward)
    total_rows, width = hidden_ref.shape
    side = total_rows // 2
    rest = side - sure
    tile = half
    tiles = near_w.shape[1] * near_w.shape[2] // tile
    per = near_w.shape[2] // tile
    chunk = 512
    weights = (gate_ref, up_ref, down_ref)

    barrier = pltpu.get_barrier_semaphore()
    for target in (onward, backward, partner, peer):
        pl.semaphore_signal(barrier, inc=1, device_id=target, device_id_type=MESH_ID)
    pl.semaphore_wait(barrier, 4)

    def remote(source, target, send, recv, device):
        return pltpu.make_async_remote_copy(
            src_ref=source, dst_ref=target, send_sem=send, recv_sem=recv, device_id=device, device_id_type=MESH_ID
        )

    def span(way):
        return pl.ds(way * side, side)

    def row_copy(way, step):
        source = rows.at[step - 1, span(way)]
        return remote(source, rows.at[step, span(way)], row_send.at[way, step], row_recv.at[way, step], ways[way])

    def first_row_copy(way):
        return remote(hidden_ref.at[span(way)], rows.at[1, span(way)], row_send.at[way, 1], row_recv.at[way, 1], ways[way])

    def grad_copy(way, step, source):
        return remote(source, slot_ref.at[way, step], grad_send.at[way, step], grad_recv.at[way, step], ways[way])

    def sum_copy(way, step):
        here = pl.ds(way * sure, sure)
        return remote(stage.at[step % 2, here], sums.at[step, here], sum_send.at[way, step], sum_recv.at[way, step], ways[way])

    def rest_copy(way, step):
        here = pl.ds(way * rest, rest)
        there = pl.ds(sure + way * rest, rest)
        return remote(
            stage_rest.at[step % 2, here], rows.at[step, there], rest_send.at[way, step], rest_recv.at[way, step], ways[way]
        )

    def far_copy(which):
        return remote(weights[which], far_ref.at[which, 0], far_send.at[which], far_recv.at[which], peer)

    def forward_copy(which):
        return remote(far_ref.at[which, 0], far_ref.at[which, 1], fwd_send.at[which], fwd_recv.at[which], partner)

    def pair_copy(which):
        return remote(weights[which], near_w.at[which, 1], pair_send.at[which], pair_recv.at[which], partner)

    def local(source, target, place):
        return pltpu.make_async_copy(source, target, local_sem.at[place])

    for way in range(2):
        first_row_copy(way).start()
    for which in range(3):
        far_copy(which).start()
    grad_copy(0, 1, term_ref.at[0, count - 1]).start()
    grad_copy(1, 1, term_ref.at[1, 1]).start()
    loads = [local(weights[which], near_w.at[which, 0], which) for which in range(3)]
    loads.append(local(hidden_ref, rows.at[0], 3))
    for load in loads:
        load.start()
    for which in range(3):
        pair_copy(which).start()
    sums[0] = jnp.zeros_like(sums[0])
    for load in loads:
        load.wait()
    for which in range(3):
        pair_copy(which).wait_recv()

    def gradient_step(step):
        pulls = []
        for way in range(2):
            grad_copy(way, step, slot_ref.at[way, step]).wait_recv()
            pulls.append(local(slot_ref.at[way, step], grad_in.at[way], way))
            index = (2 * count - 1 - step) % count if way == 0 else (1 + step) % count
            pulls.append(local(term_ref.at[way, index], term_in.at[way], 2 + way))
        for pull in pulls:
            pull.start()
        for pull in pulls:
            pull.wait()
        for way in range(2):
            value = grad_in[way].astype(jnp.float32) + term_in[way].astype(jnp.float32)

            @pl.when(step < count - 1)
            def _():
                @pl.when(step >= 3)
                def _():
                    grad_copy(way, step - 1, grad_out.at[way, step % 2]).wait_send()

                grad_out[way, step % 2] = value.astype(jnp.bfloat16)
                grad_copy(way, step + 1, grad_out.at[way, step % 2]).start()

            @pl.when(step == count - 1)
            def _():
                total_grad[:, pl.ds(way * value.shape[1], value.shape[1])] = value

    def gated(value, gate, up):
        pre = lax.dot_general(value, gate, NT, preferred_element_type=jnp.float32)
        lifted = lax.dot_general(value, up, NT, preferred_element_type=jnp.float32)
        return pre * (1.0 / (1.0 + jnp.exp(-pre))) * lifted

    def near_step(step):
        slot = step % count

        def one(index, _):
            place = pl.ds(pl.multiple_of((index % per) * tile, tile), tile)
            value = gated(rows[slot], near_w[0, index // per, place], near_w[1, index // per, place])
            act[index] = value.astype(jnp.bfloat16)
            return 0

        lax.fori_loop(0, tiles, one, 0)

        @pl.when(step >= 2)
        def _():
            for way in range(2):
                sum_copy(way, step - 1).wait_recv()

        @pl.when(step >= 3)
        def _():
            for way in range(2):
                sum_copy(way, step - 2).wait_send()

        def two(index, _):
            columns = pl.ds(pl.multiple_of(index * chunk, chunk), chunk)
            total = None
            for number in range(tiles):
                place = pl.ds((number % per) * tile, tile)
                term = jnp.dot(
                    act[number], near_w[2, number // per, place, columns], preferred_element_type=jnp.float32
                )
                total = term if total is None else total + term
            before = sums[step - 1, :, columns].astype(jnp.float32)
            stage[step % 2, 0:sure, columns] = (total[0:sure] + before[0:sure]).astype(jnp.bfloat16)
            stage[step % 2, sure : 2 * sure, columns] = (total[total_rows - sure :] + before[sure:]).astype(jnp.bfloat16)
            mine = near_ref[slot]
            part[slot, 0:loose, columns] = jnp.where(
                mine[0:loose, 0:1] > 0, total[sure : sure + loose], 0.0
            ).astype(jnp.bfloat16)
            part[slot, loose : 2 * loose, columns] = jnp.where(
                mine[loose:, 0:1] > 0, total[side : side + loose], 0.0
            ).astype(jnp.bfloat16)
            return 0

        lax.fori_loop(0, width // chunk, two, 0)

    def far_step(low, high):
        def one(index, _):
            place = pl.ds(pl.multiple_of((index % per) * tile, tile), tile)
            fetch = [
                local(far_ref.at[0, index // per, place], gate_tile, 0),
                local(far_ref.at[1, index // per, place], up_tile, 1),
            ]
            for item in fetch:
                item.start()
            for item in fetch:
                item.wait()

            def two(step, _):
                slot = step % count
                value = gated(rows[slot, sure : sure + 2 * rest], gate_tile[...], up_tile[...])
                far_act[slot, index] = jnp.where(keep_ref[slot][:, 0:1] > 0, value, 0.0).astype(jnp.bfloat16)
                return 0

            lax.fori_loop(low, high, two, 0)
            return 0

        lax.fori_loop(0, tiles, one, 0)

    def ring_step(step, _):
        @pl.when(step < count)
        def _():
            for way in range(2):
                row_copy(way, step).wait_recv()

                @pl.when(step < count - 1)
                def _():
                    row_copy(way, step + 1).start()

            gradient_step(step)

        near_step(step)

        @pl.when(step < count)
        def _():
            for way in range(2):
                sum_copy(way, step).start()

        for which, when in ((0, count // 2), (1, count - 2), (2, count)):
            @pl.when(step == when)
            def _():
                far_copy(which).wait_recv()
                forward_copy(which).start()

        @pl.when(step == count - 2)
        def _():
            for which in range(2):
                forward_copy(which).wait_recv()

        @pl.when(step >= count - 2)
        def _():
            low = jnp.where(step == count - 2, 1, 2 * step + 7 - 2 * count)
            high = jnp.where(step == count - 2, 5, 2 * step + 9 - 2 * count)
            far_step(low, high)

        return 0

    lax.fori_loop(1, count + 1, ring_step, 0)

    for way in range(2):
        for step in range(1, count):
            row_copy(way, step).wait_send()
    pl.semaphore_signal(free_sem.at[0], inc=1, device_id=backward, device_id_type=MESH_ID)
    pl.semaphore_signal(free_sem.at[1], inc=1, device_id=onward, device_id_type=MESH_ID)
    pulls = [local(far_ref.at[2, 0], near_w.at[0, 0], 0), local(far_ref.at[2, 1], near_w.at[0, 1], 1)]
    pulls[0].start()
    forward_copy(2).wait_recv()
    pulls[1].start()
    for pull in pulls:
        pull.wait()
    for way in range(2):
        pl.semaphore_wait(free_sem.at[way], 1)

    def rest_step(step, _):
        slot = step % count

        @pl.when(step >= 2)
        def _():
            for way in range(2):
                rest_copy(way, step - 1).wait_recv()

        @pl.when(step >= 3)
        def _():
            for way in range(2):
                rest_copy(way, step - 2).wait_send()

        def two(index, _):
            columns = pl.ds(pl.multiple_of(index * chunk, chunk), chunk)
            total = None
            for number in range(tiles):
                place = pl.ds((number % per) * tile, tile)
                term = jnp.dot(
                    far_act[slot, number], near_w[0, number // per, place, columns], preferred_element_type=jnp.float32
                )
                total = term if total is None else total + term
            came = rows[step - 1, sure : sure + 2 * rest, columns].astype(jnp.float32)
            total = total + jnp.where(step >= 2, came, 0.0)
            piece = part[slot, :, columns].astype(jnp.float32)
            for way in range(2):
                base = way * rest
                stage_rest[step % 2, base : base + loose, columns] = (
                    total[base : base + loose] + piece[way * loose : (way + 1) * loose]
                ).astype(jnp.bfloat16)
                stage_rest[step % 2, base + loose : base + rest, columns] = total[base + loose : base + rest].astype(
                    jnp.bfloat16
                )
            return 0

        lax.fori_loop(0, width // chunk, two, 0)

        @pl.when(step < count)
        def _():
            for way in range(2):
                rest_copy(way, step).start()

        return 0

    lax.fori_loop(1, count + 1, rest_step, 0)

    def last(index, _):
        columns = pl.ds(pl.multiple_of(index * chunk, chunk), chunk)
        base = rows[0, :, columns].astype(jnp.float32)
        certain = stage[count % 2, :, columns].astype(jnp.float32)
        others = stage_rest[count % 2, :, columns].astype(jnp.float32)
        rows[0, 0:sure, columns] = (base[0:sure] + certain[0:sure]).astype(jnp.bfloat16)
        rows[0, sure : sure + 2 * rest, columns] = (base[sure : sure + 2 * rest] + others).astype(jnp.bfloat16)
        rows[0, total_rows - sure :, columns] = (base[total_rows - sure :] + certain[sure:]).astype(jnp.bfloat16)
        return 0

    lax.fori_loop(0, width // chunk, last, 0)
    pushes = [local(rows.at[0], out_ref, 0), local(total_grad, grad_ref, 1)]
    for push in pushes:
        push.start()
    for push in pushes:
        push.wait()
    for way in range(2):
        sum_copy(way, count - 1).wait_send()
        rest_copy(way, count - 1).wait_send()
        grad_copy(way, 1, term_ref.at[way, 0]).wait_send()
        for step in range(max(2, count - 2), count):
            grad_copy(way, step, grad_out.at[way, step % 2]).wait_send()
    for which in range(3):
        pair_copy(which).wait_send()
        far_copy(which).wait_send()
        forward_copy(which).wait_send()


def two_experts(
    tokens, w_query, w_key, w_value, w_out, w_gate, w_up, w_down, route, old_out, cotangent
):
    own = lax.axis_index("expert")
    length, width = tokens.shape
    blocks = length // BLOCK
    piece = BLOCK // 2
    strip = piece // 2
    capacity = max(2, blocks // 2 + 1)
    certain = blocks - capacity
    free = blocks - 2 * certain
    sure, loose, rest = certain * strip, free * strip, capacity * strip
    side = blocks * strip
    routes = route[:, 0]
    outer, section = lax.axis_size("outer"), lax.axis_size("section")
    ring = []
    for line in range(outer):
        places = [line * section + place for place in range(section)]
        ring += places if line % 2 == 0 else places[::-1]
    count = len(ring)

    own_hit = order_of(routes, own, capacity)
    peer_hit = order_of(routes, 1 - own, capacity)
    own_table, peer_table = own_hit.astype(jnp.bfloat16), peer_hit.astype(jnp.bfloat16)
    sorted_routes = jnp.sum(jnp.where(own_hit, routes[None, :], 0), axis=1)
    loose_own = (sorted_routes[certain:capacity] == own).astype(jnp.float32)
    flags = jnp.broadcast_to(loose_own[None, :, None], (1, free, 128))
    shift = 1
    while shift < count:
        moved = lax.ppermute(flags, GROUP, [(ring[i], ring[(i + shift) % count]) for i in range(count)])
        flags = jnp.concatenate([flags, moved], axis=0)
        shift *= 2
    flags = jnp.repeat(flags, strip, axis=1)
    turned = jnp.concatenate([flags[:1], flags[1:][::-1]], axis=0)
    near_mask = jnp.concatenate([flags, turned], axis=1)
    ones = jnp.ones((count, sure, 128), jnp.float32)
    keep_mask = jnp.concatenate([1.0 - flags, ones, 1.0 - turned, ones], axis=1)

    heads_out = attend_local(tokens, w_query, w_key, w_value)

    def mine_of(value, place):
        cut = value.reshape(blocks, 2, 2, strip, value.shape[-1])
        return lax.dynamic_index_in_dim(cut, place, 1, keepdims=False)

    def arranged(value, table):
        depth = value.shape[-1]
        rows = jnp.einsum("pb,bfrd->fprd", table, value, preferred_element_type=jnp.float32)
        rows = rows.astype(jnp.bfloat16).reshape(2, side, depth)
        return jnp.concatenate([rows[0], rows[1, sure:], rows[1, :sure]], axis=0)

    theirs = arranged(mine_of(heads_out, 1 - own), peer_table)
    parcel = jnp.dot(theirs, w_out, preferred_element_type=jnp.float32).astype(jnp.bfloat16)
    got = swap(parcel, "expert")
    kept = arranged(mine_of(heads_out, own), own_table)
    base = arranged(mine_of(tokens, own), own_table)
    value = jnp.dot(kept, w_out, preferred_element_type=jnp.float32)
    hidden = (value + base.astype(jnp.float32) + got.astype(jnp.float32)).astype(jnp.bfloat16)

    parts = cotangent.reshape(length, outer, 2, width // (outer * 2))
    core = lax.axis_index("pair")

    def part(number):
        return lax.dynamic_index_in_dim(parts, number, 2, keepdims=False).reshape(length, width // 2)

    left = jnp.concatenate([part(core), swap(part(1 - core), "pair")], axis=0)
    term = lax.dot_general(
        left, both(heads_out), (((0,), (0,)), ((), ())), preferred_element_type=jnp.float32
    ).astype(jnp.bfloat16)
    high, deep = width // (2 * count), term.shape[1]
    x, z = lax.axis_index("outer"), lax.axis_index("section")
    spot = x * (count - 1) + z * (1 - 2 * x)
    spots = (spot + lax.broadcasted_iota(jnp.int32, (count, count), 0)) % count
    lines = spots // section
    wanted = lines * section + (spots % section) * (1 - 2 * lines) + (section - 1) * lines
    pick_term = (wanted == lax.broadcasted_iota(jnp.int32, (count, count), 1)).astype(jnp.bfloat16)
    term = jnp.einsum(
        "jc,chwd->wjhd", pick_term, term.reshape(count, high, 2, deep // 2), preferred_element_type=jnp.float32
    ).astype(jnp.bfloat16)

    hidden_units = w_gate.shape[1]
    half = hidden_units // 2
    tiles = 4
    any_space = pl.BlockSpec(memory_space=pl.ANY)
    vmem = pl.BlockSpec(memory_space=pltpu.VMEM)
    low = jnp.bfloat16
    dma = pltpu.SemaphoreType.DMA
    out, gradient, _, _ = pl.pallas_call(
        functools.partial(moe_kernel, sure, loose, half),
        out_shape=(
            jax.ShapeDtypeStruct((2 * side, width), low),
            jax.ShapeDtypeStruct((high, deep), jnp.float32),
            jax.ShapeDtypeStruct((3, 2, hidden_units, width), low),
            jax.ShapeDtypeStruct((2, count, high, deep // 2), low),
        ),
        in_specs=[any_space] * 5 + [vmem] * 2,
        out_specs=[any_space] * 4,
        scratch_shapes=[
            pltpu.VMEM((3, 2, hidden_units, width), low),
            pltpu.VMEM((count, 2 * side, width), low),
            pltpu.VMEM((count, 2 * sure, width), low),
            pltpu.VMEM((2, 2 * sure, width), low),
            pltpu.VMEM((2, 2 * rest, width), low),
            pltpu.VMEM((count, 2 * loose, width), low),
            pltpu.VMEM((count, tiles, 2 * rest, half), low),
            pltpu.VMEM((tiles, 2 * side, half), low),
            pltpu.VMEM((half, width), low),
            pltpu.VMEM((half, width), low),
            pltpu.VMEM((2, high, deep // 2), low),
            pltpu.VMEM((2, high, deep // 2), low),
            pltpu.VMEM((2, 2, high, deep // 2), low),
            pltpu.VMEM((high, deep), jnp.float32),
            dma((2, count)), dma((2, count)), dma((2, count)), dma((2, count)),
            dma((2, count)), dma((2, count)), dma((2, count)), dma((2, count)),
            dma((3,)), dma((3,)), dma((3,)), dma((3,)), dma((3,)), dma((3,)),
            dma((4,)), pltpu.SemaphoreType.REGULAR((2,)),
        ],
        compiler_params=pltpu.CompilerParams(
            collective_id=0, has_side_effects=True, vmem_limit_bytes=67043328
        ),
        cost_estimate=pl.CostEstimate(flops=10**11, bytes_accessed=10**8, transcendentals=0),
    )(hidden, w_gate[0], w_up[0], w_down[0], term, near_mask, keep_mask)

    whole = jnp.stack([out[:side], jnp.concatenate([out[side + rest :], out[side : side + rest]], axis=0)], axis=0)
    whole = whole.reshape(2, blocks, strip, width)
    joined = jnp.einsum("pb,fprd->bfrd", own_table, whole, preferred_element_type=jnp.float32)
    joined = joined.astype(jnp.bfloat16).reshape(blocks, piece, width)
    fresh = (routes >= 1).astype(jnp.float32)
    gap = joined.astype(jnp.float32) - old_out.astype(jnp.float32)
    divergence = 0.5 * jnp.mean(gap * gap, axis=-1) * fresh[:, None]
    return (joined, divergence, gradient)


def solution(mesh):
    sizes = mesh.shape
    pair = 2 if sizes["dp"] % 2 == 0 else 1
    replicas_in_ring = sizes["dp"] // pair * sizes["section"]
    body = two_experts if sizes["expert"] == 2 and pair == 2 and replicas_in_ring == 8 else per_device
    split = Mesh(
        mesh.devices.reshape(sizes["dp"] // pair, pair, sizes["section"], sizes["expert"]),
        ("outer", "pair", "section", "expert"),
    )
    replicas = ("outer", "pair", "section")
    return jax.shard_map(
        body,
        mesh=split,
        in_specs=(
            P(replicas, None),
            P(None, "expert"),
            P(None, "expert"),
            P(None, "expert"),
            P("expert", None),
            P("expert", replicas, None),
            P("expert", replicas, None),
            P("expert", replicas, None),
            P(replicas, None),
            P(replicas, "expert", None),
            P(replicas, None),
        ),
        out_specs=(
            P(replicas, "expert", None),
            P(replicas, "expert"),
            P(replicas, "expert"),
        ),
        check_vma=False,
    )
```

```python
import functools
import math

import jax
import jax.numpy as jnp
from jax import lax
from jax.experimental import pallas as pl
from jax.experimental.pallas import tpu as pltpu
from jax.sharding import Mesh
from jax.sharding import PartitionSpec as P

HEAD_DIM = 128
BLOCK = 64
GROUP = ("outer", "section")


def attend_local(tokens, w_query, w_key, w_value):
    length = tokens.shape[0]
    key_heads = w_key.shape[1] // HEAD_DIM
    group = w_query.shape[1] // w_key.shape[1]
    queries = jnp.dot(tokens, w_query, preferred_element_type=jnp.float32).astype(jnp.bfloat16)
    queries = queries.reshape(length, key_heads, group, HEAD_DIM)
    keys = jnp.dot(tokens, w_key, preferred_element_type=jnp.float32).astype(jnp.bfloat16)
    keys = keys.reshape(length, key_heads, HEAD_DIM)
    values = jnp.dot(tokens, w_value, preferred_element_type=jnp.float32).astype(jnp.bfloat16)
    values = values.reshape(length, key_heads, HEAD_DIM)
    scores = jnp.einsum("qkgd,skd->kgqs", queries, keys, preferred_element_type=jnp.float32)
    scores = scores * (1.0 / math.sqrt(HEAD_DIM))
    query_pos = lax.broadcasted_iota(jnp.int32, (length, length), 0)
    key_pos = lax.broadcasted_iota(jnp.int32, (length, length), 1)
    scores = jnp.where(query_pos >= key_pos, scores, -jnp.inf)
    top = jnp.max(scores, axis=-1, keepdims=True)
    weights = jnp.exp(scores - top)
    probs = (weights / jnp.sum(weights, axis=-1, keepdims=True)).astype(jnp.bfloat16)
    mixed = jnp.einsum("kgqs,skd->qkgd", probs, values, preferred_element_type=jnp.float32)
    return mixed.astype(jnp.bfloat16).reshape(length, key_heads * group * HEAD_DIM)


def routing_table(routes, experts, capacity):
    number = routes.shape[0]
    same = routes[:, None] == routes[None, :]
    earlier = lax.broadcasted_iota(jnp.int32, (number, number), 1) < lax.broadcasted_iota(
        jnp.int32, (number, number), 0
    )
    slot = jnp.sum((same & earlier).astype(jnp.int32), axis=1)
    expert_hit = routes[None, :] == lax.broadcasted_iota(jnp.int32, (experts, number), 0)
    slot_hit = slot[None, :] == lax.broadcasted_iota(jnp.int32, (capacity, number), 0)
    return (expert_hit[:, None, :] & slot_hit[None, :, :]).astype(jnp.bfloat16)


def swap(value, axis):
    return lax.ppermute(value, axis, [(0, 1), (1, 0)])


def both(value, axis=0):
    if lax.axis_size("pair") == 1:
        return value
    return jnp.concatenate([value, swap(value, "pair")], axis=axis)


def pick(blocks, table):
    rows = jnp.einsum("cb,brd->crd", table, blocks, preferred_element_type=jnp.float32)
    return rows.astype(jnp.bfloat16)


def wo_gradient(cotangent, heads_out):
    length, width = cotangent.shape
    outer, pair = lax.axis_size("outer"), lax.axis_size("pair")
    parts = cotangent.reshape(length, outer, pair, width // (outer * pair))
    mine = lax.axis_index("pair")

    def part(number):
        return lax.dynamic_index_in_dim(parts, number, 2, keepdims=False).reshape(length, width // pair)

    left = part(mine)
    if pair == 2:
        left = jnp.concatenate([left, swap(part(1 - mine), "pair")], axis=0)
    term = lax.dot_general(
        left, both(heads_out), (((0,), (0,)), ((), ())), preferred_element_type=jnp.float32
    ).astype(jnp.bfloat16)
    return lax.psum_scatter(term, GROUP, scatter_dimension=0, tiled=True).astype(jnp.float32)


def per_device(
    tokens, w_query, w_key, w_value, w_out, w_gate, w_up, w_down, route, old_out, cotangent
):
    experts = lax.axis_size("expert")
    own = lax.axis_index("expert")
    length, width = tokens.shape
    blocks = length // BLOCK
    piece_rows = BLOCK // experts
    capacity = max(2, blocks // experts + 1)
    old_count = experts - max(1, experts // 4)
    routes = route[:, 0]
    table = routing_table(routes, experts, capacity)
    own_table = lax.dynamic_index_in_dim(table, own, 0, keepdims=False)
    token_rows = pick(tokens.reshape(blocks, BLOCK, width), own_table)

    heads_out = attend_local(tokens, w_query, w_key, w_value)
    head_blocks = heads_out.reshape(blocks, BLOCK, heads_out.shape[1])

    def project(rows):
        return jnp.dot(
            rows.reshape(-1, rows.shape[-1]), w_out, preferred_element_type=jnp.float32
        ).reshape(rows.shape[:-1] + (width,))

    if experts == 2:
        half = capacity * BLOCK // 2
        peer_table = lax.dynamic_index_in_dim(table, 1 - own, 0, keepdims=False)
        outgoing = project(pick(head_blocks, peer_table)).astype(jnp.bfloat16).reshape(-1, width)
        kept = project(pick(head_blocks, own_table)).reshape(-1, width)
        kept = kept + token_rows.reshape(-1, width).astype(jnp.float32)
        first = (kept[:half] + swap(outgoing[:half], "expert").astype(jnp.float32)).astype(jnp.bfloat16)
        second = (kept[half:] + swap(outgoing[half:], "expert").astype(jnp.float32)).astype(jnp.bfloat16)
    else:
        half = capacity * BLOCK // 2
        rows = jnp.einsum("jcb,brd->jcrd", table, head_blocks, preferred_element_type=jnp.float32)
        outgoing = project(rows.astype(jnp.bfloat16)).astype(jnp.bfloat16)
        total = lax.psum_scatter(outgoing, "expert", scatter_dimension=0, tiled=True)[0]
        total = (token_rows.astype(jnp.float32) + total.astype(jnp.float32)).astype(jnp.bfloat16)
        total = total.reshape(-1, width)
        first, second = total[:half], total[half:]

    gradient = wo_gradient(cotangent, heads_out)
    gate_rows, up_rows, down_rows = both(w_gate[0]), both(w_up[0]), both(w_down[0])
    contract = (((1,), (1,)), ((), ()))

    def expert(top, bottom):
        rows = jnp.concatenate([top, bottom], axis=0)
        gate = lax.dot_general(rows, gate_rows, contract, preferred_element_type=jnp.float32)
        lifted = lax.dot_general(rows, up_rows, contract, preferred_element_type=jnp.float32)
        active = (jax.nn.silu(gate) * lifted).astype(jnp.bfloat16)
        return jnp.dot(active, down_rows, preferred_element_type=jnp.float32)

    outer, section = lax.axis_size("outer"), lax.axis_size("section")
    ring = []
    for line in range(outer):
        places = [line * section + place for place in range(section)]
        ring += places if line % 2 == 0 else places[::-1]
    count = len(ring)
    onward = [(ring[i], ring[(i + 1) % count]) for i in range(count)]
    backward = [(target, source) for source, target in onward]
    front, back = first, second
    sums = None
    for _ in range(count - 1):
        front = lax.ppermute(front, GROUP, onward)
        back = lax.ppermute(back, GROUP, backward)
        terms = expert(front, back)
        upper, lower = terms[:half], terms[half:]
        if sums is not None:
            upper = upper + lax.ppermute(sums[0], GROUP, onward).astype(jnp.float32)
            lower = lower + lax.ppermute(sums[1], GROUP, backward).astype(jnp.float32)
        sums = (upper.astype(jnp.bfloat16), lower.astype(jnp.bfloat16))
    terms = expert(first, second)
    upper = terms[:half] + lax.ppermute(sums[0], GROUP, onward).astype(jnp.float32)
    lower = terms[half:] + lax.ppermute(sums[1], GROUP, backward).astype(jnp.float32)
    expert_sum = jnp.concatenate([upper, lower], axis=0)
    hidden = jnp.concatenate([first, second], axis=0).astype(jnp.float32)
    whole = (hidden + expert_sum.astype(jnp.bfloat16).astype(jnp.float32)).astype(jnp.bfloat16)
    whole = whole.reshape(capacity, experts, piece_rows, width)
    if experts == 2:
        mine = lax.dynamic_index_in_dim(whole, own, 1, keepdims=False)
        theirs = swap(lax.dynamic_index_in_dim(whole, 1 - own, 1, keepdims=False), "expert")
        joined = jnp.einsum("cb,crd->brd", own_table, mine, preferred_element_type=jnp.float32)
        joined = joined + jnp.einsum("cb,crd->brd", peer_table, theirs, preferred_element_type=jnp.float32)
    else:
        returned = lax.all_to_all(
            whole.transpose(1, 0, 2, 3), "expert", split_axis=0, concat_axis=0, tiled=True
        )
        joined = jnp.einsum("jcb,jcrd->brd", table, returned, preferred_element_type=jnp.float32)
    joined = joined.astype(jnp.bfloat16)
    fresh = (routes >= old_count).astype(jnp.float32)
    gap = joined.astype(jnp.float32) - old_out.astype(jnp.float32)
    divergence = 0.5 * jnp.mean(gap * gap, axis=-1) * fresh[:, None]
    return (joined, divergence, gradient)


MESH_ID = pl.DeviceIdType.MESH
NT = (((1,), (1,)), ((), ()))


def order_of(routes, first, capacity):
    number = routes.shape[0]
    certain = number - capacity
    same = routes[:, None] == routes[None, :]
    earlier = lax.broadcasted_iota(jnp.int32, (number, number), 1) < lax.broadcasted_iota(
        jnp.int32, (number, number), 0
    )
    slot = jnp.sum((same & earlier).astype(jnp.int32), axis=1)
    loose = slot >= certain
    rank = jnp.sum((loose[None, :] & earlier).astype(jnp.int32), axis=1)
    fixed = jnp.where(routes == first, slot, capacity + slot)
    place = jnp.where(loose, certain + rank, fixed)
    return place[None, :] == lax.broadcasted_iota(jnp.int32, (number, number), 0)


def moe_kernel(
    sure, loose, half,
    hidden_ref, gate_ref, up_ref, down_ref, term_ref, near_ref, keep_ref,
    out_ref, grad_ref, far_ref, slot_ref,
    near_w, rows, sums, stage, stage_rest, part, far_act, act, gate_tile, up_tile, grad_in, term_in, grad_out, total_grad,
    row_send, row_recv, sum_send, sum_recv, grad_send, grad_recv, rest_send, rest_recv,
    pair_send, pair_recv, far_send, far_recv, fwd_send, fwd_recv, local_sem, free_sem,
):
    outer, section = lax.axis_size("outer"), lax.axis_size("section")
    count = outer * section
    x, z = lax.axis_index("outer"), lax.axis_index("section")
    spot = x * (count - 1) + z * (1 - 2 * x)

    def at(place):
        line = place // section
        within = place % section
        return {"outer": line, "section": within * (1 - 2 * line) + (section - 1) * line}

    onward, backward = at((spot + 1) % count), at((spot + count - 1) % count)
    partner = {"pair": 1 - lax.axis_index("pair")}
    peer = {"expert": 1 - lax.axis_index("expert")}
    ways = (onward, backward)
    total_rows, width = hidden_ref.shape
    side = total_rows // 2
    rest = side - sure
    tile = half
    tiles = near_w.shape[1] * near_w.shape[2] // tile
    per = near_w.shape[2] // tile
    chunk = 512
    weights = (gate_ref, up_ref, down_ref)

    barrier = pltpu.get_barrier_semaphore()
    for target in (onward, backward, partner, peer):
        pl.semaphore_signal(barrier, inc=1, device_id=target, device_id_type=MESH_ID)
    pl.semaphore_wait(barrier, 4)

    def remote(source, target, send, recv, device):
        return pltpu.make_async_remote_copy(
            src_ref=source, dst_ref=target, send_sem=send, recv_sem=recv, device_id=device, device_id_type=MESH_ID
        )

    def span(way):
        return pl.ds(way * side, side)

    def row_copy(way, step):
        source = rows.at[step - 1, span(way)]
        return remote(source, rows.at[step, span(way)], row_send.at[way, step], row_recv.at[way, step], ways[way])

    def first_row_copy(way):
        return remote(hidden_ref.at[span(way)], rows.at[1, span(way)], row_send.at[way, 1], row_recv.at[way, 1], ways[way])

    high, deep = grad_in.shape[1], grad_in.shape[2]

    def term_at(way, index):
        place = (spot + index) % count
        line = place // section
        within = place % section
        block = line * section + within * (1 - 2 * line) + (section - 1) * line
        return term_ref.at[pl.ds(pl.multiple_of(block * high, high), high), pl.ds(way * deep, deep)]

    def grad_copy(way, step, source):
        return remote(source, slot_ref.at[way, step], grad_send.at[way, step], grad_recv.at[way, step], ways[way])

    def sum_copy(way, step):
        here = pl.ds(way * sure, sure)
        return remote(stage.at[step % 2, here], sums.at[step, here], sum_send.at[way, step], sum_recv.at[way, step], ways[way])

    def rest_copy(way, half_index, step):
        here = pl.ds(way * rest, rest)
        there = pl.ds(sure + way * rest, rest)
        columns = pl.ds(half_index * (width // 2), width // 2)
        return remote(
            stage_rest.at[step % 2, here, columns],
            rows.at[step, there, columns],
            rest_send.at[way, half_index, step],
            rest_recv.at[way, half_index, step],
            ways[way],
        )

    def far_copy(which):
        return remote(weights[which], far_ref.at[which, 0], far_send.at[which], far_recv.at[which], peer)

    def forward_copy(which):
        return remote(far_ref.at[which, 0], far_ref.at[which, 1], fwd_send.at[which], fwd_recv.at[which], partner)

    def pair_copy(which):
        return remote(weights[which], near_w.at[which, 1], pair_send.at[which], pair_recv.at[which], partner)

    def local(source, target, place):
        return pltpu.make_async_copy(source, target, local_sem.at[place])

    for way in range(2):
        first_row_copy(way).start()
    for which in range(3):
        far_copy(which).start()
    grad_copy(0, 1, term_at(0, count - 1)).start()
    grad_copy(1, 1, term_at(1, 1)).start()
    loads = [local(weights[which], near_w.at[which, 0], which) for which in range(3)]
    loads.append(local(hidden_ref, rows.at[0], 3))
    for load in loads:
        load.start()
    for which in range(3):
        pair_copy(which).start()
    for load in loads:
        load.wait()
    for which in range(3):
        pair_copy(which).wait_recv()

    def gradient_step(step):
        pulls = []
        for way in range(2):
            grad_copy(way, step, slot_ref.at[way, step]).wait_recv()
            pulls.append(local(slot_ref.at[way, step], grad_in.at[way], way))
            index = (2 * count - 1 - step) % count if way == 0 else (1 + step) % count
            pulls.append(local(term_at(way, index), term_in.at[way], 2 + way))
        for pull in pulls:
            pull.start()
        for pull in pulls:
            pull.wait()
        for way in range(2):
            value = grad_in[way].astype(jnp.float32) + term_in[way].astype(jnp.float32)

            @pl.when(step < count - 1)
            def _():
                @pl.when(step >= 3)
                def _():
                    grad_copy(way, step - 1, grad_out.at[way, step % 2]).wait_send()

                grad_out[way, step % 2] = value.astype(jnp.bfloat16)
                grad_copy(way, step + 1, grad_out.at[way, step % 2]).start()

            @pl.when(step == count - 1)
            def _():
                total_grad[:, pl.ds(way * value.shape[1], value.shape[1])] = value

    def gated(value, gate, up):
        pre = lax.dot_general(value, gate, NT, preferred_element_type=jnp.float32)
        lifted = lax.dot_general(value, up, NT, preferred_element_type=jnp.float32)
        return pre * (1.0 / (1.0 + jnp.exp(-pre))) * lifted

    def near_step(step):
        slot = step

        def one(index, _):
            place = pl.ds(pl.multiple_of((index % per) * tile, tile), tile)
            value = gated(rows[slot], near_w[0, index // per, place], near_w[1, index // per, place])
            act[index] = value.astype(jnp.bfloat16)
            return 0

        lax.fori_loop(0, tiles, one, 0)

        @pl.when(step >= 2)
        def _():
            for way in range(2):
                sum_copy(way, step - 1).wait_recv()

        @pl.when(step >= 3)
        def _():
            for way in range(2):
                sum_copy(way, step - 2).wait_send()

        def two(index, _):
            columns = pl.ds(pl.multiple_of(index * chunk, chunk), chunk)
            total = None
            for number in range(tiles):
                place = pl.ds((number % per) * tile, tile)
                term = jnp.dot(
                    act[number], near_w[2, number // per, place, columns], preferred_element_type=jnp.float32
                )
                total = term if total is None else total + term
            before = sums[jnp.maximum(step - 1, 0), :, columns].astype(jnp.float32)
            before = jnp.where(step >= 2, before, 0.0)
            stage[step % 2, 0:sure, columns] = (total[0:sure] + before[0:sure]).astype(jnp.bfloat16)
            stage[step % 2, sure : 2 * sure, columns] = (total[total_rows - sure :] + before[sure:]).astype(jnp.bfloat16)
            mine = near_ref[slot]
            part[slot, 0:loose, columns] = jnp.where(
                mine[0:loose, 0:1] > 0, total[sure : sure + loose], 0.0
            ).astype(jnp.bfloat16)
            part[slot, loose : 2 * loose, columns] = jnp.where(
                mine[loose:, 0:1] > 0, total[side : side + loose], 0.0
            ).astype(jnp.bfloat16)
            return 0

        lax.fori_loop(0, width // chunk, two, 0)

    def far_step(low, high):
        def one(index, _):
            place = pl.ds(pl.multiple_of((index % per) * tile, tile), tile)
            fetch = [
                local(far_ref.at[0, index // per, place], gate_tile, 0),
                local(far_ref.at[1, index // per, place], up_tile, 1),
            ]
            for item in fetch:
                item.start()
            for item in fetch:
                item.wait()

            def two(step, _):
                slot = step % count
                value = gated(rows[slot, sure : sure + 2 * rest], gate_tile[...], up_tile[...])
                far_act[slot, index] = jnp.where(keep_ref[slot][:, 0:1] > 0, value, 0.0).astype(jnp.bfloat16)
                return 0

            lax.fori_loop(low, high, two, 0)
            return 0

        lax.fori_loop(0, tiles, one, 0)

    def ring_step(step, _):
        @pl.when(step >= 1)
        def _():
            for way in range(2):
                row_copy(way, step).wait_recv()

                @pl.when(step < count - 1)
                def _():
                    row_copy(way, step + 1).start()

            gradient_step(step)

        near_step(step)

        @pl.when(step >= 1)
        def _():
            for way in range(2):
                sum_copy(way, step).start()

        @pl.when(step == 0)
        def _():
            sums[0] = stage[0]

        for which, when in ((0, count // 2 - 1), (1, count - 3), (2, count - 1)):
            @pl.when(step == when)
            def _():
                far_copy(which).wait_recv()
                forward_copy(which).start()

        @pl.when(step == count - 3)
        def _():
            for which in range(2):
                forward_copy(which).wait_recv()

        @pl.when((step >= count - 3) & (step < count - 1))
        def _():
            low = 3 * (step - (count - 3))
            far_step(low, low + 3)

        return 0

    lax.fori_loop(0, count, ring_step, 0)

    for way in range(2):
        for step in range(1, count):
            row_copy(way, step).wait_send()

    def grant(turn):
        pl.semaphore_signal(free_sem.at[0, turn], inc=1, device_id=backward, device_id_type=MESH_ID)
        pl.semaphore_signal(free_sem.at[1, turn], inc=1, device_id=onward, device_id_type=MESH_ID)

    grant(0)
    pulls = [local(far_ref.at[2, 0], near_w.at[0, 0], 0), local(far_ref.at[2, 1], near_w.at[0, 1], 1)]
    pulls[0].start()
    forward_copy(2).wait_recv()
    pulls[1].start()
    for pull in pulls:
        pull.wait()

    def rest_step(step, _):
        slot = step % count

        def two(index, _):
            columns = pl.ds(pl.multiple_of(index * chunk, chunk), chunk)
            total = None
            for number in range(tiles):
                place = pl.ds((number % per) * tile, tile)
                term = jnp.dot(
                    far_act[slot, number], near_w[0, number // per, place, columns], preferred_element_type=jnp.float32
                )
                total = term if total is None else total + term
            piece = part[slot, :, columns].astype(jnp.float32)
            for way in range(2):
                base = way * rest
                near_w[1, 0, base : base + loose, columns] = (
                    total[base : base + loose] + piece[way * loose : (way + 1) * loose]
                ).astype(jnp.bfloat16)
                near_w[1, 0, base + loose : base + rest, columns] = total[base + loose : base + rest].astype(jnp.bfloat16)
            return 0

        lax.fori_loop(0, width // chunk, two, 0)

        for turn, when in ((0, 1), (1, count - 2)):
            @pl.when(step == when)
            def _():
                for way in range(2):
                    pl.semaphore_wait(free_sem.at[way, turn], 1)

        for half_index in range(2):
            for way in range(2):
                here = slice(way * rest, (way + 1) * rest)
                there = slice(sure + way * rest, sure + (way + 1) * rest)
                columns = slice(half_index * (width // 2), (half_index + 1) * (width // 2))

                @pl.when(step >= 3)
                def _():
                    rest_copy(way, half_index, step - 2).wait_send()

                @pl.when(step >= 2)
                def _():
                    rest_copy(way, half_index, step - 1).wait_recv()
                    stage_rest[step % 2, here, columns] = (
                        near_w[1, 0, here, columns].astype(jnp.float32) + rows[step - 1, there, columns].astype(jnp.float32)
                    ).astype(jnp.bfloat16)

                @pl.when(step < 2)
                def _():
                    stage_rest[step % 2, here, columns] = near_w[1, 0, here, columns]

                @pl.when(step < count)
                def _():
                    rest_copy(way, half_index, step).start()

        @pl.when(step == 1)
        def _():
            far_step(count - 2, count)
            grant(1)

        return 0

    lax.fori_loop(1, count + 1, rest_step, 0)
    for way in range(2):
        sum_copy(way, count - 1).wait_recv()

    def last(index, _):
        columns = pl.ds(pl.multiple_of(index * chunk, chunk), chunk)
        base = rows[0, :, columns].astype(jnp.float32)
        certain = sums[0, :, columns].astype(jnp.float32) + sums[count - 1, :, columns].astype(jnp.float32)
        certain = certain.astype(jnp.bfloat16).astype(jnp.float32)
        others = stage_rest[count % 2, :, columns].astype(jnp.float32)
        rows[0, 0:sure, columns] = (base[0:sure] + certain[0:sure]).astype(jnp.bfloat16)
        rows[0, sure : sure + 2 * rest, columns] = (base[sure : sure + 2 * rest] + others).astype(jnp.bfloat16)
        rows[0, total_rows - sure :, columns] = (base[total_rows - sure :] + certain[sure:]).astype(jnp.bfloat16)
        return 0

    lax.fori_loop(0, width // chunk, last, 0)
    pushes = [local(rows.at[0], out_ref, 0), local(total_grad, grad_ref, 1)]
    for push in pushes:
        push.start()
    for push in pushes:
        push.wait()
    for way in range(2):
        sum_copy(way, count - 2).wait_send()
        sum_copy(way, count - 1).wait_send()
        for half_index in range(2):
            rest_copy(way, half_index, count - 1).wait_send()
        grad_copy(way, 1, term_at(way, 0)).wait_send()
        for step in range(max(2, count - 2), count):
            grad_copy(way, step, grad_out.at[way, step % 2]).wait_send()
    for which in range(3):
        pair_copy(which).wait_send()
        far_copy(which).wait_send()
        forward_copy(which).wait_send()


def two_experts(
    tokens, w_query, w_key, w_value, w_out, w_gate, w_up, w_down, route, old_out, cotangent
):
    own = lax.axis_index("expert")
    length, width = tokens.shape
    blocks = length // BLOCK
    piece = BLOCK // 2
    strip = piece // 2
    capacity = max(2, blocks // 2 + 1)
    certain = blocks - capacity
    free = blocks - 2 * certain
    sure, loose, rest = certain * strip, free * strip, capacity * strip
    side = blocks * strip
    routes = route[:, 0]
    outer, section = lax.axis_size("outer"), lax.axis_size("section")
    ring = []
    for line in range(outer):
        places = [line * section + place for place in range(section)]
        ring += places if line % 2 == 0 else places[::-1]
    count = len(ring)

    own_hit = order_of(routes, own, capacity)
    peer_hit = order_of(routes, 1 - own, capacity)
    own_table, peer_table = own_hit.astype(jnp.bfloat16), peer_hit.astype(jnp.bfloat16)
    sorted_routes = jnp.sum(jnp.where(own_hit, routes[None, :], 0), axis=1)
    loose_own = (sorted_routes[certain:capacity] == own).astype(jnp.float32)
    flags = jnp.broadcast_to(loose_own[None, :, None], (1, free, 128))
    shift = 1
    while shift < count:
        moved = lax.ppermute(flags, GROUP, [(ring[i], ring[(i + shift) % count]) for i in range(count)])
        flags = jnp.concatenate([flags, moved], axis=0)
        shift *= 2
    flags = jnp.repeat(flags, strip, axis=1)
    turned = jnp.concatenate([flags[:1], flags[1:][::-1]], axis=0)
    near_mask = jnp.concatenate([flags, turned], axis=1)
    ones = jnp.ones((count, sure, 128), jnp.float32)
    keep_mask = jnp.concatenate([1.0 - flags, ones, 1.0 - turned, ones], axis=1)

    heads_out = attend_local(tokens, w_query, w_key, w_value)

    def mine_of(value, place):
        cut = value.reshape(blocks, 2, 2, strip, value.shape[-1])
        return lax.dynamic_index_in_dim(cut, place, 1, keepdims=False)

    def arranged(value, table):
        depth = value.shape[-1]
        rows = jnp.einsum("pb,bfrd->fprd", table, value, preferred_element_type=jnp.float32)
        rows = rows.astype(jnp.bfloat16).reshape(2, side, depth)
        return jnp.concatenate([rows[0], rows[1, sure:], rows[1, :sure]], axis=0)

    theirs = arranged(mine_of(heads_out, 1 - own), peer_table)
    parcel = jnp.dot(theirs, w_out, preferred_element_type=jnp.float32).astype(jnp.bfloat16)
    got = swap(parcel, "expert")
    kept = arranged(mine_of(heads_out, own), own_table)
    base = arranged(mine_of(tokens, own), own_table)
    value = jnp.dot(kept, w_out, preferred_element_type=jnp.float32)
    hidden = (value + base.astype(jnp.float32) + got.astype(jnp.float32)).astype(jnp.bfloat16)

    core = lax.axis_index("pair")
    span = width // (outer * 2)

    def part(number):
        pieces = [
            lax.dynamic_slice_in_dim(cotangent, (line * 2 + number) * span, span, axis=1) for line in range(outer)
        ]
        return jnp.concatenate(pieces, axis=1)

    left = jnp.concatenate([part(core), swap(part(1 - core), "pair")], axis=0)
    term = lax.dot_general(
        left, both(heads_out), (((0,), (0,)), ((), ())), preferred_element_type=jnp.float32
    ).astype(jnp.bfloat16)
    high, deep = width // (2 * count), term.shape[1]

    hidden_units = w_gate.shape[1]
    half = hidden_units // 2
    tiles = 4
    any_space = pl.BlockSpec(memory_space=pl.ANY)
    vmem = pl.BlockSpec(memory_space=pltpu.VMEM)
    low = jnp.bfloat16
    dma = pltpu.SemaphoreType.DMA
    out, gradient, _, _ = pl.pallas_call(
        functools.partial(moe_kernel, sure, loose, half),
        out_shape=(
            jax.ShapeDtypeStruct((2 * side, width), low),
            jax.ShapeDtypeStruct((high, deep), jnp.float32),
            jax.ShapeDtypeStruct((3, 2, hidden_units, width), low),
            jax.ShapeDtypeStruct((2, count, high, deep // 2), low),
        ),
        in_specs=[any_space] * 5 + [vmem] * 2,
        out_specs=[any_space] * 4,
        scratch_shapes=[
            pltpu.VMEM((3, 2, hidden_units, width), low),
            pltpu.VMEM((count, 2 * side, width), low),
            pltpu.VMEM((count, 2 * sure, width), low),
            pltpu.VMEM((2, 2 * sure, width), low),
            pltpu.VMEM((2, 2 * rest, width), low),
            pltpu.VMEM((count, 2 * loose, width), low),
            pltpu.VMEM((count, tiles, 2 * rest, half), low),
            pltpu.VMEM((tiles, 2 * side, half), low),
            pltpu.VMEM((half, width), low),
            pltpu.VMEM((half, width), low),
            pltpu.VMEM((2, high, deep // 2), low),
            pltpu.VMEM((2, high, deep // 2), low),
            pltpu.VMEM((2, 2, high, deep // 2), low),
            pltpu.VMEM((high, deep), jnp.float32),
            dma((2, count)), dma((2, count)), dma((2, count)), dma((2, count)),
            dma((2, count)), dma((2, count)), dma((2, 2, count)), dma((2, 2, count)),
            dma((3,)), dma((3,)), dma((3,)), dma((3,)), dma((3,)), dma((3,)),
            dma((4,)), pltpu.SemaphoreType.REGULAR((2, 2)),
        ],
        compiler_params=pltpu.CompilerParams(
            collective_id=0, has_side_effects=True, vmem_limit_bytes=67043328
        ),
        cost_estimate=pl.CostEstimate(flops=10**11, bytes_accessed=10**8, transcendentals=0),
    )(hidden, w_gate[0], w_up[0], w_down[0], term, near_mask, keep_mask)

    whole = jnp.stack([out[:side], jnp.concatenate([out[side + rest :], out[side : side + rest]], axis=0)], axis=0)
    whole = whole.reshape(2, blocks, strip, width)
    joined = jnp.einsum("pb,fprd->bfrd", own_table, whole, preferred_element_type=jnp.float32)
    joined = joined.astype(jnp.bfloat16).reshape(blocks, piece, width)
    fresh = (routes >= 1).astype(jnp.float32)
    gap = joined.astype(jnp.float32) - old_out.astype(jnp.float32)
    divergence = 0.5 * jnp.mean(gap * gap, axis=-1) * fresh[:, None]
    return (joined, divergence, gradient)


def solution(mesh):
    sizes = mesh.shape
    pair = 2 if sizes["dp"] % 2 == 0 else 1
    replicas_in_ring = sizes["dp"] // pair * sizes["section"]
    body = two_experts if sizes["expert"] == 2 and pair == 2 and replicas_in_ring == 8 else per_device
    split = Mesh(
        mesh.devices.reshape(sizes["dp"] // pair, pair, sizes["section"], sizes["expert"]),
        ("outer", "pair", "section", "expert"),
    )
    replicas = ("outer", "pair", "section")
    return jax.shard_map(
        body,
        mesh=split,
        in_specs=(
            P(replicas, None),
            P(None, "expert"),
            P(None, "expert"),
            P(None, "expert"),
            P("expert", None),
            P("expert", replicas, None),
            P("expert", replicas, None),
            P("expert", replicas, None),
            P(replicas, None),
            P(replicas, "expert", None),
            P(replicas, None),
        ),
        out_specs=(
            P(replicas, "expert", None),
            P(replicas, "expert"),
            P(replicas, "expert"),
        ),
        check_vma=False,
    )
```

```python
import functools
import math

import jax
import jax.numpy as jnp
from jax import lax
from jax.experimental import pallas as pl
from jax.experimental.pallas import tpu as pltpu
from jax.sharding import Mesh
from jax.sharding import PartitionSpec as P

HEAD_DIM = 128
BLOCK = 64
GROUP = ("outer", "section")


def attend_local(tokens, w_query, w_key, w_value):
    length = tokens.shape[0]
    key_heads = w_key.shape[1] // HEAD_DIM
    group = w_query.shape[1] // w_key.shape[1]
    queries = jnp.dot(tokens, w_query, preferred_element_type=jnp.float32).astype(jnp.bfloat16)
    queries = queries.reshape(length, key_heads, group, HEAD_DIM)
    keys = jnp.dot(tokens, w_key, preferred_element_type=jnp.float32).astype(jnp.bfloat16)
    keys = keys.reshape(length, key_heads, HEAD_DIM)
    values = jnp.dot(tokens, w_value, preferred_element_type=jnp.float32).astype(jnp.bfloat16)
    values = values.reshape(length, key_heads, HEAD_DIM)
    scores = jnp.einsum("qkgd,skd->kgqs", queries, keys, preferred_element_type=jnp.float32)
    scores = scores * (1.0 / math.sqrt(HEAD_DIM))
    query_pos = lax.broadcasted_iota(jnp.int32, (length, length), 0)
    key_pos = lax.broadcasted_iota(jnp.int32, (length, length), 1)
    scores = jnp.where(query_pos >= key_pos, scores, -jnp.inf)
    top = jnp.max(scores, axis=-1, keepdims=True)
    weights = jnp.exp(scores - top)
    probs = (weights / jnp.sum(weights, axis=-1, keepdims=True)).astype(jnp.bfloat16)
    mixed = jnp.einsum("kgqs,skd->qkgd", probs, values, preferred_element_type=jnp.float32)
    return mixed.astype(jnp.bfloat16).reshape(length, key_heads * group * HEAD_DIM)


def routing_table(routes, experts, capacity):
    number = routes.shape[0]
    same = routes[:, None] == routes[None, :]
    earlier = lax.broadcasted_iota(jnp.int32, (number, number), 1) < lax.broadcasted_iota(
        jnp.int32, (number, number), 0
    )
    slot = jnp.sum((same & earlier).astype(jnp.int32), axis=1)
    expert_hit = routes[None, :] == lax.broadcasted_iota(jnp.int32, (experts, number), 0)
    slot_hit = slot[None, :] == lax.broadcasted_iota(jnp.int32, (capacity, number), 0)
    return (expert_hit[:, None, :] & slot_hit[None, :, :]).astype(jnp.bfloat16)


def swap(value, axis):
    return lax.ppermute(value, axis, [(0, 1), (1, 0)])


def both(value, axis=0):
    if lax.axis_size("pair") == 1:
        return value
    return jnp.concatenate([value, swap(value, "pair")], axis=axis)


def pick(blocks, table):
    rows = jnp.einsum("cb,brd->crd", table, blocks, preferred_element_type=jnp.float32)
    return rows.astype(jnp.bfloat16)


def wo_gradient(cotangent, heads_out):
    length, width = cotangent.shape
    outer, pair = lax.axis_size("outer"), lax.axis_size("pair")
    parts = cotangent.reshape(length, outer, pair, width // (outer * pair))
    mine = lax.axis_index("pair")

    def part(number):
        return lax.dynamic_index_in_dim(parts, number, 2, keepdims=False).reshape(length, width // pair)

    left = part(mine)
    if pair == 2:
        left = jnp.concatenate([left, swap(part(1 - mine), "pair")], axis=0)
    term = lax.dot_general(
        left, both(heads_out), (((0,), (0,)), ((), ())), preferred_element_type=jnp.float32
    ).astype(jnp.bfloat16)
    return lax.psum_scatter(term, GROUP, scatter_dimension=0, tiled=True).astype(jnp.float32)


def per_device(
    tokens, w_query, w_key, w_value, w_out, w_gate, w_up, w_down, route, old_out, cotangent
):
    experts = lax.axis_size("expert")
    own = lax.axis_index("expert")
    length, width = tokens.shape
    blocks = length // BLOCK
    piece_rows = BLOCK // experts
    capacity = max(2, blocks // experts + 1)
    old_count = experts - max(1, experts // 4)
    routes = route[:, 0]
    table = routing_table(routes, experts, capacity)
    own_table = lax.dynamic_index_in_dim(table, own, 0, keepdims=False)
    token_rows = pick(tokens.reshape(blocks, BLOCK, width), own_table)

    heads_out = attend_local(tokens, w_query, w_key, w_value)
    head_blocks = heads_out.reshape(blocks, BLOCK, heads_out.shape[1])

    def project(rows):
        return jnp.dot(
            rows.reshape(-1, rows.shape[-1]), w_out, preferred_element_type=jnp.float32
        ).reshape(rows.shape[:-1] + (width,))

    if experts == 2:
        half = capacity * BLOCK // 2
        peer_table = lax.dynamic_index_in_dim(table, 1 - own, 0, keepdims=False)
        outgoing = project(pick(head_blocks, peer_table)).astype(jnp.bfloat16).reshape(-1, width)
        kept = project(pick(head_blocks, own_table)).reshape(-1, width)
        kept = kept + token_rows.reshape(-1, width).astype(jnp.float32)
        first = (kept[:half] + swap(outgoing[:half], "expert").astype(jnp.float32)).astype(jnp.bfloat16)
        second = (kept[half:] + swap(outgoing[half:], "expert").astype(jnp.float32)).astype(jnp.bfloat16)
    else:
        half = capacity * BLOCK // 2
        rows = jnp.einsum("jcb,brd->jcrd", table, head_blocks, preferred_element_type=jnp.float32)
        outgoing = project(rows.astype(jnp.bfloat16)).astype(jnp.bfloat16)
        total = lax.psum_scatter(outgoing, "expert", scatter_dimension=0, tiled=True)[0]
        total = (token_rows.astype(jnp.float32) + total.astype(jnp.float32)).astype(jnp.bfloat16)
        total = total.reshape(-1, width)
        first, second = total[:half], total[half:]

    gradient = wo_gradient(cotangent, heads_out)
    gate_rows, up_rows, down_rows = both(w_gate[0]), both(w_up[0]), both(w_down[0])
    contract = (((1,), (1,)), ((), ()))

    def expert(top, bottom):
        rows = jnp.concatenate([top, bottom], axis=0)
        gate = lax.dot_general(rows, gate_rows, contract, preferred_element_type=jnp.float32)
        lifted = lax.dot_general(rows, up_rows, contract, preferred_element_type=jnp.float32)
        active = (jax.nn.silu(gate) * lifted).astype(jnp.bfloat16)
        return jnp.dot(active, down_rows, preferred_element_type=jnp.float32)

    outer, section = lax.axis_size("outer"), lax.axis_size("section")
    ring = []
    for line in range(outer):
        places = [line * section + place for place in range(section)]
        ring += places if line % 2 == 0 else places[::-1]
    count = len(ring)
    onward = [(ring[i], ring[(i + 1) % count]) for i in range(count)]
    backward = [(target, source) for source, target in onward]
    front, back = first, second
    sums = None
    for _ in range(count - 1):
        front = lax.ppermute(front, GROUP, onward)
        back = lax.ppermute(back, GROUP, backward)
        terms = expert(front, back)
        upper, lower = terms[:half], terms[half:]
        if sums is not None:
            upper = upper + lax.ppermute(sums[0], GROUP, onward).astype(jnp.float32)
            lower = lower + lax.ppermute(sums[1], GROUP, backward).astype(jnp.float32)
        sums = (upper.astype(jnp.bfloat16), lower.astype(jnp.bfloat16))
    terms = expert(first, second)
    upper = terms[:half] + lax.ppermute(sums[0], GROUP, onward).astype(jnp.float32)
    lower = terms[half:] + lax.ppermute(sums[1], GROUP, backward).astype(jnp.float32)
    expert_sum = jnp.concatenate([upper, lower], axis=0)
    hidden = jnp.concatenate([first, second], axis=0).astype(jnp.float32)
    whole = (hidden + expert_sum.astype(jnp.bfloat16).astype(jnp.float32)).astype(jnp.bfloat16)
    whole = whole.reshape(capacity, experts, piece_rows, width)
    if experts == 2:
        mine = lax.dynamic_index_in_dim(whole, own, 1, keepdims=False)
        theirs = swap(lax.dynamic_index_in_dim(whole, 1 - own, 1, keepdims=False), "expert")
        joined = jnp.einsum("cb,crd->brd", own_table, mine, preferred_element_type=jnp.float32)
        joined = joined + jnp.einsum("cb,crd->brd", peer_table, theirs, preferred_element_type=jnp.float32)
    else:
        returned = lax.all_to_all(
            whole.transpose(1, 0, 2, 3), "expert", split_axis=0, concat_axis=0, tiled=True
        )
        joined = jnp.einsum("jcb,jcrd->brd", table, returned, preferred_element_type=jnp.float32)
    joined = joined.astype(jnp.bfloat16)
    fresh = (routes >= old_count).astype(jnp.float32)
    gap = joined.astype(jnp.float32) - old_out.astype(jnp.float32)
    divergence = 0.5 * jnp.mean(gap * gap, axis=-1) * fresh[:, None]
    return (joined, divergence, gradient)


MESH_ID = pl.DeviceIdType.MESH
NT = (((1,), (1,)), ((), ()))


def order_of(routes, first, capacity):
    number = routes.shape[0]
    certain = number - capacity
    same = routes[:, None] == routes[None, :]
    earlier = lax.broadcasted_iota(jnp.int32, (number, number), 1) < lax.broadcasted_iota(
        jnp.int32, (number, number), 0
    )
    slot = jnp.sum((same & earlier).astype(jnp.int32), axis=1)
    loose = slot >= certain
    rank = jnp.sum((loose[None, :] & earlier).astype(jnp.int32), axis=1)
    fixed = jnp.where(routes == first, slot, capacity + slot)
    place = jnp.where(loose, certain + rank, fixed)
    return place[None, :] == lax.broadcasted_iota(jnp.int32, (number, number), 0)


def moe_kernel(
    sure, loose, half,
    parcel_ref, kept_ref, gate_ref, up_ref, down_ref, term_ref, flag_ref,
    out_ref, grad_ref, far_ref, slot_ref,
    near_w, rows, sums, stage, stage_rest, part, far_act, act, gate_tile, up_tile, grad_in, term_in, grad_out, total_grad,
    kept_in, flags,
    row_send, row_recv, sum_send, sum_recv, grad_send, grad_recv, rest_send, rest_recv,
    pair_send, pair_recv, far_send, far_recv, fwd_send, fwd_recv, got_send, got_recv, flag_send, flag_recv,
    local_sem, free_sem,
):
    outer, section = lax.axis_size("outer"), lax.axis_size("section")
    count = outer * section
    x, z = lax.axis_index("outer"), lax.axis_index("section")
    spot = x * (count - 1) + z * (1 - 2 * x)

    def at(place):
        line = place // section
        within = place % section
        return {"outer": line, "section": within * (1 - 2 * line) + (section - 1) * line}

    onward, backward = at((spot + 1) % count), at((spot + count - 1) % count)
    partner = {"pair": 1 - lax.axis_index("pair")}
    peer = {"expert": 1 - lax.axis_index("expert")}
    ways = (onward, backward)
    total_rows, width = rows.shape[1:]
    side = total_rows // 2
    block = part.shape[1]
    layers = side // block
    wide = width // 2
    rest = side - sure
    tile = half
    tiles = near_w.shape[1] * near_w.shape[2] // tile
    per = near_w.shape[2] // tile
    chunk = 512
    weights = (gate_ref, up_ref, down_ref)

    barrier = pltpu.get_barrier_semaphore()
    for target in (onward, backward, partner, peer):
        pl.semaphore_signal(barrier, inc=1, device_id=target, device_id_type=MESH_ID)
    pl.semaphore_wait(barrier, 4)

    def remote(source, target, send, recv, device):
        return pltpu.make_async_remote_copy(
            src_ref=source, dst_ref=target, send_sem=send, recv_sem=recv, device_id=device, device_id_type=MESH_ID
        )

    def span(way):
        return pl.ds(way * side, side)

    def row_copy(way, piece, step):
        columns = pl.ds(piece * wide, wide)
        return remote(
            rows.at[step - 1, span(way), columns],
            rows.at[step, span(way), columns],
            row_send.at[way, piece, step],
            row_recv.at[way, piece, step],
            ways[way],
        )

    def flag_copy(way, step):
        return remote(
            flags.at[way, step - 1], flags.at[way, step], flag_send.at[way, step], flag_recv.at[way, step], ways[way]
        )

    def got_copy(way, piece):
        here = (pl.ds(way * layers, layers), slice(None), pl.ds(piece * wide, wide))
        return remote(parcel_ref.at[here], part.at[here], got_send.at[way, piece], got_recv.at[way, piece], peer)

    high, deep = grad_in.shape[1], grad_in.shape[2]

    def term_at(way, index):
        place = (spot + index) % count
        line = place // section
        within = place % section
        block = line * section + within * (1 - 2 * line) + (section - 1) * line
        return term_ref.at[pl.ds(pl.multiple_of(block * high, high), high), pl.ds(way * deep, deep)]

    def grad_copy(way, step, source):
        return remote(source, slot_ref.at[way, step], grad_send.at[way, step], grad_recv.at[way, step], ways[way])

    def sum_copy(way, step):
        here = pl.ds(way * sure, sure)
        return remote(stage.at[step % 2, here], sums.at[step, here], sum_send.at[way, step], sum_recv.at[way, step], ways[way])

    def rest_copy(way, half_index, step):
        here = pl.ds(way * rest, rest)
        there = pl.ds(sure + way * rest, rest)
        columns = pl.ds(half_index * (width // 2), width // 2)
        return remote(
            stage_rest.at[step % 2, here, columns],
            rows.at[step, there, columns],
            rest_send.at[way, half_index, step],
            rest_recv.at[way, half_index, step],
            ways[way],
        )

    def far_copy(which):
        return remote(weights[which], far_ref.at[which, 0], far_send.at[which], far_recv.at[which], peer)

    def forward_copy(which):
        return remote(far_ref.at[which, 0], far_ref.at[which, 1], fwd_send.at[which], fwd_recv.at[which], partner)

    def pair_copy(which):
        return remote(weights[which], near_w.at[which, 1], pair_send.at[which], pair_recv.at[which], partner)

    def local(source, target, place):
        return pltpu.make_async_copy(source, target, local_sem.at[place])

    def gradient_step(step):
        pulls = []
        for way in range(2):
            grad_copy(way, step, slot_ref.at[way, step]).wait_recv()
            pulls.append(local(slot_ref.at[way, step], grad_in.at[way], way))
            index = (2 * count - 1 - step) % count if way == 0 else (1 + step) % count
            pulls.append(local(term_at(way, index), term_in.at[way], 2 + way))
        for pull in pulls:
            pull.start()
        for pull in pulls:
            pull.wait()
        for way in range(2):
            value = grad_in[way].astype(jnp.float32) + term_in[way].astype(jnp.float32)

            step = jnp.asarray(step, jnp.int32)

            @pl.when(step < count - 1)
            def _():
                @pl.when(step >= 3)
                def _():
                    grad_copy(way, step - 1, grad_out.at[way, step % 2]).wait_send()

                grad_out[way, step % 2] = value.astype(jnp.bfloat16)
                grad_copy(way, step + 1, grad_out.at[way, step % 2]).start()

            @pl.when(step == count - 1)
            def _():
                total_grad[:, pl.ds(way * value.shape[1], value.shape[1])] = value

    for piece in range(2):
        for way in range(2):
            got_copy(way, piece).start()
    for which in range(3):
        far_copy(which).start()
    grad_copy(0, 1, term_at(0, count - 1)).start()
    grad_copy(1, 1, term_at(1, 1)).start()
    marks = [local(flag_ref, flags.at[way, 0], way) for way in range(2)]
    for mark in marks:
        mark.start()
    for mark in marks:
        mark.wait()
    for way in range(2):
        flag_copy(way, 1).start()
    loads = [local(weights[which], near_w.at[which, 0], 1 + which) for which in range(3)]
    for load in loads:
        load.start()
    for which in range(3):
        pair_copy(which).start()
    for load in loads:
        load.wait()
    for number in range(4):
        piece, way = number // 2, number % 2
        columns = pl.ds(piece * wide, wide)
        pull = local(kept_ref.at[pl.ds(way * layers, layers), :, columns], kept_in, 0)
        pull.start()
        pull.wait()
        got_copy(way, piece).wait_recv()

        def join(index, _):
            place = pl.ds(pl.multiple_of(way * side + index * block, block), block)
            value = kept_in[index] + part[way * layers + index, :, columns].astype(jnp.float32)
            rows[0, place, columns] = value.astype(jnp.bfloat16)
            return 0

        lax.fori_loop(0, layers, join, 0)
        row_copy(way, piece, 1).start()
        if number < 3:
            gradient_step(number + 1)
    for which in range(3):
        pair_copy(which).wait_recv()

    def gated(value, gate, up):
        pre = lax.dot_general(value, gate, NT, preferred_element_type=jnp.float32)
        lifted = lax.dot_general(value, up, NT, preferred_element_type=jnp.float32)
        return pre * (1.0 / (1.0 + jnp.exp(-pre))) * lifted

    def near_step(step):
        slot = step

        def one(index, _):
            place = pl.ds(pl.multiple_of((index % per) * tile, tile), tile)
            value = gated(rows[slot], near_w[0, index // per, place], near_w[1, index // per, place])
            act[index] = value.astype(jnp.bfloat16)
            return 0

        lax.fori_loop(0, tiles, one, 0)

        @pl.when(step >= 2)
        def _():
            for way in range(2):
                sum_copy(way, step - 1).wait_recv()

        @pl.when(step >= 3)
        def _():
            for way in range(2):
                sum_copy(way, step - 2).wait_send()

        def two(index, _):
            columns = pl.ds(pl.multiple_of(index * chunk, chunk), chunk)
            total = None
            for number in range(tiles):
                place = pl.ds((number % per) * tile, tile)
                term = jnp.dot(
                    act[number], near_w[2, number // per, place, columns], preferred_element_type=jnp.float32
                )
                total = term if total is None else total + term
            before = sums[jnp.maximum(step - 1, 0), :, columns].astype(jnp.float32)
            before = jnp.where(step >= 2, before, 0.0)
            stage[step % 2, 0:sure, columns] = (total[0:sure] + before[0:sure]).astype(jnp.bfloat16)
            stage[step % 2, sure : 2 * sure, columns] = (total[total_rows - sure :] + before[sure:]).astype(jnp.bfloat16)
            part[slot, 0:loose, columns] = jnp.where(
                flags[0, slot][:, 0:1] > 0, total[sure : sure + loose], 0.0
            ).astype(jnp.bfloat16)
            part[slot, loose : 2 * loose, columns] = jnp.where(
                flags[1, slot][:, 0:1] > 0, total[side : side + loose], 0.0
            ).astype(jnp.bfloat16)
            return 0

        lax.fori_loop(0, width // chunk, two, 0)

    def far_step(low, high):
        def one(index, _):
            place = pl.ds(pl.multiple_of((index % per) * tile, tile), tile)
            fetch = [
                local(far_ref.at[0, index // per, place], gate_tile, 0),
                local(far_ref.at[1, index // per, place], up_tile, 1),
            ]
            for item in fetch:
                item.start()
            for item in fetch:
                item.wait()

            def two(step, _):
                slot = step % count
                value = gated(rows[slot, sure : sure + 2 * rest], gate_tile[...], up_tile[...])
                for way in range(2):
                    base = way * rest
                    far_act[slot, index, base : base + loose] = jnp.where(
                        flags[way, slot][:, 0:1] > 0, 0.0, value[base : base + loose]
                    ).astype(jnp.bfloat16)
                    far_act[slot, index, base + loose : base + rest] = value[base + loose : base + rest].astype(
                        jnp.bfloat16
                    )
                return 0

            lax.fori_loop(low, high, two, 0)
            return 0

        lax.fori_loop(0, tiles, one, 0)

    def ring_step(step, _):
        @pl.when(step >= 1)
        def _():
            for piece in range(2):
                for way in range(2):
                    row_copy(way, piece, step).wait_recv()

                    @pl.when(step < count - 1)
                    def _():
                        row_copy(way, piece, step + 1).start()

            for way in range(2):
                flag_copy(way, step).wait_recv()

                @pl.when(step < count - 1)
                def _():
                    flag_copy(way, step + 1).start()

        @pl.when((step >= 1) & (step < count - 3))
        def _():
            gradient_step(step + 3)

        near_step(step)

        @pl.when(step >= 1)
        def _():
            for way in range(2):
                sum_copy(way, step).start()

        @pl.when(step == 0)
        def _():
            sums[0] = stage[0]

        for which, when in ((0, count // 2 - 1), (1, count - 3), (2, count - 1)):
            @pl.when(step == when)
            def _():
                far_copy(which).wait_recv()
                forward_copy(which).start()

        @pl.when(step == count - 3)
        def _():
            for which in range(2):
                forward_copy(which).wait_recv()

        @pl.when((step >= count - 3) & (step < count - 1))
        def _():
            low = 3 * (step - (count - 3))
            far_step(low, low + 3)

        return 0

    lax.fori_loop(0, count, ring_step, 0)

    for way in range(2):
        for step in range(1, count):
            flag_copy(way, step).wait_send()
            for piece in range(2):
                row_copy(way, piece, step).wait_send()

    def grant(turn):
        pl.semaphore_signal(free_sem.at[0, turn], inc=1, device_id=backward, device_id_type=MESH_ID)
        pl.semaphore_signal(free_sem.at[1, turn], inc=1, device_id=onward, device_id_type=MESH_ID)

    grant(0)
    pulls = [local(far_ref.at[2, 0], near_w.at[0, 0], 0), local(far_ref.at[2, 1], near_w.at[0, 1], 1)]
    pulls[0].start()
    forward_copy(2).wait_recv()
    pulls[1].start()
    for pull in pulls:
        pull.wait()

    def rest_step(step, _):
        slot = step % count

        def two(index, _):
            columns = pl.ds(pl.multiple_of(index * chunk, chunk), chunk)
            total = None
            for number in range(tiles):
                place = pl.ds((number % per) * tile, tile)
                term = jnp.dot(
                    far_act[slot, number], near_w[0, number // per, place, columns], preferred_element_type=jnp.float32
                )
                total = term if total is None else total + term
            piece = part[slot, :, columns].astype(jnp.float32)
            for way in range(2):
                base = way * rest
                near_w[1, 0, base : base + loose, columns] = (
                    total[base : base + loose] + piece[way * loose : (way + 1) * loose]
                ).astype(jnp.bfloat16)
                near_w[1, 0, base + loose : base + rest, columns] = total[base + loose : base + rest].astype(jnp.bfloat16)
            return 0

        lax.fori_loop(0, width // chunk, two, 0)

        for turn, when in ((0, 1), (1, count - 2)):
            @pl.when(step == when)
            def _():
                for way in range(2):
                    pl.semaphore_wait(free_sem.at[way, turn], 1)

        for half_index in range(2):
            for way in range(2):
                here = slice(way * rest, (way + 1) * rest)
                there = slice(sure + way * rest, sure + (way + 1) * rest)
                columns = slice(half_index * (width // 2), (half_index + 1) * (width // 2))

                @pl.when(step >= 3)
                def _():
                    rest_copy(way, half_index, step - 2).wait_send()

                @pl.when(step >= 2)
                def _():
                    rest_copy(way, half_index, step - 1).wait_recv()
                    stage_rest[step % 2, here, columns] = (
                        near_w[1, 0, here, columns].astype(jnp.float32) + rows[step - 1, there, columns].astype(jnp.float32)
                    ).astype(jnp.bfloat16)

                @pl.when(step < 2)
                def _():
                    stage_rest[step % 2, here, columns] = near_w[1, 0, here, columns]

                @pl.when(step < count)
                def _():
                    rest_copy(way, half_index, step).start()

        @pl.when(step == 1)
        def _():
            far_step(count - 2, count)
            grant(1)

        return 0

    lax.fori_loop(1, count + 1, rest_step, 0)
    for way in range(2):
        sum_copy(way, count - 1).wait_recv()

    def last(index, _):
        columns = pl.ds(pl.multiple_of(index * chunk, chunk), chunk)
        base = rows[0, :, columns].astype(jnp.float32)
        certain = sums[0, :, columns].astype(jnp.float32) + sums[count - 1, :, columns].astype(jnp.float32)
        certain = certain.astype(jnp.bfloat16).astype(jnp.float32)
        others = stage_rest[count % 2, :, columns].astype(jnp.float32)
        rows[0, 0:sure, columns] = (base[0:sure] + certain[0:sure]).astype(jnp.bfloat16)
        rows[0, sure : sure + 2 * rest, columns] = (base[sure : sure + 2 * rest] + others).astype(jnp.bfloat16)
        rows[0, total_rows - sure :, columns] = (base[total_rows - sure :] + certain[sure:]).astype(jnp.bfloat16)
        return 0

    lax.fori_loop(0, width // chunk, last, 0)
    pushes = [local(rows.at[0], out_ref, 0), local(total_grad, grad_ref, 1)]
    for push in pushes:
        push.start()
    for push in pushes:
        push.wait()
    for way in range(2):
        sum_copy(way, count - 2).wait_send()
        sum_copy(way, count - 1).wait_send()
        for half_index in range(2):
            rest_copy(way, half_index, count - 1).wait_send()
        grad_copy(way, 1, term_at(way, 0)).wait_send()
        for step in range(max(2, count - 2), count):
            grad_copy(way, step, grad_out.at[way, step % 2]).wait_send()
        for piece in range(2):
            got_copy(way, piece).wait_send()
    for which in range(3):
        pair_copy(which).wait_send()
        far_copy(which).wait_send()
        forward_copy(which).wait_send()


def project_kernel(theirs_ref, mine_ref, weight_ref, base_ref, parcel_ref, kept_ref):
    weight = weight_ref[...]
    parcel_ref[...] = jnp.dot(theirs_ref[...], weight, preferred_element_type=jnp.float32).astype(jnp.bfloat16)
    kept_ref[...] = jnp.dot(mine_ref[...], weight, preferred_element_type=jnp.float32) + base_ref[...].astype(jnp.float32)


def projected(theirs, mine, weight, base):
    count, depth = theirs.shape
    width = weight.shape[1]
    tile = 512
    whole = pl.BlockSpec((count, depth), lambda i: (0, 0))
    piece = pl.BlockSpec((count, tile), lambda i: (0, i))
    return pl.pallas_call(
        project_kernel,
        grid=(width // tile,),
        in_specs=[whole, whole, pl.BlockSpec((depth, tile), lambda i: (0, i)), piece],
        out_specs=[piece, piece],
        out_shape=(
            jax.ShapeDtypeStruct((count, width), jnp.bfloat16),
            jax.ShapeDtypeStruct((count, width), jnp.float32),
        ),
        cost_estimate=pl.CostEstimate(flops=4 * count * depth * width, bytes_accessed=2 * 10**7, transcendentals=0),
    )(theirs, mine, weight, base)


def two_experts(
    tokens, w_query, w_key, w_value, w_out, w_gate, w_up, w_down, route, old_out, cotangent
):
    own = lax.axis_index("expert")
    length, width = tokens.shape
    blocks = length // BLOCK
    piece = BLOCK // 2
    strip = piece // 2
    capacity = max(2, blocks // 2 + 1)
    certain = blocks - capacity
    free = blocks - 2 * certain
    sure, loose, rest = certain * strip, free * strip, capacity * strip
    side = blocks * strip
    routes = route[:, 0]
    outer, section = lax.axis_size("outer"), lax.axis_size("section")
    ring = []
    for line in range(outer):
        places = [line * section + place for place in range(section)]
        ring += places if line % 2 == 0 else places[::-1]
    count = len(ring)

    own_hit = order_of(routes, own, capacity)
    peer_hit = order_of(routes, 1 - own, capacity)
    own_table, peer_table = own_hit.astype(jnp.bfloat16), peer_hit.astype(jnp.bfloat16)
    sorted_routes = jnp.sum(jnp.where(own_hit, routes[None, :], 0), axis=1)
    loose_own = (sorted_routes[certain:capacity] == own).astype(jnp.float32)
    flag_rows = jnp.broadcast_to(jnp.repeat(loose_own, strip)[:, None], (loose, 128))

    heads_out = attend_local(tokens, w_query, w_key, w_value)

    def mine_of(value, place):
        cut = value.reshape(blocks, 2, 2, strip, value.shape[-1])
        return lax.dynamic_index_in_dim(cut, place, 1, keepdims=False)

    def arranged(value, table):
        depth = value.shape[-1]
        rows = jnp.einsum("pb,bfrd->fprd", table, value, preferred_element_type=jnp.float32)
        rows = rows.astype(jnp.bfloat16).reshape(2, side, depth)
        return jnp.concatenate([rows[0], rows[1, sure:], rows[1, :sure]], axis=0)

    theirs = arranged(mine_of(heads_out, 1 - own), peer_table)
    kept = arranged(mine_of(heads_out, own), own_table)
    base = arranged(mine_of(tokens, own), own_table)
    parcel, kept = projected(theirs, kept, w_out, base)

    core = lax.axis_index("pair")
    span = width // (outer * 2)

    def part(number):
        pieces = [
            lax.dynamic_slice_in_dim(cotangent, (line * 2 + number) * span, span, axis=1) for line in range(outer)
        ]
        return jnp.concatenate(pieces, axis=1)

    left = jnp.concatenate([part(core), swap(part(1 - core), "pair")], axis=0)
    term = lax.dot_general(
        left, both(heads_out), (((0,), (0,)), ((), ())), preferred_element_type=jnp.float32
    ).astype(jnp.bfloat16)
    high, deep = width // (2 * count), term.shape[1]

    hidden_units = w_gate.shape[1]
    half = hidden_units // 2
    tiles = 4
    any_space = pl.BlockSpec(memory_space=pl.ANY)
    low = jnp.bfloat16
    dma = pltpu.SemaphoreType.DMA
    out, gradient, _, _ = pl.pallas_call(
        functools.partial(moe_kernel, sure, loose, half),
        out_shape=(
            jax.ShapeDtypeStruct((2 * side, width), low),
            jax.ShapeDtypeStruct((high, deep), jnp.float32),
            jax.ShapeDtypeStruct((3, 2, hidden_units, width), low),
            jax.ShapeDtypeStruct((2, count, high, deep // 2), low),
        ),
        in_specs=[any_space] * 7,
        out_specs=[any_space] * 4,
        scratch_shapes=[
            pltpu.VMEM((3, 2, hidden_units, width), low),
            pltpu.VMEM((count, 2 * side, width), low),
            pltpu.VMEM((count, 2 * sure, width), low),
            pltpu.VMEM((2, 2 * sure, width), low),
            pltpu.VMEM((2, 2 * rest, width), low),
            pltpu.VMEM((count, 2 * loose, width), low),
            pltpu.VMEM((count, tiles, 2 * rest, half), low),
            pltpu.VMEM((tiles, 2 * side, half), low),
            pltpu.VMEM((half, width), low),
            pltpu.VMEM((half, width), low),
            pltpu.VMEM((2, high, deep // 2), low),
            pltpu.VMEM((2, high, deep // 2), low),
            pltpu.VMEM((2, 2, high, deep // 2), low),
            pltpu.VMEM((high, deep), jnp.float32),
            pltpu.VMEM((side // (2 * loose), 2 * loose, width // 2), jnp.float32),
            pltpu.VMEM((2, count, loose, 128), jnp.float32),
            dma((2, 2, count)), dma((2, 2, count)), dma((2, count)), dma((2, count)),
            dma((2, count)), dma((2, count)), dma((2, 2, count)), dma((2, 2, count)),
            dma((3,)), dma((3,)), dma((3,)), dma((3,)), dma((3,)), dma((3,)),
            dma((2, 2)), dma((2, 2)), dma((2, count)), dma((2, count)),
            dma((4,)), pltpu.SemaphoreType.REGULAR((2, 2)),
        ],
        compiler_params=pltpu.CompilerParams(
            collective_id=0, has_side_effects=True, vmem_limit_bytes=67043328
        ),
        cost_estimate=pl.CostEstimate(flops=10**11, bytes_accessed=10**8, transcendentals=0),
    )(
        parcel.reshape(-1, 2 * loose, width),
        kept.reshape(-1, 2 * loose, width),
        w_gate[0],
        w_up[0],
        w_down[0],
        term,
        flag_rows,
    )

    whole = jnp.stack([out[:side], jnp.concatenate([out[side + rest :], out[side : side + rest]], axis=0)], axis=0)
    whole = whole.reshape(2, blocks, strip, width)
    joined = jnp.einsum("pb,fprd->bfrd", own_table, whole, preferred_element_type=jnp.float32)
    joined = joined.astype(jnp.bfloat16).reshape(blocks, piece, width)
    fresh = (routes >= 1).astype(jnp.float32)
    gap = joined.astype(jnp.float32) - old_out.astype(jnp.float32)
    divergence = 0.5 * jnp.mean(gap * gap, axis=-1) * fresh[:, None]
    return (joined, divergence, gradient)


def solution(mesh):
    sizes = mesh.shape
    pair = 2 if sizes["dp"] % 2 == 0 else 1
    replicas_in_ring = sizes["dp"] // pair * sizes["section"]
    body = two_experts if sizes["expert"] == 2 and pair == 2 and replicas_in_ring == 8 else per_device
    split = Mesh(
        mesh.devices.reshape(sizes["dp"] // pair, pair, sizes["section"], sizes["expert"]),
        ("outer", "pair", "section", "expert"),
    )
    replicas = ("outer", "pair", "section")
    return jax.shard_map(
        body,
        mesh=split,
        in_specs=(
            P(replicas, None),
            P(None, "expert"),
            P(None, "expert"),
            P(None, "expert"),
            P("expert", None),
            P("expert", replicas, None),
            P("expert", replicas, None),
            P("expert", replicas, None),
            P(replicas, None),
            P(replicas, "expert", None),
            P(replicas, None),
        ),
        out_specs=(
            P(replicas, "expert", None),
            P(replicas, "expert"),
            P(replicas, "expert"),
        ),
        check_vma=False,
    )
```

```python
import functools
import math

import jax
import jax.numpy as jnp
from jax import lax
from jax.experimental import pallas as pl
from jax.experimental.pallas import tpu as pltpu
from jax.sharding import Mesh
from jax.sharding import PartitionSpec as P


HEAD_DIM = 128
BLOCK = 64
GROUP = ("outer", "section")


def attend_local(tokens, w_query, w_key, w_value):
    length = tokens.shape[0]
    key_heads = w_key.shape[1] // HEAD_DIM
    group = w_query.shape[1] // w_key.shape[1]
    queries = jnp.dot(tokens, w_query, preferred_element_type=jnp.float32).astype(jnp.bfloat16)
    queries = queries.reshape(length, key_heads, group, HEAD_DIM)
    keys = jnp.dot(tokens, w_key, preferred_element_type=jnp.float32).astype(jnp.bfloat16)
    keys = keys.reshape(length, key_heads, HEAD_DIM)
    values = jnp.dot(tokens, w_value, preferred_element_type=jnp.float32).astype(jnp.bfloat16)
    values = values.reshape(length, key_heads, HEAD_DIM)
    scores = jnp.einsum("qkgd,skd->kgqs", queries, keys, preferred_element_type=jnp.float32)
    scores = scores * (1.0 / math.sqrt(HEAD_DIM))
    query_pos = lax.broadcasted_iota(jnp.int32, (length, length), 0)
    key_pos = lax.broadcasted_iota(jnp.int32, (length, length), 1)
    scores = jnp.where(query_pos >= key_pos, scores, -jnp.inf)
    top = jnp.max(scores, axis=-1, keepdims=True)
    weights = jnp.exp(scores - top)
    probs = (weights / jnp.sum(weights, axis=-1, keepdims=True)).astype(jnp.bfloat16)
    mixed = jnp.einsum("kgqs,skd->qkgd", probs, values, preferred_element_type=jnp.float32)
    return mixed.astype(jnp.bfloat16).reshape(length, key_heads * group * HEAD_DIM)


def routing_table(routes, experts, capacity):
    number = routes.shape[0]
    same = routes[:, None] == routes[None, :]
    earlier = lax.broadcasted_iota(jnp.int32, (number, number), 1) < lax.broadcasted_iota(
        jnp.int32, (number, number), 0
    )
    slot = jnp.sum((same & earlier).astype(jnp.int32), axis=1)
    expert_hit = routes[None, :] == lax.broadcasted_iota(jnp.int32, (experts, number), 0)
    slot_hit = slot[None, :] == lax.broadcasted_iota(jnp.int32, (capacity, number), 0)
    return (expert_hit[:, None, :] & slot_hit[None, :, :]).astype(jnp.bfloat16)


def swap(value, axis):
    return lax.ppermute(value, axis, [(0, 1), (1, 0)])


def both(value, axis=0):
    if lax.axis_size("pair") == 1:
        return value
    return jnp.concatenate([value, swap(value, "pair")], axis=axis)


def pick(blocks, table):
    rows = jnp.einsum("cb,brd->crd", table, blocks, preferred_element_type=jnp.float32)
    return rows.astype(jnp.bfloat16)


def wo_gradient(cotangent, heads_out):
    length, width = cotangent.shape
    outer, pair = lax.axis_size("outer"), lax.axis_size("pair")
    parts = cotangent.reshape(length, outer, pair, width // (outer * pair))
    mine = lax.axis_index("pair")

    def part(number):
        return lax.dynamic_index_in_dim(parts, number, 2, keepdims=False).reshape(length, width // pair)

    left = part(mine)
    if pair == 2:
        left = jnp.concatenate([left, swap(part(1 - mine), "pair")], axis=0)
    term = lax.dot_general(
        left, both(heads_out), (((0,), (0,)), ((), ())), preferred_element_type=jnp.float32
    ).astype(jnp.bfloat16)
    return lax.psum_scatter(term, GROUP, scatter_dimension=0, tiled=True).astype(jnp.float32)


def per_device(
    tokens, w_query, w_key, w_value, w_out, w_gate, w_up, w_down, route, old_out, cotangent
):
    experts = lax.axis_size("expert")
    own = lax.axis_index("expert")
    length, width = tokens.shape
    blocks = length // BLOCK
    piece_rows = BLOCK // experts
    capacity = max(2, blocks // experts + 1)
    old_count = experts - max(1, experts // 4)
    routes = route[:, 0]
    table = routing_table(routes, experts, capacity)
    own_table = lax.dynamic_index_in_dim(table, own, 0, keepdims=False)
    token_rows = pick(tokens.reshape(blocks, BLOCK, width), own_table)

    heads_out = attend_local(tokens, w_query, w_key, w_value)
    head_blocks = heads_out.reshape(blocks, BLOCK, heads_out.shape[1])

    def project(rows):
        return jnp.dot(
            rows.reshape(-1, rows.shape[-1]), w_out, preferred_element_type=jnp.float32
        ).reshape(rows.shape[:-1] + (width,))

    if experts == 2:
        half = capacity * BLOCK // 2
        peer_table = lax.dynamic_index_in_dim(table, 1 - own, 0, keepdims=False)
        outgoing = project(pick(head_blocks, peer_table)).astype(jnp.bfloat16).reshape(-1, width)
        kept = project(pick(head_blocks, own_table)).reshape(-1, width)
        kept = kept + token_rows.reshape(-1, width).astype(jnp.float32)
        first = (kept[:half] + swap(outgoing[:half], "expert").astype(jnp.float32)).astype(jnp.bfloat16)
        second = (kept[half:] + swap(outgoing[half:], "expert").astype(jnp.float32)).astype(jnp.bfloat16)
    else:
        half = capacity * BLOCK // 2
        rows = jnp.einsum("jcb,brd->jcrd", table, head_blocks, preferred_element_type=jnp.float32)
        outgoing = project(rows.astype(jnp.bfloat16)).astype(jnp.bfloat16)
        total = lax.psum_scatter(outgoing, "expert", scatter_dimension=0, tiled=True)[0]
        total = (token_rows.astype(jnp.float32) + total.astype(jnp.float32)).astype(jnp.bfloat16)
        total = total.reshape(-1, width)
        first, second = total[:half], total[half:]

    gradient = wo_gradient(cotangent, heads_out)
    gate_rows, up_rows, down_rows = both(w_gate[0]), both(w_up[0]), both(w_down[0])
    contract = (((1,), (1,)), ((), ()))

    def expert(top, bottom):
        rows = jnp.concatenate([top, bottom], axis=0)
        gate = lax.dot_general(rows, gate_rows, contract, preferred_element_type=jnp.float32)
        lifted = lax.dot_general(rows, up_rows, contract, preferred_element_type=jnp.float32)
        active = (jax.nn.silu(gate) * lifted).astype(jnp.bfloat16)
        return jnp.dot(active, down_rows, preferred_element_type=jnp.float32)

    outer, section = lax.axis_size("outer"), lax.axis_size("section")
    ring = []
    for line in range(outer):
        places = [line * section + place for place in range(section)]
        ring += places if line % 2 == 0 else places[::-1]
    count = len(ring)
    onward = [(ring[i], ring[(i + 1) % count]) for i in range(count)]
    backward = [(target, source) for source, target in onward]
    front, back = first, second
    sums = None
    for _ in range(count - 1):
        front = lax.ppermute(front, GROUP, onward)
        back = lax.ppermute(back, GROUP, backward)
        terms = expert(front, back)
        upper, lower = terms[:half], terms[half:]
        if sums is not None:
            upper = upper + lax.ppermute(sums[0], GROUP, onward).astype(jnp.float32)
            lower = lower + lax.ppermute(sums[1], GROUP, backward).astype(jnp.float32)
        sums = (upper.astype(jnp.bfloat16), lower.astype(jnp.bfloat16))
    terms = expert(first, second)
    upper = terms[:half] + lax.ppermute(sums[0], GROUP, onward).astype(jnp.float32)
    lower = terms[half:] + lax.ppermute(sums[1], GROUP, backward).astype(jnp.float32)
    expert_sum = jnp.concatenate([upper, lower], axis=0)
    hidden = jnp.concatenate([first, second], axis=0).astype(jnp.float32)
    whole = (hidden + expert_sum.astype(jnp.bfloat16).astype(jnp.float32)).astype(jnp.bfloat16)
    whole = whole.reshape(capacity, experts, piece_rows, width)
    if experts == 2:
        mine = lax.dynamic_index_in_dim(whole, own, 1, keepdims=False)
        theirs = swap(lax.dynamic_index_in_dim(whole, 1 - own, 1, keepdims=False), "expert")
        joined = jnp.einsum("cb,crd->brd", own_table, mine, preferred_element_type=jnp.float32)
        joined = joined + jnp.einsum("cb,crd->brd", peer_table, theirs, preferred_element_type=jnp.float32)
    else:
        returned = lax.all_to_all(
            whole.transpose(1, 0, 2, 3), "expert", split_axis=0, concat_axis=0, tiled=True
        )
        joined = jnp.einsum("jcb,jcrd->brd", table, returned, preferred_element_type=jnp.float32)
    joined = joined.astype(jnp.bfloat16)
    fresh = (routes >= old_count).astype(jnp.float32)
    gap = joined.astype(jnp.float32) - old_out.astype(jnp.float32)
    divergence = 0.5 * jnp.mean(gap * gap, axis=-1) * fresh[:, None]
    return (joined, divergence, gradient)


MESH_ID = pl.DeviceIdType.MESH
NT = (((1,), (1,)), ((), ()))


def moe_kernel(
    sure, loose, half,
    parcel_ref, kept_ref, early_ref, gate_ref, up_ref, down_ref, term_ref, flag_ref,
    out_ref, grad_ref, far_ref, slot_ref,
    near_w, rows, sums, stage, stage_rest, part, far_act, act, gate_tile, up_tile, grad_in, term_in, grad_out, total_grad,
    kept_in, flags,
    row_send, row_recv, sum_send, sum_recv, grad_send, grad_recv, rest_send, rest_recv,
    pair_send, pair_recv, far_send, far_recv, fwd_send, fwd_recv, got_send, got_recv, flag_send, flag_recv,
    local_sem, free_sem,
):
    outer, section = lax.axis_size("outer"), lax.axis_size("section")
    count = outer * section
    x, z = lax.axis_index("outer"), lax.axis_index("section")
    spot = x * (count - 1) + z * (1 - 2 * x)

    def at(place):
        line = place // section
        within = place % section
        return {"outer": line, "section": within * (1 - 2 * line) + (section - 1) * line}

    onward, backward = at((spot + 1) % count), at((spot + count - 1) % count)
    partner = {"pair": 1 - lax.axis_index("pair")}
    peer = {"expert": 1 - lax.axis_index("expert")}
    ways = (onward, backward)
    total_rows, width = rows.shape[1:]
    side = total_rows // 2
    block = part.shape[1]
    layers = side // block
    wide = width // 2
    rest = side - sure
    tile = half
    tiles = near_w.shape[1] * near_w.shape[2] // tile
    per = near_w.shape[2] // tile
    chunk = 512
    weights = (gate_ref, up_ref, down_ref)

    barrier = pltpu.get_barrier_semaphore()
    for target in (onward, backward, partner, peer):
        pl.semaphore_signal(barrier, inc=1, device_id=target, device_id_type=MESH_ID)
    pl.semaphore_wait(barrier, 4)

    def remote(source, target, send, recv, device):
        return pltpu.make_async_remote_copy(
            src_ref=source, dst_ref=target, send_sem=send, recv_sem=recv, device_id=device, device_id_type=MESH_ID
        )

    def span(way):
        return pl.ds(way * side, side)

    def row_copy(way, piece, step):
        columns = pl.ds(piece * wide, wide)
        return remote(
            rows.at[step - 1, span(way), columns],
            rows.at[step, span(way), columns],
            row_send.at[way, piece, step],
            row_recv.at[way, piece, step],
            ways[way],
        )

    def flag_copy(way, step):
        return remote(
            flags.at[way, step - 1], flags.at[way, step], flag_send.at[way, step], flag_recv.at[way, step], ways[way]
        )

    def got_copy(way, piece):
        here = (pl.ds(way * layers, layers), slice(None), pl.ds(piece * wide, wide))
        return remote(parcel_ref.at[here], part.at[here], got_send.at[way, piece], got_recv.at[way, piece], peer)

    high, deep = grad_in.shape[1], grad_in.shape[2]

    def term_at(way, index):
        place = (spot + index) % count
        line = place // section
        within = place % section
        block = line * section + within * (1 - 2 * line) + (section - 1) * line
        return term_ref.at[pl.ds(pl.multiple_of(block * high, high), high), pl.ds(way * deep, deep)]

    def grad_copy(way, step, source):
        return remote(source, slot_ref.at[way, step], grad_send.at[way, step], grad_recv.at[way, step], ways[way])

    def sum_copy(way, step):
        here = pl.ds(way * sure, sure)
        return remote(stage.at[step % 2, here], sums.at[step, here], sum_send.at[way, step], sum_recv.at[way, step], ways[way])

    def rest_copy(way, half_index, step):
        here = pl.ds(way * rest, rest)
        there = pl.ds(sure + way * rest, rest)
        columns = pl.ds(half_index * (width // 2), width // 2)
        return remote(
            stage_rest.at[step % 2, here, columns],
            rows.at[step, there, columns],
            rest_send.at[way, half_index, step],
            rest_recv.at[way, half_index, step],
            ways[way],
        )

    late = pl.ds(tile, near_w.shape[2] - tile)
    head = pl.ds(0, tile)

    def far_copy(which):
        source, target = weights[which], far_ref.at[which, 0]
        if which == 0:
            source, target = source.at[late], target.at[late]
        return remote(source, target, far_send.at[which], far_recv.at[which], peer)

    def forward_copy(which):
        source, target = far_ref.at[which, 0], far_ref.at[which, 1]
        if which == 0:
            source, target = source.at[late], target.at[late]
        return remote(source, target, fwd_send.at[which], fwd_recv.at[which], partner)

    def early_copy():
        return remote(early_ref, far_ref.at[0, 1, head], fwd_send.at[3], fwd_recv.at[3], partner)

    def pair_copy(which):
        return remote(weights[which], near_w.at[which, 1], pair_send.at[which], pair_recv.at[which], partner)

    def local(source, target, place):
        return pltpu.make_async_copy(source, target, local_sem.at[place])

    def gradient_step(step):
        pulls = []
        for way in range(2):
            grad_copy(way, step, slot_ref.at[way, step]).wait_recv()
            pulls.append(local(slot_ref.at[way, step], grad_in.at[way], way))
            index = (2 * count - 1 - step) % count if way == 0 else (1 + step) % count
            pulls.append(local(term_at(way, index), term_in.at[way], 2 + way))
        for pull in pulls:
            pull.start()
        for pull in pulls:
            pull.wait()
        for way in range(2):
            value = grad_in[way].astype(jnp.float32) + term_in[way].astype(jnp.float32)

            step = jnp.asarray(step, jnp.int32)

            @pl.when(step < count - 1)
            def _():
                @pl.when(step >= 3)
                def _():
                    grad_copy(way, step - 1, grad_out.at[way, step % 2]).wait_send()

                grad_out[way, step % 2] = value.astype(jnp.bfloat16)
                grad_copy(way, step + 1, grad_out.at[way, step % 2]).start()

            @pl.when(step == count - 1)
            def _():
                total_grad[:, pl.ds(way * value.shape[1], value.shape[1])] = value

    for piece in range(2):
        for way in range(2):
            got_copy(way, piece).start()
    for which in range(3):
        far_copy(which).start()
    grad_copy(0, 1, term_at(0, count - 1)).start()
    grad_copy(1, 1, term_at(1, 1)).start()
    marks = [local(flag_ref, flags.at[way, 0], way) for way in range(2)]
    for mark in marks:
        mark.start()
    for mark in marks:
        mark.wait()
    for way in range(2):
        flag_copy(way, 1).start()
    loads = [local(weights[which], near_w.at[which, 0], 1 + which) for which in range(3)]
    for load in loads:
        load.start()
    for which in range(3):
        pair_copy(which).start()
    early_copy().start()
    for load in loads:
        load.wait()
    for number in range(4):
        piece, way = number // 2, number % 2
        columns = pl.ds(piece * wide, wide)
        pull = local(kept_ref.at[pl.ds(way * layers, layers), :, columns], kept_in, 0)
        pull.start()
        pull.wait()
        got_copy(way, piece).wait_recv()

        def join(index, _):
            place = pl.ds(pl.multiple_of(way * side + index * block, block), block)
            value = kept_in[index] + part[way * layers + index, :, columns].astype(jnp.float32)
            rows[0, place, columns] = value.astype(jnp.bfloat16)
            return 0

        lax.fori_loop(0, layers, join, 0)
        row_copy(way, piece, 1).start()
        if number < 3:
            gradient_step(number + 1)
    for which in range(3):
        pair_copy(which).wait_recv()

    def gated(value, gate, up):
        pre = lax.dot_general(value, gate, NT, preferred_element_type=jnp.float32)
        lifted = lax.dot_general(value, up, NT, preferred_element_type=jnp.float32)
        return pre * (1.0 / (1.0 + jnp.exp(-pre))) * lifted

    def near_step(step):
        slot = step

        def one(index, _):
            place = pl.ds(pl.multiple_of((index % per) * tile, tile), tile)
            value = gated(rows[slot], near_w[0, index // per, place], near_w[1, index // per, place])
            act[index] = value.astype(jnp.bfloat16)
            return 0

        lax.fori_loop(0, tiles, one, 0)

        @pl.when(step >= 2)
        def _():
            for way in range(2):
                sum_copy(way, step - 1).wait_recv()

        @pl.when(step >= 3)
        def _():
            for way in range(2):
                sum_copy(way, step - 2).wait_send()

        def two(index, _):
            columns = pl.ds(pl.multiple_of(index * chunk, chunk), chunk)
            total = None
            for number in range(tiles):
                place = pl.ds((number % per) * tile, tile)
                term = jnp.dot(
                    act[number], near_w[2, number // per, place, columns], preferred_element_type=jnp.float32
                )
                total = term if total is None else total + term
            before = sums[jnp.maximum(step - 1, 0), :, columns].astype(jnp.float32)
            before = jnp.where(step >= 2, before, 0.0)
            stage[step % 2, 0:sure, columns] = (total[0:sure] + before[0:sure]).astype(jnp.bfloat16)
            stage[step % 2, sure : 2 * sure, columns] = (total[total_rows - sure :] + before[sure:]).astype(jnp.bfloat16)
            part[slot, 0:loose, columns] = jnp.where(
                flags[0, slot][:, 0:1] > 0, total[sure : sure + loose], 0.0
            ).astype(jnp.bfloat16)
            part[slot, loose : 2 * loose, columns] = jnp.where(
                flags[1, slot][:, 0:1] > 0, total[side : side + loose], 0.0
            ).astype(jnp.bfloat16)
            return 0

        lax.fori_loop(0, width // chunk, two, 0)

    def far_step(low, high):
        def one(index, _):
            place = pl.ds(pl.multiple_of((index % per) * tile, tile), tile)
            gate_fetch = local(far_ref.at[0, index // per, place], gate_tile, 0)
            up_fetch = local(far_ref.at[1, index // per, place], up_tile, 1)

            @pl.when(index == 0)
            def _():
                fetch = local(early_ref, gate_tile, 0)
                fetch.start()
                fetch.wait()

            up_fetch.start()

            @pl.when(index > 0)
            def _():
                gate_fetch.start()
                gate_fetch.wait()

            up_fetch.wait()

            def two(step, _):
                slot = step % count
                value = gated(rows[slot, sure : sure + 2 * rest], gate_tile[...], up_tile[...])
                for way in range(2):
                    base = way * rest
                    far_act[slot, index, base : base + loose] = jnp.where(
                        flags[way, slot][:, 0:1] > 0, 0.0, value[base : base + loose]
                    ).astype(jnp.bfloat16)
                    far_act[slot, index, base + loose : base + rest] = value[base + loose : base + rest].astype(
                        jnp.bfloat16
                    )
                return 0

            lax.fori_loop(low, high, two, 0)
            return 0

        lax.fori_loop(0, tiles, one, 0)

    def ring_step(step, _):
        @pl.when(step >= 1)
        def _():
            for piece in range(2):
                for way in range(2):
                    row_copy(way, piece, step).wait_recv()

                    @pl.when(step < count - 1)
                    def _():
                        row_copy(way, piece, step + 1).start()

            for way in range(2):
                flag_copy(way, step).wait_recv()

                @pl.when(step < count - 1)
                def _():
                    flag_copy(way, step + 1).start()

        @pl.when((step >= 1) & (step < count - 3))
        def _():
            gradient_step(step + 3)

        near_step(step)

        @pl.when(step >= 1)
        def _():
            for way in range(2):
                sum_copy(way, step).start()

        @pl.when(step == 0)
        def _():
            sums[0] = stage[0]

        for which, when in ((0, count // 2 - 1), (1, count - 3), (2, count - 1)):
            @pl.when(step == when)
            def _():
                far_copy(which).wait_recv()
                forward_copy(which).start()

        @pl.when(step == count - 3)
        def _():
            early_copy().wait_recv()
            for which in range(2):
                forward_copy(which).wait_recv()

        @pl.when((step >= count - 3) & (step < count - 1))
        def _():
            low = 3 * (step - (count - 3))
            far_step(low, low + 3)

        return 0

    lax.fori_loop(0, count, ring_step, 0)

    for way in range(2):
        for step in range(1, count):
            flag_copy(way, step).wait_send()
            for piece in range(2):
                row_copy(way, piece, step).wait_send()

    def grant(turn):
        pl.semaphore_signal(free_sem.at[0, turn], inc=1, device_id=backward, device_id_type=MESH_ID)
        pl.semaphore_signal(free_sem.at[1, turn], inc=1, device_id=onward, device_id_type=MESH_ID)

    grant(0)
    pulls = [local(far_ref.at[2, 0], near_w.at[0, 0], 0), local(far_ref.at[2, 1], near_w.at[0, 1], 1)]
    pulls[0].start()
    forward_copy(2).wait_recv()
    pulls[1].start()
    for pull in pulls:
        pull.wait()

    def rest_step(step, _):
        slot = step % count

        def two(index, _):
            columns = pl.ds(pl.multiple_of(index * chunk, chunk), chunk)
            total = None
            for number in range(tiles):
                place = pl.ds((number % per) * tile, tile)
                term = jnp.dot(
                    far_act[slot, number], near_w[0, number // per, place, columns], preferred_element_type=jnp.float32
                )
                total = term if total is None else total + term
            piece = part[slot, :, columns].astype(jnp.float32)
            for way in range(2):
                base = way * rest
                near_w[1, 0, base : base + loose, columns] = (
                    total[base : base + loose] + piece[way * loose : (way + 1) * loose]
                ).astype(jnp.bfloat16)
                near_w[1, 0, base + loose : base + rest, columns] = total[base + loose : base + rest].astype(jnp.bfloat16)
            return 0

        lax.fori_loop(0, width // chunk, two, 0)

        for turn, when in ((0, 1), (1, count - 2)):
            @pl.when(step == when)
            def _():
                for way in range(2):
                    pl.semaphore_wait(free_sem.at[way, turn], 1)

        for half_index in range(2):
            for way in range(2):
                here = slice(way * rest, (way + 1) * rest)
                there = slice(sure + way * rest, sure + (way + 1) * rest)
                columns = slice(half_index * (width // 2), (half_index + 1) * (width // 2))

                @pl.when(step >= 3)
                def _():
                    rest_copy(way, half_index, step - 2).wait_send()

                @pl.when(step >= 2)
                def _():
                    rest_copy(way, half_index, step - 1).wait_recv()
                    stage_rest[step % 2, here, columns] = (
                        near_w[1, 0, here, columns].astype(jnp.float32) + rows[step - 1, there, columns].astype(jnp.float32)
                    ).astype(jnp.bfloat16)

                @pl.when(step < 2)
                def _():
                    stage_rest[step % 2, here, columns] = near_w[1, 0, here, columns]

                @pl.when(step < count)
                def _():
                    rest_copy(way, half_index, step).start()

        @pl.when(step == 1)
        def _():
            far_step(count - 2, count)
            grant(1)

        return 0

    lax.fori_loop(1, count + 1, rest_step, 0)
    for way in range(2):
        sum_copy(way, count - 1).wait_recv()

    def last(index, _):
        columns = pl.ds(pl.multiple_of(index * chunk, chunk), chunk)
        base = rows[0, :, columns].astype(jnp.float32)
        certain = sums[0, :, columns].astype(jnp.float32) + sums[count - 1, :, columns].astype(jnp.float32)
        certain = certain.astype(jnp.bfloat16).astype(jnp.float32)
        others = stage_rest[count % 2, :, columns].astype(jnp.float32)
        rows[0, 0:sure, columns] = (base[0:sure] + certain[0:sure]).astype(jnp.bfloat16)
        rows[0, sure : sure + 2 * rest, columns] = (base[sure : sure + 2 * rest] + others).astype(jnp.bfloat16)
        rows[0, total_rows - sure :, columns] = (base[total_rows - sure :] + certain[sure:]).astype(jnp.bfloat16)
        return 0

    lax.fori_loop(0, width // chunk, last, 0)
    pushes = [local(rows.at[0], out_ref, 0), local(total_grad, grad_ref, 1)]
    for push in pushes:
        push.start()
    for push in pushes:
        push.wait()
    for way in range(2):
        sum_copy(way, count - 2).wait_send()
        sum_copy(way, count - 1).wait_send()
        for half_index in range(2):
            rest_copy(way, half_index, count - 1).wait_send()
        grad_copy(way, 1, term_at(way, 0)).wait_send()
        for step in range(max(2, count - 2), count):
            grad_copy(way, step, grad_out.at[way, step % 2]).wait_send()
        for piece in range(2):
            got_copy(way, piece).wait_send()
    early_copy().wait_send()
    for which in range(3):
        pair_copy(which).wait_send()
        far_copy(which).wait_send()
        forward_copy(which).wait_send()


def attend_kernel(tokens_ref, query_ref, key_ref, value_ref, out_ref):
    tokens = tokens_ref[...]
    length = tokens.shape[0]
    low = jnp.bfloat16
    queries = jnp.dot(tokens, query_ref[...], preferred_element_type=jnp.float32).astype(low)
    keys = jnp.dot(tokens, key_ref[...], preferred_element_type=jnp.float32).astype(low)
    values = jnp.dot(tokens, value_ref[...], preferred_element_type=jnp.float32).astype(low)
    group = queries.shape[1] // keys.shape[1]
    step = 128 if length % 128 == 0 else length
    for head in range(queries.shape[1] // HEAD_DIM):
        across = slice(head * HEAD_DIM, (head + 1) * HEAD_DIM)
        shared = slice(head // group * HEAD_DIM, (head // group + 1) * HEAD_DIM)
        for start in range(0, length, step):
            end = start + step
            scores = lax.dot_general(
                queries[start:end, across], keys[:end, shared], NT, preferred_element_type=jnp.float32
            )
            scores = scores * (1.0 / math.sqrt(HEAD_DIM))
            query_pos = lax.broadcasted_iota(jnp.int32, scores.shape, 0) + start
            key_pos = lax.broadcasted_iota(jnp.int32, scores.shape, 1)
            scores = jnp.where(query_pos >= key_pos, scores, -jnp.inf)
            top = jnp.max(scores, axis=-1, keepdims=True)
            parts = jnp.exp(scores - top)
            probs = (parts / jnp.sum(parts, axis=-1, keepdims=True)).astype(low)
            mixed = jnp.dot(probs, values[:end, shared], preferred_element_type=jnp.float32)
            out_ref[start:end, across] = mixed.astype(low)


def attended(tokens, w_query, w_key, w_value):
    length, width = tokens.shape
    heads, keys = w_query.shape[1], w_key.shape[1]
    steps = 2 if keys // HEAD_DIM % 2 == 0 else 1
    wide, narrow = heads // steps, keys // steps
    return pl.pallas_call(
        attend_kernel,
        grid=(steps,),
        in_specs=[
            pl.BlockSpec((length, width), lambda i: (0, 0)),
            pl.BlockSpec((width, wide), lambda i: (0, i)),
            pl.BlockSpec((width, narrow), lambda i: (0, i)),
            pl.BlockSpec((width, narrow), lambda i: (0, i)),
        ],
        out_specs=pl.BlockSpec((length, wide), lambda i: (0, i)),
        out_shape=jax.ShapeDtypeStruct((length, heads), jnp.bfloat16),
        cost_estimate=pl.CostEstimate(
            flops=2 * length * width * (heads + 2 * keys), bytes_accessed=2 * width * (length + heads + 2 * keys), transcendentals=0
        ),
    )(tokens, w_query, w_key, w_value)


def project_kernel(
    capacity, route_ref, own_ref, heads_ref, weight_ref, tokens_ref, parcel_ref, kept_ref, place_ref, flag_ref, order_ref, picked
):
    strips, strip = order_ref.shape[1], heads_ref.shape[1]
    half = strips * strip
    blocks = strips // 2
    certain = blocks - capacity
    own = own_ref[0]

    @pl.when(pl.program_id(0) == 0)
    def _():
        routes = [route_ref[index] for index in range(blocks)]
        loose_before = jnp.int32(0)
        marks = [jnp.int32(0) for _ in range(blocks - 2 * certain)]
        for index in range(blocks):
            slot = jnp.int32(0)
            for other in range(index):
                slot = slot + jnp.where(routes[other] == routes[index], 1, 0)
            for which, first in ((0, 1 - own), (1, own)):
                fixed = jnp.where(routes[index] == first, slot, capacity + slot)
                place = jnp.where(slot >= certain, certain + loose_before, fixed)
                behind = blocks + (place + blocks - certain) % blocks
                strip_at = index * 4 + first * 2
                order_ref[which, place] = strip_at
                order_ref[which, behind] = strip_at + 1
                if which == 1:
                    place_ref[0, index] = place
                    place_ref[1, index] = behind
            for mark in range(len(marks)):
                mine = (slot >= certain) & (loose_before == mark) & (routes[index] == own)
                marks[mark] = marks[mark] + jnp.where(mine, 1, 0)
            loose_before = loose_before + jnp.where(slot >= certain, 1, 0)
        for mark, found in enumerate(marks):
            flag_ref[mark * strip : (mark + 1) * strip] = jnp.full((strip, 128), found.astype(jnp.float32))
        for which in range(2):
            for index in range(strips):
                start = which * half + index * strip
                picked[start : start + strip] = heads_ref[order_ref[which, index]]

    value = jnp.dot(picked[...], weight_ref[...], preferred_element_type=jnp.float32)
    parcel_ref[...] = value[:half].astype(jnp.bfloat16)
    for index in range(strips):
        here = slice(index * strip, (index + 1) * strip)
        kept_ref[here] = value[half + index * strip : half + (index + 1) * strip] + tokens_ref[
            order_ref[1, index]
        ].astype(jnp.float32)


def projected(routes, own, heads_out, weight, tokens, strip, capacity):
    depth, width = weight.shape
    blocks = routes.shape[0]
    count = 2 * blocks * strip
    strips = heads_out.shape[0] // strip
    free = blocks - 2 * (blocks - capacity)
    tile = 1024
    piece = pl.BlockSpec((count, tile), lambda i, route, own: (0, i))
    return pl.pallas_call(
        functools.partial(project_kernel, capacity),
        grid_spec=pltpu.PrefetchScalarGridSpec(
            num_scalar_prefetch=2,
            grid=(width // tile,),
            in_specs=[
                pl.BlockSpec((strips, strip, depth), lambda i, route, own: (0, 0, 0)),
                pl.BlockSpec((depth, tile), lambda i, route, own: (0, i)),
                pl.BlockSpec((strips, strip, tile), lambda i, route, own: (0, 0, i)),
            ],
            out_specs=[
                piece,
                piece,
                pl.BlockSpec((2, blocks), lambda i, route, own: (0, 0), memory_space=pltpu.SMEM),
                pl.BlockSpec((free * strip, 128), lambda i, route, own: (0, 0)),
            ],
            scratch_shapes=[pltpu.SMEM((2, 2 * blocks), jnp.int32), pltpu.VMEM((2 * count, depth), jnp.bfloat16)],
        ),
        out_shape=(
            jax.ShapeDtypeStruct((count, width), jnp.bfloat16),
            jax.ShapeDtypeStruct((count, width), jnp.float32),
            jax.ShapeDtypeStruct((2, blocks), jnp.int32),
            jax.ShapeDtypeStruct((free * strip, 128), jnp.float32),
        ),
        cost_estimate=pl.CostEstimate(flops=4 * count * depth * width, bytes_accessed=2 * 10**7, transcendentals=0),
    )(routes, own.reshape(1), heads_out.reshape(strips, strip, depth), weight, tokens.reshape(strips, strip, width))


def finish_kernel(place_ref, route_ref, front_ref, back_ref, old_ref, joined_ref, divergence_ref):
    strip = front_ref.shape[1]
    fresh = jnp.where(route_ref[pl.program_id(0)] >= 1, 1.0, 0.0)
    for index, source in enumerate((front_ref, back_ref)):
        here = slice(index * strip, (index + 1) * strip)
        value = source[0]
        joined_ref[0, here] = value
        gap = value.astype(jnp.float32) - old_ref[0, here].astype(jnp.float32)
        divergence_ref[0, here] = 0.5 * jnp.mean(gap * gap, axis=-1, keepdims=True) * fresh


def finished(place, fresh, out, old_out, strip):
    blocks, piece, width = old_out.shape
    whole = pl.BlockSpec((1, piece, width), lambda i, place, fresh: (i, 0, 0))
    return pl.pallas_call(
        finish_kernel,
        grid_spec=pltpu.PrefetchScalarGridSpec(
            num_scalar_prefetch=2,
            grid=(blocks,),
            in_specs=[
                pl.BlockSpec((1, strip, width), lambda i, place, fresh: (place[0, i], 0, 0)),
                pl.BlockSpec((1, strip, width), lambda i, place, fresh: (place[1, i], 0, 0)),
                whole,
            ],
            out_specs=[whole, pl.BlockSpec((1, piece, 1), lambda i, place, fresh: (i, 0, 0))],
        ),
        out_shape=(
            jax.ShapeDtypeStruct((blocks, piece, width), jnp.bfloat16),
            jax.ShapeDtypeStruct((blocks, piece, 1), jnp.float32),
        ),
    )(place, fresh, out.reshape(-1, strip, width), out.reshape(-1, strip, width), old_out)


def two_experts(
    tokens, w_query, w_key, w_value, w_out, w_gate, w_up, w_down, route, old_out, cotangent
):
    own = lax.axis_index("expert")
    length, width = tokens.shape
    blocks = length // BLOCK
    piece = BLOCK // 2
    strip = piece // 2
    capacity = max(2, blocks // 2 + 1)
    certain = blocks - capacity
    free = blocks - 2 * certain
    sure, loose, rest = certain * strip, free * strip, capacity * strip
    side = blocks * strip
    routes = route[:, 0]
    outer, section = lax.axis_size("outer"), lax.axis_size("section")
    ring = []
    for line in range(outer):
        places = [line * section + place for place in range(section)]
        ring += places if line % 2 == 0 else places[::-1]
    count = len(ring)

    early = swap(w_gate[0][: w_gate.shape[1] // 2], "expert")
    heads_out = attended(tokens, w_query, w_key, w_value)
    parcel, kept, place, flag_rows = projected(routes, own, heads_out, w_out, tokens, strip, capacity)

    core = lax.axis_index("pair")
    span = width // (outer * 2)

    def part(number):
        pieces = [
            lax.dynamic_slice_in_dim(cotangent, (line * 2 + number) * span, span, axis=1) for line in range(outer)
        ]
        return jnp.concatenate(pieces, axis=1)

    left = jnp.concatenate([part(core), swap(part(1 - core), "pair")], axis=0)
    term = lax.dot_general(
        left, both(heads_out), (((0,), (0,)), ((), ())), preferred_element_type=jnp.float32
    ).astype(jnp.bfloat16)
    high, deep = width // (2 * count), term.shape[1]

    hidden_units = w_gate.shape[1]
    half = hidden_units // 2
    tiles = 4
    any_space = pl.BlockSpec(memory_space=pl.ANY)
    low = jnp.bfloat16
    dma = pltpu.SemaphoreType.DMA
    out, gradient, _, _ = pl.pallas_call(
        functools.partial(moe_kernel, sure, loose, half),
        out_shape=(
            jax.ShapeDtypeStruct((2 * side, width), low),
            jax.ShapeDtypeStruct((high, deep), jnp.float32),
            jax.ShapeDtypeStruct((3, 2, hidden_units, width), low),
            jax.ShapeDtypeStruct((2, count, high, deep // 2), low),
        ),
        in_specs=[any_space] * 8,
        out_specs=[any_space] * 4,
        scratch_shapes=[
            pltpu.VMEM((3, 2, hidden_units, width), low),
            pltpu.VMEM((count, 2 * side, width), low),
            pltpu.VMEM((count, 2 * sure, width), low),
            pltpu.VMEM((2, 2 * sure, width), low),
            pltpu.VMEM((2, 2 * rest, width), low),
            pltpu.VMEM((count, 2 * loose, width), low),
            pltpu.VMEM((count, tiles, 2 * rest, half), low),
            pltpu.VMEM((tiles, 2 * side, half), low),
            pltpu.VMEM((half, width), low),
            pltpu.VMEM((half, width), low),
            pltpu.VMEM((2, high, deep // 2), low),
            pltpu.VMEM((2, high, deep // 2), low),
            pltpu.VMEM((2, 2, high, deep // 2), low),
            pltpu.VMEM((high, deep), jnp.float32),
            pltpu.VMEM((side // (2 * loose), 2 * loose, width // 2), jnp.float32),
            pltpu.VMEM((2, count, loose, 128), jnp.float32),
            dma((2, 2, count)), dma((2, 2, count)), dma((2, count)), dma((2, count)),
            dma((2, count)), dma((2, count)), dma((2, 2, count)), dma((2, 2, count)),
            dma((3,)), dma((3,)), dma((3,)), dma((3,)), dma((4,)), dma((4,)),
            dma((2, 2)), dma((2, 2)), dma((2, count)), dma((2, count)),
            dma((4,)), pltpu.SemaphoreType.REGULAR((2, 2)),
        ],
        compiler_params=pltpu.CompilerParams(
            collective_id=0, has_side_effects=True, vmem_limit_bytes=67043328
        ),
        cost_estimate=pl.CostEstimate(flops=10**11, bytes_accessed=10**8, transcendentals=0),
    )(
        parcel.reshape(-1, 2 * loose, width),
        kept.reshape(-1, 2 * loose, width),
        early,
        w_gate[0],
        w_up[0],
        w_down[0],
        term,
        flag_rows,
    )

    joined, divergence = finished(place, routes, out, old_out, strip)
    divergence = divergence.reshape(blocks, piece)
    return (joined, divergence, gradient)


def solution(mesh):
    sizes = mesh.shape
    pair = 2 if sizes["dp"] % 2 == 0 else 1
    replicas_in_ring = sizes["dp"] // pair * sizes["section"]
    body = two_experts if sizes["expert"] == 2 and pair == 2 and replicas_in_ring == 8 else per_device
    split = Mesh(
        mesh.devices.reshape(sizes["dp"] // pair, pair, sizes["section"], sizes["expert"]),
        ("outer", "pair", "section", "expert"),
    )
    replicas = ("outer", "pair", "section")
    return jax.shard_map(
        body,
        mesh=split,
        in_specs=(
            P(replicas, None),
            P(None, "expert"),
            P(None, "expert"),
            P(None, "expert"),
            P("expert", None),
            P("expert", replicas, None),
            P("expert", replicas, None),
            P("expert", replicas, None),
            P(replicas, None),
            P(replicas, "expert", None),
            P(replicas, None),
        ),
        out_specs=(
            P(replicas, "expert", None),
            P(replicas, "expert"),
            P(replicas, "expert"),
        ),
        check_vma=False,
    )
```

```python
import functools
import math

import jax
import jax.numpy as jnp
from jax import lax
from jax.experimental import pallas as pl
from jax.experimental.pallas import tpu as pltpu
from jax.sharding import Mesh
from jax.sharding import PartitionSpec as P


HEAD_DIM = 128
BLOCK = 64
GROUP = ("outer", "section")


def attend_local(tokens, w_query, w_key, w_value):
    length = tokens.shape[0]
    key_heads = w_key.shape[1] // HEAD_DIM
    group = w_query.shape[1] // w_key.shape[1]
    queries = jnp.dot(tokens, w_query, preferred_element_type=jnp.float32).astype(jnp.bfloat16)
    queries = queries.reshape(length, key_heads, group, HEAD_DIM)
    keys = jnp.dot(tokens, w_key, preferred_element_type=jnp.float32).astype(jnp.bfloat16)
    keys = keys.reshape(length, key_heads, HEAD_DIM)
    values = jnp.dot(tokens, w_value, preferred_element_type=jnp.float32).astype(jnp.bfloat16)
    values = values.reshape(length, key_heads, HEAD_DIM)
    scores = jnp.einsum("qkgd,skd->kgqs", queries, keys, preferred_element_type=jnp.float32)
    scores = scores * (1.0 / math.sqrt(HEAD_DIM))
    query_pos = lax.broadcasted_iota(jnp.int32, (length, length), 0)
    key_pos = lax.broadcasted_iota(jnp.int32, (length, length), 1)
    scores = jnp.where(query_pos >= key_pos, scores, -jnp.inf)
    top = jnp.max(scores, axis=-1, keepdims=True)
    weights = jnp.exp(scores - top)
    probs = (weights / jnp.sum(weights, axis=-1, keepdims=True)).astype(jnp.bfloat16)
    mixed = jnp.einsum("kgqs,skd->qkgd", probs, values, preferred_element_type=jnp.float32)
    return mixed.astype(jnp.bfloat16).reshape(length, key_heads * group * HEAD_DIM)


def routing_table(routes, experts, capacity):
    number = routes.shape[0]
    same = routes[:, None] == routes[None, :]
    earlier = lax.broadcasted_iota(jnp.int32, (number, number), 1) < lax.broadcasted_iota(
        jnp.int32, (number, number), 0
    )
    slot = jnp.sum((same & earlier).astype(jnp.int32), axis=1)
    expert_hit = routes[None, :] == lax.broadcasted_iota(jnp.int32, (experts, number), 0)
    slot_hit = slot[None, :] == lax.broadcasted_iota(jnp.int32, (capacity, number), 0)
    return (expert_hit[:, None, :] & slot_hit[None, :, :]).astype(jnp.bfloat16)


def swap(value, axis):
    return lax.ppermute(value, axis, [(0, 1), (1, 0)])


def both(value, axis=0):
    if lax.axis_size("pair") == 1:
        return value
    return jnp.concatenate([value, swap(value, "pair")], axis=axis)


def pick(blocks, table):
    rows = jnp.einsum("cb,brd->crd", table, blocks, preferred_element_type=jnp.float32)
    return rows.astype(jnp.bfloat16)


def wo_gradient(cotangent, heads_out):
    length, width = cotangent.shape
    outer, pair = lax.axis_size("outer"), lax.axis_size("pair")
    parts = cotangent.reshape(length, outer, pair, width // (outer * pair))
    mine = lax.axis_index("pair")

    def part(number):
        return lax.dynamic_index_in_dim(parts, number, 2, keepdims=False).reshape(length, width // pair)

    left = part(mine)
    if pair == 2:
        left = jnp.concatenate([left, swap(part(1 - mine), "pair")], axis=0)
    term = lax.dot_general(
        left, both(heads_out), (((0,), (0,)), ((), ())), preferred_element_type=jnp.float32
    ).astype(jnp.bfloat16)
    return lax.psum_scatter(term, GROUP, scatter_dimension=0, tiled=True).astype(jnp.float32)


def per_device(
    tokens, w_query, w_key, w_value, w_out, w_gate, w_up, w_down, route, old_out, cotangent
):
    experts = lax.axis_size("expert")
    own = lax.axis_index("expert")
    length, width = tokens.shape
    blocks = length // BLOCK
    piece_rows = BLOCK // experts
    capacity = max(2, blocks // experts + 1)
    old_count = experts - max(1, experts // 4)
    routes = route[:, 0]
    table = routing_table(routes, experts, capacity)
    own_table = lax.dynamic_index_in_dim(table, own, 0, keepdims=False)
    token_rows = pick(tokens.reshape(blocks, BLOCK, width), own_table)

    heads_out = attend_local(tokens, w_query, w_key, w_value)
    head_blocks = heads_out.reshape(blocks, BLOCK, heads_out.shape[1])

    def project(rows):
        return jnp.dot(
            rows.reshape(-1, rows.shape[-1]), w_out, preferred_element_type=jnp.float32
        ).reshape(rows.shape[:-1] + (width,))

    if experts == 2:
        half = capacity * BLOCK // 2
        peer_table = lax.dynamic_index_in_dim(table, 1 - own, 0, keepdims=False)
        outgoing = project(pick(head_blocks, peer_table)).astype(jnp.bfloat16).reshape(-1, width)
        kept = project(pick(head_blocks, own_table)).reshape(-1, width)
        kept = kept + token_rows.reshape(-1, width).astype(jnp.float32)
        first = (kept[:half] + swap(outgoing[:half], "expert").astype(jnp.float32)).astype(jnp.bfloat16)
        second = (kept[half:] + swap(outgoing[half:], "expert").astype(jnp.float32)).astype(jnp.bfloat16)
    else:
        half = capacity * BLOCK // 2
        rows = jnp.einsum("jcb,brd->jcrd", table, head_blocks, preferred_element_type=jnp.float32)
        outgoing = project(rows.astype(jnp.bfloat16)).astype(jnp.bfloat16)
        total = lax.psum_scatter(outgoing, "expert", scatter_dimension=0, tiled=True)[0]
        total = (token_rows.astype(jnp.float32) + total.astype(jnp.float32)).astype(jnp.bfloat16)
        total = total.reshape(-1, width)
        first, second = total[:half], total[half:]

    gradient = wo_gradient(cotangent, heads_out)
    gate_rows, up_rows, down_rows = both(w_gate[0]), both(w_up[0]), both(w_down[0])
    contract = (((1,), (1,)), ((), ()))

    def expert(top, bottom):
        rows = jnp.concatenate([top, bottom], axis=0)
        gate = lax.dot_general(rows, gate_rows, contract, preferred_element_type=jnp.float32)
        lifted = lax.dot_general(rows, up_rows, contract, preferred_element_type=jnp.float32)
        active = (jax.nn.silu(gate) * lifted).astype(jnp.bfloat16)
        return jnp.dot(active, down_rows, preferred_element_type=jnp.float32)

    outer, section = lax.axis_size("outer"), lax.axis_size("section")
    ring = []
    for line in range(outer):
        places = [line * section + place for place in range(section)]
        ring += places if line % 2 == 0 else places[::-1]
    count = len(ring)
    onward = [(ring[i], ring[(i + 1) % count]) for i in range(count)]
    backward = [(target, source) for source, target in onward]
    front, back = first, second
    sums = None
    for _ in range(count - 1):
        front = lax.ppermute(front, GROUP, onward)
        back = lax.ppermute(back, GROUP, backward)
        terms = expert(front, back)
        upper, lower = terms[:half], terms[half:]
        if sums is not None:
            upper = upper + lax.ppermute(sums[0], GROUP, onward).astype(jnp.float32)
            lower = lower + lax.ppermute(sums[1], GROUP, backward).astype(jnp.float32)
        sums = (upper.astype(jnp.bfloat16), lower.astype(jnp.bfloat16))
    terms = expert(first, second)
    upper = terms[:half] + lax.ppermute(sums[0], GROUP, onward).astype(jnp.float32)
    lower = terms[half:] + lax.ppermute(sums[1], GROUP, backward).astype(jnp.float32)
    expert_sum = jnp.concatenate([upper, lower], axis=0)
    hidden = jnp.concatenate([first, second], axis=0).astype(jnp.float32)
    whole = (hidden + expert_sum.astype(jnp.bfloat16).astype(jnp.float32)).astype(jnp.bfloat16)
    whole = whole.reshape(capacity, experts, piece_rows, width)
    if experts == 2:
        mine = lax.dynamic_index_in_dim(whole, own, 1, keepdims=False)
        theirs = swap(lax.dynamic_index_in_dim(whole, 1 - own, 1, keepdims=False), "expert")
        joined = jnp.einsum("cb,crd->brd", own_table, mine, preferred_element_type=jnp.float32)
        joined = joined + jnp.einsum("cb,crd->brd", peer_table, theirs, preferred_element_type=jnp.float32)
    else:
        returned = lax.all_to_all(
            whole.transpose(1, 0, 2, 3), "expert", split_axis=0, concat_axis=0, tiled=True
        )
        joined = jnp.einsum("jcb,jcrd->brd", table, returned, preferred_element_type=jnp.float32)
    joined = joined.astype(jnp.bfloat16)
    fresh = (routes >= old_count).astype(jnp.float32)
    gap = joined.astype(jnp.float32) - old_out.astype(jnp.float32)
    divergence = 0.5 * jnp.mean(gap * gap, axis=-1) * fresh[:, None]
    return (joined, divergence, gradient)


MESH_ID = pl.DeviceIdType.MESH
NT = (((1,), (1,)), ((), ()))


def moe_kernel(
    sure, loose, half,
    parcel_ref, kept_ref, early_ref, gate_ref, up_ref, down_ref, term_ref, flag_ref,
    out_ref, grad_ref, far_ref, slot_ref,
    near_w, rows, sums, stage, stage_rest, part, far_act, act, gate_tile, up_tile, grad_in, term_in, grad_out, total_grad,
    kept_in, flags,
    row_send, row_recv, sum_send, sum_recv, grad_send, grad_recv, rest_send, rest_recv,
    pair_send, pair_recv, far_send, far_recv, fwd_send, fwd_recv, got_send, got_recv, flag_send, flag_recv,
    local_sem, free_sem,
):
    outer, section = lax.axis_size("outer"), lax.axis_size("section")
    count = outer * section
    x, z = lax.axis_index("outer"), lax.axis_index("section")
    spot = x * (count - 1) + z * (1 - 2 * x)

    def at(place):
        line = place // section
        within = place % section
        return {"outer": line, "section": within * (1 - 2 * line) + (section - 1) * line}

    onward, backward = at((spot + 1) % count), at((spot + count - 1) % count)
    partner = {"pair": 1 - lax.axis_index("pair")}
    peer = {"expert": 1 - lax.axis_index("expert")}
    ways = (onward, backward)
    total_rows, width = rows.shape[1:]
    side = total_rows // 2
    block = part.shape[1]
    layers = side // block
    wide = width // 2
    rest = side - sure
    tile = half
    tiles = near_w.shape[1] * near_w.shape[2] // tile
    per = near_w.shape[2] // tile
    chunk = 512
    weights = (gate_ref, up_ref, down_ref)

    barrier = pltpu.get_barrier_semaphore()
    for target in (onward, backward, partner, peer):
        pl.semaphore_signal(barrier, inc=1, device_id=target, device_id_type=MESH_ID)
    pl.semaphore_wait(barrier, 4)

    def remote(source, target, send, recv, device):
        return pltpu.make_async_remote_copy(
            src_ref=source, dst_ref=target, send_sem=send, recv_sem=recv, device_id=device, device_id_type=MESH_ID
        )

    def span(way):
        return pl.ds(way * side, side)

    def row_copy(way, piece, step):
        columns = pl.ds(piece * wide, wide)
        return remote(
            rows.at[step - 1, span(way), columns],
            rows.at[step, span(way), columns],
            row_send.at[way, piece, step],
            row_recv.at[way, piece, step],
            ways[way],
        )

    def flag_copy(way, step):
        return remote(
            flags.at[way, step - 1], flags.at[way, step], flag_send.at[way, step], flag_recv.at[way, step], ways[way]
        )

    def got_copy(way, piece):
        here = (pl.ds(way * layers, layers), slice(None), pl.ds(piece * wide, wide))
        return remote(parcel_ref.at[here], part.at[here], got_send.at[way, piece], got_recv.at[way, piece], peer)

    high, deep = grad_in.shape[2], grad_in.shape[3]

    def term_at(way, index, part_index):
        place = (spot + index) % count
        line = place // section
        within = place % section
        block = (line * section + within * (1 - 2 * line) + (section - 1) * line) * 2 + part_index
        return term_ref.at[pl.ds(pl.multiple_of(block * high, high), high), pl.ds(way * deep, deep)]

    def grad_copy(way, part_index, step, source):
        return remote(
            source,
            slot_ref.at[way, part_index, step],
            grad_send.at[way, part_index, step],
            grad_recv.at[way, part_index, step],
            ways[way],
        )

    def sum_copy(way, step):
        here = pl.ds(way * sure, sure)
        return remote(stage.at[step % 2, here], sums.at[step, here], sum_send.at[way, step], sum_recv.at[way, step], ways[way])

    def rest_copy(way, half_index, step):
        here = pl.ds(way * rest, rest)
        there = pl.ds(sure + way * rest, rest)
        columns = pl.ds(half_index * (width // 2), width // 2)
        return remote(
            stage_rest.at[step % 2, here, columns],
            rows.at[step, there, columns],
            rest_send.at[way, half_index, step],
            rest_recv.at[way, half_index, step],
            ways[way],
        )

    late = pl.ds(tile, near_w.shape[2] - tile)
    head = pl.ds(0, tile)

    def far_copy(which):
        source, target = weights[which], far_ref.at[which, 0]
        if which == 0:
            source, target = source.at[late], target.at[late]
        return remote(source, target, far_send.at[which], far_recv.at[which], peer)

    def forward_copy(which):
        source, target = far_ref.at[which, 0], far_ref.at[which, 1]
        if which == 0:
            source, target = source.at[late], target.at[late]
        return remote(source, target, fwd_send.at[which], fwd_recv.at[which], partner)

    def early_copy():
        return remote(early_ref, far_ref.at[0, 1, head], fwd_send.at[3], fwd_recv.at[3], partner)

    def pair_copy(which):
        return remote(weights[which], near_w.at[which, 1], pair_send.at[which], pair_recv.at[which], partner)

    def local(source, target, place):
        return pltpu.make_async_copy(source, target, local_sem.at[place])

    def gradient_step(step):
        for part_index in range(2):
            for way in range(2):
                index = (2 * count - 1 - step) % count if way == 0 else (1 + step) % count
                local(term_at(way, index, part_index), term_in.at[way, part_index], 4 + 2 * way + part_index).start()
        for part_index in range(2):
            pulls = []
            for way in range(2):
                grad_copy(way, part_index, step, slot_ref.at[way, part_index, step]).wait_recv()
                pulls.append(local(slot_ref.at[way, part_index, step], grad_in.at[way, part_index], 2 * way + part_index))
                pulls[-1].start()
            for way in range(2):
                pulls[way].wait()
                local(term_at(way, 0, part_index), term_in.at[way, part_index], 4 + 2 * way + part_index).wait()
                value = grad_in[way, part_index].astype(jnp.float32) + term_in[way, part_index].astype(jnp.float32)
                if step < count - 1:
                    if step >= 3:
                        grad_copy(way, part_index, step - 1, grad_out.at[way, part_index, step % 2]).wait_send()
                    grad_out[way, part_index, step % 2] = value.astype(jnp.bfloat16)
                    grad_copy(way, part_index, step + 1, grad_out.at[way, part_index, step % 2]).start()
                else:
                    total_grad[pl.ds(part_index * high, high), pl.ds(way * deep, deep)] = value

    for piece in range(2):
        for way in range(2):
            got_copy(way, piece).start()
    for which in range(3):
        far_copy(which).start()
    for part_index in range(2):
        grad_copy(0, part_index, 1, term_at(0, count - 1, part_index)).start()
        grad_copy(1, part_index, 1, term_at(1, 1, part_index)).start()
    marks = [local(flag_ref, flags.at[way, 0], way) for way in range(2)]
    for mark in marks:
        mark.start()
    for mark in marks:
        mark.wait()
    for way in range(2):
        flag_copy(way, 1).start()
    loads = [local(weights[which], near_w.at[which, 0], 1 + which) for which in range(3)]
    for load in loads:
        load.start()
    for which in range(3):
        pair_copy(which).start()
    early_copy().start()
    for load in loads:
        load.wait()
    for number in range(4):
        piece, way = number // 2, number % 2
        columns = pl.ds(piece * wide, wide)
        pull = local(kept_ref.at[pl.ds(way * layers, layers), :, columns], kept_in, 0)
        pull.start()
        pull.wait()
        got_copy(way, piece).wait_recv()

        def join(index, _):
            place = pl.ds(pl.multiple_of(way * side + index * block, block), block)
            value = kept_in[index] + part[way * layers + index, :, columns].astype(jnp.float32)
            rows[0, place, columns] = value.astype(jnp.bfloat16)
            return 0

        lax.fori_loop(0, layers, join, 0)
        row_copy(way, piece, 1).start()
        for step in range(2 * number + 1, min(2 * number + 3, count)):
            gradient_step(step)
    for which in range(3):
        pair_copy(which).wait_recv()

    def gated(value, gate, up):
        pre = lax.dot_general(value, gate, NT, preferred_element_type=jnp.float32)
        lifted = lax.dot_general(value, up, NT, preferred_element_type=jnp.float32)
        return pre * (1.0 / (1.0 + jnp.exp(-pre))) * lifted

    def near_step(step):
        slot = step

        def one(index, _):
            place = pl.ds(pl.multiple_of((index % per) * tile, tile), tile)
            value = gated(rows[slot], near_w[0, index // per, place], near_w[1, index // per, place])
            act[index] = value.astype(jnp.bfloat16)
            return 0

        lax.fori_loop(0, tiles, one, 0)

        @pl.when(step >= 2)
        def _():
            for way in range(2):
                sum_copy(way, step - 1).wait_recv()

        @pl.when(step >= 3)
        def _():
            for way in range(2):
                sum_copy(way, step - 2).wait_send()

        def two(index, _):
            columns = pl.ds(pl.multiple_of(index * chunk, chunk), chunk)
            total = None
            for number in range(tiles):
                place = pl.ds((number % per) * tile, tile)
                term = jnp.dot(
                    act[number], near_w[2, number // per, place, columns], preferred_element_type=jnp.float32
                )
                total = term if total is None else total + term
            before = sums[jnp.maximum(step - 1, 0), :, columns].astype(jnp.float32)
            before = jnp.where(step >= 2, before, 0.0)
            stage[step % 2, 0:sure, columns] = (total[0:sure] + before[0:sure]).astype(jnp.bfloat16)
            stage[step % 2, sure : 2 * sure, columns] = (total[total_rows - sure :] + before[sure:]).astype(jnp.bfloat16)
            part[slot, 0:loose, columns] = jnp.where(
                flags[0, slot][:, 0:1] > 0, total[sure : sure + loose], 0.0
            ).astype(jnp.bfloat16)
            part[slot, loose : 2 * loose, columns] = jnp.where(
                flags[1, slot][:, 0:1] > 0, total[side : side + loose], 0.0
            ).astype(jnp.bfloat16)
            return 0

        lax.fori_loop(0, width // chunk, two, 0)

    def far_step(low, high):
        def one(index, _):
            place = pl.ds(pl.multiple_of((index % per) * tile, tile), tile)
            gate_fetch = local(far_ref.at[0, index // per, place], gate_tile, 0)
            up_fetch = local(far_ref.at[1, index // per, place], up_tile, 1)

            @pl.when(index == 0)
            def _():
                fetch = local(early_ref, gate_tile, 0)
                fetch.start()
                fetch.wait()

            up_fetch.start()

            @pl.when(index > 0)
            def _():
                gate_fetch.start()
                gate_fetch.wait()

            up_fetch.wait()

            def two(step, _):
                slot = step % count
                value = gated(rows[slot, sure : sure + 2 * rest], gate_tile[...], up_tile[...])
                for way in range(2):
                    base = way * rest
                    far_act[slot, index, base : base + loose] = jnp.where(
                        flags[way, slot][:, 0:1] > 0, 0.0, value[base : base + loose]
                    ).astype(jnp.bfloat16)
                    far_act[slot, index, base + loose : base + rest] = value[base + loose : base + rest].astype(
                        jnp.bfloat16
                    )
                return 0

            lax.fori_loop(low, high, two, 0)
            return 0

        lax.fori_loop(0, tiles, one, 0)

    def ring_step(step, _):
        @pl.when(step >= 1)
        def _():
            for piece in range(2):
                for way in range(2):
                    row_copy(way, piece, step).wait_recv()

                    @pl.when(step < count - 1)
                    def _():
                        row_copy(way, piece, step + 1).start()

            for way in range(2):
                flag_copy(way, step).wait_recv()

                @pl.when(step < count - 1)
                def _():
                    flag_copy(way, step + 1).start()

        near_step(step)

        @pl.when(step >= 1)
        def _():
            for way in range(2):
                sum_copy(way, step).start()

        @pl.when(step == 0)
        def _():
            sums[0] = stage[0]

        for which, when in ((0, count // 2 - 1), (1, count - 3), (2, count - 1)):
            @pl.when(step == when)
            def _():
                far_copy(which).wait_recv()
                forward_copy(which).start()

        @pl.when(step == count - 3)
        def _():
            early_copy().wait_recv()
            for which in range(2):
                forward_copy(which).wait_recv()

        @pl.when((step >= count - 3) & (step < count - 1))
        def _():
            low = 3 * (step - (count - 3))
            far_step(low, low + 3)

        return 0

    lax.fori_loop(0, count, ring_step, 0)

    for way in range(2):
        for step in range(1, count):
            flag_copy(way, step).wait_send()
            for piece in range(2):
                row_copy(way, piece, step).wait_send()

    def grant(turn):
        pl.semaphore_signal(free_sem.at[0, turn], inc=1, device_id=backward, device_id_type=MESH_ID)
        pl.semaphore_signal(free_sem.at[1, turn], inc=1, device_id=onward, device_id_type=MESH_ID)

    grant(0)
    pulls = [local(far_ref.at[2, 0], near_w.at[0, 0], 0), local(far_ref.at[2, 1], near_w.at[0, 1], 1)]
    pulls[0].start()
    forward_copy(2).wait_recv()
    pulls[1].start()
    for pull in pulls:
        pull.wait()

    def rest_step(step, _):
        slot = step % count

        def two(index, _):
            columns = pl.ds(pl.multiple_of(index * chunk, chunk), chunk)
            total = None
            for number in range(tiles):
                place = pl.ds((number % per) * tile, tile)
                term = jnp.dot(
                    far_act[slot, number], near_w[0, number // per, place, columns], preferred_element_type=jnp.float32
                )
                total = term if total is None else total + term
            piece = part[slot, :, columns].astype(jnp.float32)
            for way in range(2):
                base = way * rest
                near_w[1, 0, base : base + loose, columns] = (
                    total[base : base + loose] + piece[way * loose : (way + 1) * loose]
                ).astype(jnp.bfloat16)
                near_w[1, 0, base + loose : base + rest, columns] = total[base + loose : base + rest].astype(jnp.bfloat16)
            return 0

        lax.fori_loop(0, width // chunk, two, 0)

        for turn, when in ((0, 1), (1, count - 2)):
            @pl.when(step == when)
            def _():
                for way in range(2):
                    pl.semaphore_wait(free_sem.at[way, turn], 1)

        for half_index in range(2):
            for way in range(2):
                here = slice(way * rest, (way + 1) * rest)
                there = slice(sure + way * rest, sure + (way + 1) * rest)
                columns = slice(half_index * (width // 2), (half_index + 1) * (width // 2))

                @pl.when(step >= 3)
                def _():
                    rest_copy(way, half_index, step - 2).wait_send()

                @pl.when(step >= 2)
                def _():
                    rest_copy(way, half_index, step - 1).wait_recv()
                    stage_rest[step % 2, here, columns] = (
                        near_w[1, 0, here, columns].astype(jnp.float32) + rows[step - 1, there, columns].astype(jnp.float32)
                    ).astype(jnp.bfloat16)

                @pl.when(step < 2)
                def _():
                    stage_rest[step % 2, here, columns] = near_w[1, 0, here, columns]

                @pl.when(step < count)
                def _():
                    rest_copy(way, half_index, step).start()

        @pl.when(step == 1)
        def _():
            far_step(count - 2, count)
            grant(1)

        return 0

    lax.fori_loop(1, count + 1, rest_step, 0)
    for way in range(2):
        sum_copy(way, count - 1).wait_recv()

    def last(index, _):
        columns = pl.ds(pl.multiple_of(index * chunk, chunk), chunk)
        base = rows[0, :, columns].astype(jnp.float32)
        certain = sums[0, :, columns].astype(jnp.float32) + sums[count - 1, :, columns].astype(jnp.float32)
        certain = certain.astype(jnp.bfloat16).astype(jnp.float32)
        others = stage_rest[count % 2, :, columns].astype(jnp.float32)
        rows[0, 0:sure, columns] = (base[0:sure] + certain[0:sure]).astype(jnp.bfloat16)
        rows[0, sure : sure + 2 * rest, columns] = (base[sure : sure + 2 * rest] + others).astype(jnp.bfloat16)
        rows[0, total_rows - sure :, columns] = (base[total_rows - sure :] + certain[sure:]).astype(jnp.bfloat16)
        return 0

    lax.fori_loop(0, width // chunk, last, 0)
    pushes = [local(rows.at[0], out_ref, 0), local(total_grad, grad_ref, 1)]
    for push in pushes:
        push.start()
    for push in pushes:
        push.wait()
    for way in range(2):
        sum_copy(way, count - 2).wait_send()
        sum_copy(way, count - 1).wait_send()
        for half_index in range(2):
            rest_copy(way, half_index, count - 1).wait_send()
        for part_index in range(2):
            grad_copy(way, part_index, 1, term_at(way, 0, part_index)).wait_send()
            for step in range(max(2, count - 2), count):
                grad_copy(way, part_index, step, grad_out.at[way, part_index, step % 2]).wait_send()
        for piece in range(2):
            got_copy(way, piece).wait_send()
    early_copy().wait_send()
    for which in range(3):
        pair_copy(which).wait_send()
        far_copy(which).wait_send()
        forward_copy(which).wait_send()


def attend_kernel(tokens_ref, query_ref, key_ref, value_ref, out_ref):
    tokens = tokens_ref[...]
    length = tokens.shape[0]
    low = jnp.bfloat16
    queries = jnp.dot(tokens, query_ref[...], preferred_element_type=jnp.float32).astype(low)
    keys = jnp.dot(tokens, key_ref[...], preferred_element_type=jnp.float32).astype(low)
    values = jnp.dot(tokens, value_ref[...], preferred_element_type=jnp.float32).astype(low)
    group = queries.shape[1] // keys.shape[1]
    step = 128 if length % 128 == 0 else length
    for head in range(queries.shape[1] // HEAD_DIM):
        across = slice(head * HEAD_DIM, (head + 1) * HEAD_DIM)
        shared = slice(head // group * HEAD_DIM, (head // group + 1) * HEAD_DIM)
        for start in range(0, length, step):
            end = start + step
            scores = lax.dot_general(
                queries[start:end, across], keys[:end, shared], NT, preferred_element_type=jnp.float32
            )
            scores = scores * (1.0 / math.sqrt(HEAD_DIM))
            query_pos = lax.broadcasted_iota(jnp.int32, scores.shape, 0) + start
            key_pos = lax.broadcasted_iota(jnp.int32, scores.shape, 1)
            scores = jnp.where(query_pos >= key_pos, scores, -jnp.inf)
            top = jnp.max(scores, axis=-1, keepdims=True)
            parts = jnp.exp(scores - top)
            probs = (parts / jnp.sum(parts, axis=-1, keepdims=True)).astype(low)
            mixed = jnp.dot(probs, values[:end, shared], preferred_element_type=jnp.float32)
            out_ref[start:end, across] = mixed.astype(low)


def attended(tokens, w_query, w_key, w_value):
    length, width = tokens.shape
    heads, keys = w_query.shape[1], w_key.shape[1]
    steps = 2 if keys // HEAD_DIM % 2 == 0 else 1
    wide, narrow = heads // steps, keys // steps
    return pl.pallas_call(
        attend_kernel,
        grid=(steps,),
        in_specs=[
            pl.BlockSpec((length, width), lambda i: (0, 0)),
            pl.BlockSpec((width, wide), lambda i: (0, i)),
            pl.BlockSpec((width, narrow), lambda i: (0, i)),
            pl.BlockSpec((width, narrow), lambda i: (0, i)),
        ],
        out_specs=pl.BlockSpec((length, wide), lambda i: (0, i)),
        out_shape=jax.ShapeDtypeStruct((length, heads), jnp.bfloat16),
        cost_estimate=pl.CostEstimate(
            flops=2 * length * width * (heads + 2 * keys), bytes_accessed=2 * width * (length + heads + 2 * keys), transcendentals=0
        ),
    )(tokens, w_query, w_key, w_value)


def project_kernel(
    capacity, route_ref, own_ref, heads_ref, weight_ref, tokens_ref, parcel_ref, kept_ref, place_ref, flag_ref, order_ref, picked
):
    strips, strip = order_ref.shape[1], heads_ref.shape[1]
    half = strips * strip
    blocks = strips // 2
    certain = blocks - capacity
    own = own_ref[0]

    @pl.when(pl.program_id(0) == 0)
    def _():
        routes = [route_ref[index] for index in range(blocks)]
        loose_before = jnp.int32(0)
        marks = [jnp.int32(0) for _ in range(blocks - 2 * certain)]
        for index in range(blocks):
            slot = jnp.int32(0)
            for other in range(index):
                slot = slot + jnp.where(routes[other] == routes[index], 1, 0)
            for which, first in ((0, 1 - own), (1, own)):
                fixed = jnp.where(routes[index] == first, slot, capacity + slot)
                place = jnp.where(slot >= certain, certain + loose_before, fixed)
                behind = blocks + (place + blocks - certain) % blocks
                strip_at = index * 4 + first * 2
                order_ref[which, place] = strip_at
                order_ref[which, behind] = strip_at + 1
                if which == 1:
                    place_ref[0, index] = place
                    place_ref[1, index] = behind
            for mark in range(len(marks)):
                mine = (slot >= certain) & (loose_before == mark) & (routes[index] == own)
                marks[mark] = marks[mark] + jnp.where(mine, 1, 0)
            loose_before = loose_before + jnp.where(slot >= certain, 1, 0)
        for mark, found in enumerate(marks):
            flag_ref[mark * strip : (mark + 1) * strip] = jnp.full((strip, 128), found.astype(jnp.float32))
        for which in range(2):
            for index in range(strips):
                start = which * half + index * strip
                picked[start : start + strip] = heads_ref[order_ref[which, index]]

    value = jnp.dot(picked[...], weight_ref[...], preferred_element_type=jnp.float32)
    parcel_ref[...] = value[:half].astype(jnp.bfloat16)
    for index in range(strips):
        here = slice(index * strip, (index + 1) * strip)
        kept_ref[here] = value[half + index * strip : half + (index + 1) * strip] + tokens_ref[
            order_ref[1, index]
        ].astype(jnp.float32)


def projected(routes, own, heads_out, weight, tokens, strip, capacity):
    depth, width = weight.shape
    blocks = routes.shape[0]
    count = 2 * blocks * strip
    strips = heads_out.shape[0] // strip
    free = blocks - 2 * (blocks - capacity)
    tile = 1024
    piece = pl.BlockSpec((count, tile), lambda i, route, own: (0, i))
    return pl.pallas_call(
        functools.partial(project_kernel, capacity),
        grid_spec=pltpu.PrefetchScalarGridSpec(
            num_scalar_prefetch=2,
            grid=(width // tile,),
            in_specs=[
                pl.BlockSpec((strips, strip, depth), lambda i, route, own: (0, 0, 0)),
                pl.BlockSpec((depth, tile), lambda i, route, own: (0, i)),
                pl.BlockSpec((strips, strip, tile), lambda i, route, own: (0, 0, i)),
            ],
            out_specs=[
                piece,
                piece,
                pl.BlockSpec((2, blocks), lambda i, route, own: (0, 0), memory_space=pltpu.SMEM),
                pl.BlockSpec((free * strip, 128), lambda i, route, own: (0, 0)),
            ],
            scratch_shapes=[pltpu.SMEM((2, 2 * blocks), jnp.int32), pltpu.VMEM((2 * count, depth), jnp.bfloat16)],
        ),
        out_shape=(
            jax.ShapeDtypeStruct((count, width), jnp.bfloat16),
            jax.ShapeDtypeStruct((count, width), jnp.float32),
            jax.ShapeDtypeStruct((2, blocks), jnp.int32),
            jax.ShapeDtypeStruct((free * strip, 128), jnp.float32),
        ),
        cost_estimate=pl.CostEstimate(flops=4 * count * depth * width, bytes_accessed=2 * 10**7, transcendentals=0),
    )(routes, own.reshape(1), heads_out.reshape(strips, strip, depth), weight, tokens.reshape(strips, strip, width))


def finish_kernel(place_ref, route_ref, out_ref, old_ref, joined_ref, divergence_ref):
    blocks, strip = old_ref.shape[0], out_ref.shape[1]
    for block in range(blocks):
        fresh = jnp.where(route_ref[block] >= 1, 1.0, 0.0)
        for index in range(2):
            here = slice(index * strip, (index + 1) * strip)
            value = out_ref[place_ref[index, block]]
            joined_ref[block, here] = value
            gap = value.astype(jnp.float32) - old_ref[block, here].astype(jnp.float32)
            divergence_ref[block, here] = 0.5 * jnp.mean(gap * gap, axis=-1, keepdims=True) * fresh


def finished(place, routes, out, old_out, strip):
    blocks, piece, width = old_out.shape
    smem, vmem = pl.BlockSpec(memory_space=pltpu.SMEM), pl.BlockSpec(memory_space=pltpu.VMEM)
    return pl.pallas_call(
        finish_kernel,
        in_specs=[smem, smem, vmem, vmem],
        out_specs=[vmem, vmem],
        out_shape=(
            jax.ShapeDtypeStruct((blocks, piece, width), jnp.bfloat16),
            jax.ShapeDtypeStruct((blocks, piece, 1), jnp.float32),
        ),
    )(place, routes, out.reshape(-1, strip, width), old_out)


def two_experts(
    tokens, w_query, w_key, w_value, w_out, w_gate, w_up, w_down, route, old_out, cotangent
):
    own = lax.axis_index("expert")
    length, width = tokens.shape
    blocks = length // BLOCK
    piece = BLOCK // 2
    strip = piece // 2
    capacity = max(2, blocks // 2 + 1)
    certain = blocks - capacity
    free = blocks - 2 * certain
    sure, loose, rest = certain * strip, free * strip, capacity * strip
    side = blocks * strip
    routes = route[:, 0]
    outer, section = lax.axis_size("outer"), lax.axis_size("section")
    ring = []
    for line in range(outer):
        places = [line * section + place for place in range(section)]
        ring += places if line % 2 == 0 else places[::-1]
    count = len(ring)

    early = swap(w_gate[0][: w_gate.shape[1] // 2], "expert")
    heads_out = attended(tokens, w_query, w_key, w_value)
    parcel, kept, place, flag_rows = projected(routes, own, heads_out, w_out, tokens, strip, capacity)

    core = lax.axis_index("pair")
    span = width // (outer * 2)

    def part(number):
        pieces = [
            lax.dynamic_slice_in_dim(cotangent, (line * 2 + number) * span, span, axis=1) for line in range(outer)
        ]
        return jnp.concatenate(pieces, axis=1)

    left = jnp.concatenate([part(core), swap(part(1 - core), "pair")], axis=0)
    term = lax.dot_general(
        left, both(heads_out), (((0,), (0,)), ((), ())), preferred_element_type=jnp.float32
    ).astype(jnp.bfloat16)
    high, deep = width // (2 * count), term.shape[1]

    hidden_units = w_gate.shape[1]
    half = hidden_units // 2
    tiles = 4
    any_space = pl.BlockSpec(memory_space=pl.ANY)
    low = jnp.bfloat16
    dma = pltpu.SemaphoreType.DMA
    out, gradient, _, _ = pl.pallas_call(
        functools.partial(moe_kernel, sure, loose, half),
        out_shape=(
            jax.ShapeDtypeStruct((2 * side, width), low),
            jax.ShapeDtypeStruct((high, deep), jnp.float32),
            jax.ShapeDtypeStruct((3, 2, hidden_units, width), low),
            jax.ShapeDtypeStruct((2, 2, count, high // 2, deep // 2), low),
        ),
        in_specs=[any_space] * 8,
        out_specs=[any_space] * 4,
        scratch_shapes=[
            pltpu.VMEM((3, 2, hidden_units, width), low),
            pltpu.VMEM((count, 2 * side, width), low),
            pltpu.VMEM((count, 2 * sure, width), low),
            pltpu.VMEM((2, 2 * sure, width), low),
            pltpu.VMEM((2, 2 * rest, width), low),
            pltpu.VMEM((count, 2 * loose, width), low),
            pltpu.VMEM((count, tiles, 2 * rest, half), low),
            pltpu.VMEM((tiles, 2 * side, half), low),
            pltpu.VMEM((half, width), low),
            pltpu.VMEM((half, width), low),
            pltpu.VMEM((2, 2, high // 2, deep // 2), low),
            pltpu.VMEM((2, 2, high // 2, deep // 2), low),
            pltpu.VMEM((2, 2, 2, high // 2, deep // 2), low),
            pltpu.VMEM((high, deep), jnp.float32),
            pltpu.VMEM((side // (2 * loose), 2 * loose, width // 2), jnp.float32),
            pltpu.VMEM((2, count, loose, 128), jnp.float32),
            dma((2, 2, count)), dma((2, 2, count)), dma((2, count)), dma((2, count)),
            dma((2, 2, count)), dma((2, 2, count)), dma((2, 2, count)), dma((2, 2, count)),
            dma((3,)), dma((3,)), dma((3,)), dma((3,)), dma((4,)), dma((4,)),
            dma((2, 2)), dma((2, 2)), dma((2, count)), dma((2, count)),
            dma((8,)), pltpu.SemaphoreType.REGULAR((2, 2)),
        ],
        compiler_params=pltpu.CompilerParams(
            collective_id=0, has_side_effects=True, vmem_limit_bytes=67043328
        ),
        cost_estimate=pl.CostEstimate(flops=10**11, bytes_accessed=10**8, transcendentals=0),
    )(
        parcel.reshape(-1, 2 * loose, width),
        kept.reshape(-1, 2 * loose, width),
        early,
        w_gate[0],
        w_up[0],
        w_down[0],
        term,
        flag_rows,
    )

    joined, divergence = finished(place, routes, out, old_out, strip)
    divergence = divergence.reshape(blocks, piece)
    return (joined, divergence, gradient)


def solution(mesh):
    sizes = mesh.shape
    pair = 2 if sizes["dp"] % 2 == 0 else 1
    replicas_in_ring = sizes["dp"] // pair * sizes["section"]
    body = two_experts if sizes["expert"] == 2 and pair == 2 and replicas_in_ring == 8 else per_device
    split = Mesh(
        mesh.devices.reshape(sizes["dp"] // pair, pair, sizes["section"], sizes["expert"]),
        ("outer", "pair", "section", "expert"),
    )
    replicas = ("outer", "pair", "section")
    return jax.shard_map(
        body,
        mesh=split,
        in_specs=(
            P(replicas, None),
            P(None, "expert"),
            P(None, "expert"),
            P(None, "expert"),
            P("expert", None),
            P("expert", replicas, None),
            P("expert", replicas, None),
            P("expert", replicas, None),
            P(replicas, None),
            P(replicas, "expert", None),
            P(replicas, None),
        ),
        out_specs=(
            P(replicas, "expert", None),
            P(replicas, "expert"),
            P(replicas, "expert"),
        ),
        check_vma=False,
    )
```

```python
import functools
import math

import jax
import jax.numpy as jnp
from jax import lax
from jax.experimental import pallas as pl
from jax.experimental.pallas import tpu as pltpu
from jax.sharding import Mesh
from jax.sharding import PartitionSpec as P


HEAD_DIM = 128
BLOCK = 64
GROUP = ("outer", "section")


def attend_local(tokens, w_query, w_key, w_value):
    length = tokens.shape[0]
    key_heads = w_key.shape[1] // HEAD_DIM
    group = w_query.shape[1] // w_key.shape[1]
    queries = jnp.dot(tokens, w_query, preferred_element_type=jnp.float32).astype(jnp.bfloat16)
    queries = queries.reshape(length, key_heads, group, HEAD_DIM)
    keys = jnp.dot(tokens, w_key, preferred_element_type=jnp.float32).astype(jnp.bfloat16)
    keys = keys.reshape(length, key_heads, HEAD_DIM)
    values = jnp.dot(tokens, w_value, preferred_element_type=jnp.float32).astype(jnp.bfloat16)
    values = values.reshape(length, key_heads, HEAD_DIM)
    scores = jnp.einsum("qkgd,skd->kgqs", queries, keys, preferred_element_type=jnp.float32)
    scores = scores * (1.0 / math.sqrt(HEAD_DIM))
    query_pos = lax.broadcasted_iota(jnp.int32, (length, length), 0)
    key_pos = lax.broadcasted_iota(jnp.int32, (length, length), 1)
    scores = jnp.where(query_pos >= key_pos, scores, -jnp.inf)
    top = jnp.max(scores, axis=-1, keepdims=True)
    weights = jnp.exp(scores - top)
    probs = (weights / jnp.sum(weights, axis=-1, keepdims=True)).astype(jnp.bfloat16)
    mixed = jnp.einsum("kgqs,skd->qkgd", probs, values, preferred_element_type=jnp.float32)
    return mixed.astype(jnp.bfloat16).reshape(length, key_heads * group * HEAD_DIM)


def routing_table(routes, experts, capacity):
    number = routes.shape[0]
    same = routes[:, None] == routes[None, :]
    earlier = lax.broadcasted_iota(jnp.int32, (number, number), 1) < lax.broadcasted_iota(
        jnp.int32, (number, number), 0
    )
    slot = jnp.sum((same & earlier).astype(jnp.int32), axis=1)
    expert_hit = routes[None, :] == lax.broadcasted_iota(jnp.int32, (experts, number), 0)
    slot_hit = slot[None, :] == lax.broadcasted_iota(jnp.int32, (capacity, number), 0)
    return (expert_hit[:, None, :] & slot_hit[None, :, :]).astype(jnp.bfloat16)


def swap(value, axis):
    return lax.ppermute(value, axis, [(0, 1), (1, 0)])


def both(value, axis=0):
    if lax.axis_size("pair") == 1:
        return value
    return jnp.concatenate([value, swap(value, "pair")], axis=axis)


def pick(blocks, table):
    rows = jnp.einsum("cb,brd->crd", table, blocks, preferred_element_type=jnp.float32)
    return rows.astype(jnp.bfloat16)


def wo_gradient(cotangent, heads_out):
    length, width = cotangent.shape
    outer, pair = lax.axis_size("outer"), lax.axis_size("pair")
    parts = cotangent.reshape(length, outer, pair, width // (outer * pair))
    mine = lax.axis_index("pair")

    def part(number):
        return lax.dynamic_index_in_dim(parts, number, 2, keepdims=False).reshape(length, width // pair)

    left = part(mine)
    if pair == 2:
        left = jnp.concatenate([left, swap(part(1 - mine), "pair")], axis=0)
    term = lax.dot_general(
        left, both(heads_out), (((0,), (0,)), ((), ())), preferred_element_type=jnp.float32
    ).astype(jnp.bfloat16)
    return lax.psum_scatter(term, GROUP, scatter_dimension=0, tiled=True).astype(jnp.float32)


def per_device(
    tokens, w_query, w_key, w_value, w_out, w_gate, w_up, w_down, route, old_out, cotangent
):
    experts = lax.axis_size("expert")
    own = lax.axis_index("expert")
    length, width = tokens.shape
    blocks = length // BLOCK
    piece_rows = BLOCK // experts
    capacity = max(2, blocks // experts + 1)
    old_count = experts - max(1, experts // 4)
    routes = route[:, 0]
    table = routing_table(routes, experts, capacity)
    own_table = lax.dynamic_index_in_dim(table, own, 0, keepdims=False)
    token_rows = pick(tokens.reshape(blocks, BLOCK, width), own_table)

    heads_out = attend_local(tokens, w_query, w_key, w_value)
    head_blocks = heads_out.reshape(blocks, BLOCK, heads_out.shape[1])

    def project(rows):
        return jnp.dot(
            rows.reshape(-1, rows.shape[-1]), w_out, preferred_element_type=jnp.float32
        ).reshape(rows.shape[:-1] + (width,))

    if experts == 2:
        half = capacity * BLOCK // 2
        peer_table = lax.dynamic_index_in_dim(table, 1 - own, 0, keepdims=False)
        outgoing = project(pick(head_blocks, peer_table)).astype(jnp.bfloat16).reshape(-1, width)
        kept = project(pick(head_blocks, own_table)).reshape(-1, width)
        kept = kept + token_rows.reshape(-1, width).astype(jnp.float32)
        first = (kept[:half] + swap(outgoing[:half], "expert").astype(jnp.float32)).astype(jnp.bfloat16)
        second = (kept[half:] + swap(outgoing[half:], "expert").astype(jnp.float32)).astype(jnp.bfloat16)
    else:
        half = capacity * BLOCK // 2
        rows = jnp.einsum("jcb,brd->jcrd", table, head_blocks, preferred_element_type=jnp.float32)
        outgoing = project(rows.astype(jnp.bfloat16)).astype(jnp.bfloat16)
        total = lax.psum_scatter(outgoing, "expert", scatter_dimension=0, tiled=True)[0]
        total = (token_rows.astype(jnp.float32) + total.astype(jnp.float32)).astype(jnp.bfloat16)
        total = total.reshape(-1, width)
        first, second = total[:half], total[half:]

    gradient = wo_gradient(cotangent, heads_out)
    gate_rows, up_rows, down_rows = both(w_gate[0]), both(w_up[0]), both(w_down[0])
    contract = (((1,), (1,)), ((), ()))

    def expert(top, bottom):
        rows = jnp.concatenate([top, bottom], axis=0)
        gate = lax.dot_general(rows, gate_rows, contract, preferred_element_type=jnp.float32)
        lifted = lax.dot_general(rows, up_rows, contract, preferred_element_type=jnp.float32)
        active = (jax.nn.silu(gate) * lifted).astype(jnp.bfloat16)
        return jnp.dot(active, down_rows, preferred_element_type=jnp.float32)

    outer, section = lax.axis_size("outer"), lax.axis_size("section")
    ring = []
    for line in range(outer):
        places = [line * section + place for place in range(section)]
        ring += places if line % 2 == 0 else places[::-1]
    count = len(ring)
    onward = [(ring[i], ring[(i + 1) % count]) for i in range(count)]
    backward = [(target, source) for source, target in onward]
    front, back = first, second
    sums = None
    for _ in range(count - 1):
        front = lax.ppermute(front, GROUP, onward)
        back = lax.ppermute(back, GROUP, backward)
        terms = expert(front, back)
        upper, lower = terms[:half], terms[half:]
        if sums is not None:
            upper = upper + lax.ppermute(sums[0], GROUP, onward).astype(jnp.float32)
            lower = lower + lax.ppermute(sums[1], GROUP, backward).astype(jnp.float32)
        sums = (upper.astype(jnp.bfloat16), lower.astype(jnp.bfloat16))
    terms = expert(first, second)
    upper = terms[:half] + lax.ppermute(sums[0], GROUP, onward).astype(jnp.float32)
    lower = terms[half:] + lax.ppermute(sums[1], GROUP, backward).astype(jnp.float32)
    expert_sum = jnp.concatenate([upper, lower], axis=0)
    hidden = jnp.concatenate([first, second], axis=0).astype(jnp.float32)
    whole = (hidden + expert_sum.astype(jnp.bfloat16).astype(jnp.float32)).astype(jnp.bfloat16)
    whole = whole.reshape(capacity, experts, piece_rows, width)
    if experts == 2:
        mine = lax.dynamic_index_in_dim(whole, own, 1, keepdims=False)
        theirs = swap(lax.dynamic_index_in_dim(whole, 1 - own, 1, keepdims=False), "expert")
        joined = jnp.einsum("cb,crd->brd", own_table, mine, preferred_element_type=jnp.float32)
        joined = joined + jnp.einsum("cb,crd->brd", peer_table, theirs, preferred_element_type=jnp.float32)
    else:
        returned = lax.all_to_all(
            whole.transpose(1, 0, 2, 3), "expert", split_axis=0, concat_axis=0, tiled=True
        )
        joined = jnp.einsum("jcb,jcrd->brd", table, returned, preferred_element_type=jnp.float32)
    joined = joined.astype(jnp.bfloat16)
    fresh = (routes >= old_count).astype(jnp.float32)
    gap = joined.astype(jnp.float32) - old_out.astype(jnp.float32)
    divergence = 0.5 * jnp.mean(gap * gap, axis=-1) * fresh[:, None]
    return (joined, divergence, gradient)


MESH_ID = pl.DeviceIdType.MESH
NT = (((1,), (1,)), ((), ()))


def moe_kernel(
    sure, loose, half,
    parcel_ref, kept_ref, early_ref, gate_ref, up_ref, down_ref, term_ref, flag_ref,
    out_ref, grad_ref, far_ref, slot_ref,
    near_w, rows, sums, stage, stage_rest, part, far_act, act, gate_tile, up_tile, grad_in, term_in, grad_out, total_grad,
    kept_in, flags,
    row_send, row_recv, sum_send, sum_recv, grad_send, grad_recv, rest_send, rest_recv,
    pair_send, pair_recv, far_send, far_recv, fwd_send, fwd_recv, got_send, got_recv, flag_send, flag_recv,
    local_sem, free_sem,
):
    outer, section = lax.axis_size("outer"), lax.axis_size("section")
    count = outer * section
    x, z = lax.axis_index("outer"), lax.axis_index("section")
    spot = x * (count - 1) + z * (1 - 2 * x)

    def at(place):
        line = place // section
        within = place % section
        return {"outer": line, "section": within * (1 - 2 * line) + (section - 1) * line}

    onward, backward = at((spot + 1) % count), at((spot + count - 1) % count)
    partner = {"pair": 1 - lax.axis_index("pair")}
    peer = {"expert": 1 - lax.axis_index("expert")}
    ways = (onward, backward)
    total_rows, width = rows.shape[1:]
    side = total_rows // 2
    block = part.shape[1]
    layers = side // block
    rest = side - sure
    edges = (0, rest // 32 * 16, rest)
    tile = half
    tiles = near_w.shape[1] * near_w.shape[2] // tile
    per = near_w.shape[2] // tile
    chunk = 512
    weights = (gate_ref, up_ref, down_ref)

    barrier = pltpu.get_barrier_semaphore()
    for target in (onward, backward, partner, peer):
        pl.semaphore_signal(barrier, inc=1, device_id=target, device_id_type=MESH_ID)
    pl.semaphore_wait(barrier, 4)

    def remote(source, target, send, recv, device):
        return pltpu.make_async_remote_copy(
            src_ref=source, dst_ref=target, send_sem=send, recv_sem=recv, device_id=device, device_id_type=MESH_ID
        )

    def row_copy(way, piece, step):
        here = pl.ds(way * side + piece * block, block)
        return remote(
            rows.at[step - 1, here], rows.at[step, here], row_send.at[way, piece, step], row_recv.at[way, piece, step], ways[way]
        )

    def flag_copy(way, step):
        return remote(
            flags.at[way, step - 1], flags.at[way, step], flag_send.at[way, step], flag_recv.at[way, step], ways[way]
        )

    def got_copy(way, piece):
        here = way * layers + piece
        return remote(parcel_ref.at[here], part.at[here], got_send.at[way, piece], got_recv.at[way, piece], peer)

    high, deep = grad_in.shape[1], grad_in.shape[2]

    def term_at(way, index):
        place = (spot + index) % count
        line = place // section
        within = place % section
        block = line * section + within * (1 - 2 * line) + (section - 1) * line
        return term_ref.at[pl.ds(pl.multiple_of(block * high, high), high), pl.ds(way * deep, deep)]

    def grad_copy(way, step, source):
        return remote(source, slot_ref.at[way, step], grad_send.at[way, step], grad_recv.at[way, step], ways[way])

    def sum_copy(way, step):
        here = pl.ds(way * sure, sure)
        return remote(stage.at[step % 2, here], sums.at[step, here], sum_send.at[way, step], sum_recv.at[way, step], ways[way])

    def rest_copy(way, half_index, step):
        first, size = edges[half_index], edges[half_index + 1] - edges[half_index]
        here = pl.ds(way * rest + first, size)
        there = pl.ds(sure + way * rest + first, size)
        return remote(
            stage_rest.at[step % 2, here],
            rows.at[step, there],
            rest_send.at[way, half_index, step],
            rest_recv.at[way, half_index, step],
            ways[way],
        )

    late = pl.ds(tile, near_w.shape[2] - tile)
    head = pl.ds(0, tile)

    def far_copy(which):
        source, target = weights[which], far_ref.at[which, 0]
        if which == 0:
            source, target = source.at[late], target.at[late]
        return remote(source, target, far_send.at[which], far_recv.at[which], peer)

    def forward_copy(which):
        source, target = far_ref.at[which, 0], far_ref.at[which, 1]
        if which == 0:
            source, target = source.at[late], target.at[late]
        return remote(source, target, fwd_send.at[which], fwd_recv.at[which], partner)

    def early_copy():
        return remote(early_ref, far_ref.at[0, 1, head], fwd_send.at[3], fwd_recv.at[3], partner)

    def pair_copy(which):
        return remote(weights[which], near_w.at[which, 1], pair_send.at[which], pair_recv.at[which], partner)

    def local(source, target, place):
        return pltpu.make_async_copy(source, target, local_sem.at[place])

    def gradient_step(step):
        pulls = []
        for way in range(2):
            grad_copy(way, step, slot_ref.at[way, step]).wait_recv()
            pulls.append(local(slot_ref.at[way, step], grad_in.at[way], way))
            index = (2 * count - 1 - step) % count if way == 0 else (1 + step) % count
            pulls.append(local(term_at(way, index), term_in.at[way], 2 + way))
        for pull in pulls:
            pull.start()
        for pull in pulls:
            pull.wait()
        for way in range(2):
            value = grad_in[way].astype(jnp.float32) + term_in[way].astype(jnp.float32)

            step = jnp.asarray(step, jnp.int32)

            @pl.when(step < count - 1)
            def _():
                @pl.when(step >= 3)
                def _():
                    grad_copy(way, step - 1, grad_out.at[way, step % 2]).wait_send()

                grad_out[way, step % 2] = value.astype(jnp.bfloat16)
                grad_copy(way, step + 1, grad_out.at[way, step % 2]).start()

            @pl.when(step == count - 1)
            def _():
                total_grad[:, pl.ds(way * value.shape[1], value.shape[1])] = value

    for piece in range(2):
        for way in range(2):
            got_copy(way, piece).start()
    for which in range(3):
        far_copy(which).start()
    grad_copy(0, 1, term_at(0, count - 1)).start()
    grad_copy(1, 1, term_at(1, 1)).start()
    marks = [local(flag_ref, flags.at[way, 0], way) for way in range(2)]
    for mark in marks:
        mark.start()
    for mark in marks:
        mark.wait()
    for way in range(2):
        flag_copy(way, 1).start()
    loads = [local(weights[which], near_w.at[which, 0], 1 + which) for which in range(3)]
    for load in loads:
        load.start()
    for which in range(3):
        pair_copy(which).start()
    early_copy().start()
    for load in loads:
        load.wait()
    for number in range(4):
        piece, way = number // 2, number % 2
        layer = way * layers + piece
        pull = local(kept_ref.at[layer], kept_in, 0)
        pull.start()
        pull.wait()
        got_copy(way, piece).wait_recv()

        def join(index, _):
            columns = pl.ds(pl.multiple_of(index * chunk, chunk), chunk)
            value = kept_in[:, columns] + part[layer, :, columns].astype(jnp.float32)
            rows[0, way * side + piece * block : way * side + (piece + 1) * block, columns] = value.astype(jnp.bfloat16)
            return 0

        lax.fori_loop(0, width // chunk, join, 0)
        row_copy(way, piece, 1).start()
        if number < 3:
            gradient_step(number + 1)
    for which in range(3):
        pair_copy(which).wait_recv()

    def gated(value, gate, up):
        pre = lax.dot_general(value, gate, NT, preferred_element_type=jnp.float32)
        lifted = lax.dot_general(value, up, NT, preferred_element_type=jnp.float32)
        return pre * (1.0 / (1.0 + jnp.exp(-pre))) * lifted

    def near_step(step):
        slot = step

        def one(index, _):
            place = pl.ds(pl.multiple_of((index % per) * tile, tile), tile)
            value = gated(rows[slot], near_w[0, index // per, place], near_w[1, index // per, place])
            act[index] = value.astype(jnp.bfloat16)
            return 0

        lax.fori_loop(0, tiles, one, 0)

        @pl.when(step >= 2)
        def _():
            for way in range(2):
                sum_copy(way, step - 1).wait_recv()

        @pl.when(step >= 3)
        def _():
            for way in range(2):
                sum_copy(way, step - 2).wait_send()

        def two(index, _):
            columns = pl.ds(pl.multiple_of(index * chunk, chunk), chunk)
            total = None
            for number in range(tiles):
                place = pl.ds((number % per) * tile, tile)
                term = jnp.dot(
                    act[number], near_w[2, number // per, place, columns], preferred_element_type=jnp.float32
                )
                total = term if total is None else total + term
            before = sums[jnp.maximum(step - 1, 0), :, columns].astype(jnp.float32)
            before = jnp.where(step >= 2, before, 0.0)
            stage[step % 2, 0:sure, columns] = (total[0:sure] + before[0:sure]).astype(jnp.bfloat16)
            stage[step % 2, sure : 2 * sure, columns] = (total[total_rows - sure :] + before[sure:]).astype(jnp.bfloat16)
            part[slot, 0:loose, columns] = jnp.where(
                flags[0, slot][:, 0:1] > 0, total[sure : sure + loose], 0.0
            ).astype(jnp.bfloat16)
            part[slot, loose : 2 * loose, columns] = jnp.where(
                flags[1, slot][:, 0:1] > 0, total[side : side + loose], 0.0
            ).astype(jnp.bfloat16)
            return 0

        lax.fori_loop(0, width // chunk, two, 0)

    def far_step(low, high):
        def one(index, _):
            place = pl.ds(pl.multiple_of((index % per) * tile, tile), tile)
            gate_fetch = local(far_ref.at[0, index // per, place], gate_tile, 0)
            up_fetch = local(far_ref.at[1, index // per, place], up_tile, 1)

            @pl.when(index == 0)
            def _():
                fetch = local(early_ref, gate_tile, 0)
                fetch.start()
                fetch.wait()

            up_fetch.start()

            @pl.when(index > 0)
            def _():
                gate_fetch.start()
                gate_fetch.wait()

            up_fetch.wait()

            def two(step, _):
                slot = step % count
                value = gated(rows[slot, sure : sure + 2 * rest], gate_tile[...], up_tile[...])
                for way in range(2):
                    base = way * rest
                    far_act[slot, index, base : base + loose] = jnp.where(
                        flags[way, slot][:, 0:1] > 0, 0.0, value[base : base + loose]
                    ).astype(jnp.bfloat16)
                    far_act[slot, index, base + loose : base + rest] = value[base + loose : base + rest].astype(
                        jnp.bfloat16
                    )
                return 0

            lax.fori_loop(low, high, two, 0)
            return 0

        lax.fori_loop(0, tiles, one, 0)

    def ring_step(step, _):
        @pl.when(step >= 1)
        def _():
            for piece in range(2):
                for way in range(2):
                    row_copy(way, piece, step).wait_recv()

                    @pl.when(step < count - 1)
                    def _():
                        row_copy(way, piece, step + 1).start()

            for way in range(2):
                flag_copy(way, step).wait_recv()

                @pl.when(step < count - 1)
                def _():
                    flag_copy(way, step + 1).start()

        @pl.when((step >= 1) & (step < count - 3))
        def _():
            gradient_step(step + 3)

        near_step(step)

        @pl.when(step >= 1)
        def _():
            for way in range(2):
                sum_copy(way, step).start()

        @pl.when(step == 0)
        def _():
            sums[0] = stage[0]

        for which, when in ((0, count // 2 - 1), (1, count - 3), (2, count - 1)):
            @pl.when(step == when)
            def _():
                far_copy(which).wait_recv()
                forward_copy(which).start()

        @pl.when(step == count - 3)
        def _():
            early_copy().wait_recv()
            for which in range(2):
                forward_copy(which).wait_recv()

        @pl.when((step >= count - 3) & (step < count - 1))
        def _():
            low = 3 * (step - (count - 3))
            far_step(low, low + 3)

        return 0

    lax.fori_loop(0, count, ring_step, 0)

    for way in range(2):
        for step in range(1, count):
            flag_copy(way, step).wait_send()
            for piece in range(2):
                row_copy(way, piece, step).wait_send()

    def grant(turn):
        pl.semaphore_signal(free_sem.at[0, turn], inc=1, device_id=backward, device_id_type=MESH_ID)
        pl.semaphore_signal(free_sem.at[1, turn], inc=1, device_id=onward, device_id_type=MESH_ID)

    grant(0)
    pulls = [local(far_ref.at[2, 0], near_w.at[0, 0], 0), local(far_ref.at[2, 1], near_w.at[0, 1], 1)]
    pulls[0].start()
    forward_copy(2).wait_recv()
    pulls[1].start()
    for pull in pulls:
        pull.wait()

    def rest_step(step, _):
        slot = step % count

        def two(index, _):
            columns = pl.ds(pl.multiple_of(index * chunk, chunk), chunk)
            total = None
            for number in range(tiles):
                place = pl.ds((number % per) * tile, tile)
                term = jnp.dot(
                    far_act[slot, number], near_w[0, number // per, place, columns], preferred_element_type=jnp.float32
                )
                total = term if total is None else total + term
            piece = part[slot, :, columns].astype(jnp.float32)
            for way in range(2):
                base = way * rest
                near_w[1, 0, base : base + loose, columns] = (
                    total[base : base + loose] + piece[way * loose : (way + 1) * loose]
                ).astype(jnp.bfloat16)
                near_w[1, 0, base + loose : base + rest, columns] = total[base + loose : base + rest].astype(jnp.bfloat16)
            return 0

        lax.fori_loop(0, width // chunk, two, 0)

        for turn, when in ((0, 1), (1, count - 2)):
            @pl.when(step == when)
            def _():
                for way in range(2):
                    pl.semaphore_wait(free_sem.at[way, turn], 1)

        for half_index in range(2):
            for way in range(2):
                here = slice(way * rest + edges[half_index], way * rest + edges[half_index + 1])
                there = slice(sure + here.start, sure + here.stop)

                @pl.when(step >= 3)
                def _():
                    rest_copy(way, half_index, step - 2).wait_send()

                @pl.when(step >= 2)
                def _():
                    rest_copy(way, half_index, step - 1).wait_recv()
                    stage_rest[step % 2, here] = (
                        near_w[1, 0, here].astype(jnp.float32) + rows[step - 1, there].astype(jnp.float32)
                    ).astype(jnp.bfloat16)

                @pl.when(step < 2)
                def _():
                    stage_rest[step % 2, here] = near_w[1, 0, here]

                @pl.when(step < count)
                def _():
                    rest_copy(way, half_index, step).start()

        @pl.when(step == 1)
        def _():
            far_step(count - 2, count)
            grant(1)

        return 0

    lax.fori_loop(1, count + 1, rest_step, 0)
    for way in range(2):
        sum_copy(way, count - 1).wait_recv()

    def last(index, _):
        columns = pl.ds(pl.multiple_of(index * chunk, chunk), chunk)
        base = rows[0, :, columns].astype(jnp.float32)
        certain = sums[0, :, columns].astype(jnp.float32) + sums[count - 1, :, columns].astype(jnp.float32)
        certain = certain.astype(jnp.bfloat16).astype(jnp.float32)
        others = stage_rest[count % 2, :, columns].astype(jnp.float32)
        rows[0, 0:sure, columns] = (base[0:sure] + certain[0:sure]).astype(jnp.bfloat16)
        rows[0, sure : sure + 2 * rest, columns] = (base[sure : sure + 2 * rest] + others).astype(jnp.bfloat16)
        rows[0, total_rows - sure :, columns] = (base[total_rows - sure :] + certain[sure:]).astype(jnp.bfloat16)
        return 0

    lax.fori_loop(0, width // chunk, last, 0)
    pushes = [local(rows.at[0], out_ref, 0), local(total_grad, grad_ref, 1)]
    for push in pushes:
        push.start()
    for push in pushes:
        push.wait()
    for way in range(2):
        sum_copy(way, count - 2).wait_send()
        sum_copy(way, count - 1).wait_send()
        for half_index in range(2):
            rest_copy(way, half_index, count - 1).wait_send()
        grad_copy(way, 1, term_at(way, 0)).wait_send()
        for step in range(max(2, count - 2), count):
            grad_copy(way, step, grad_out.at[way, step % 2]).wait_send()
        for piece in range(2):
            got_copy(way, piece).wait_send()
    early_copy().wait_send()
    for which in range(3):
        pair_copy(which).wait_send()
        far_copy(which).wait_send()
        forward_copy(which).wait_send()


def attend_kernel(tokens_ref, query_ref, key_ref, value_ref, out_ref):
    tokens = tokens_ref[...]
    length = tokens.shape[0]
    low = jnp.bfloat16
    queries = jnp.dot(tokens, query_ref[...], preferred_element_type=jnp.float32).astype(low)
    keys = jnp.dot(tokens, key_ref[...], preferred_element_type=jnp.float32).astype(low)
    values = jnp.dot(tokens, value_ref[...], preferred_element_type=jnp.float32).astype(low)
    group = queries.shape[1] // keys.shape[1]
    step = 128 if length % 128 == 0 else length
    for head in range(queries.shape[1] // HEAD_DIM):
        across = slice(head * HEAD_DIM, (head + 1) * HEAD_DIM)
        shared = slice(head // group * HEAD_DIM, (head // group + 1) * HEAD_DIM)
        for start in range(0, length, step):
            end = start + step
            scores = lax.dot_general(
                queries[start:end, across], keys[:end, shared], NT, preferred_element_type=jnp.float32
            )
            scores = scores * (1.0 / math.sqrt(HEAD_DIM))
            query_pos = lax.broadcasted_iota(jnp.int32, scores.shape, 0) + start
            key_pos = lax.broadcasted_iota(jnp.int32, scores.shape, 1)
            scores = jnp.where(query_pos >= key_pos, scores, -jnp.inf)
            top = jnp.max(scores, axis=-1, keepdims=True)
            parts = jnp.exp(scores - top)
            probs = (parts / jnp.sum(parts, axis=-1, keepdims=True)).astype(low)
            mixed = jnp.dot(probs, values[:end, shared], preferred_element_type=jnp.float32)
            out_ref[start:end, across] = mixed.astype(low)


def attended(tokens, w_query, w_key, w_value):
    length, width = tokens.shape
    heads, keys = w_query.shape[1], w_key.shape[1]
    steps = 2 if keys // HEAD_DIM % 2 == 0 else 1
    wide, narrow = heads // steps, keys // steps
    return pl.pallas_call(
        attend_kernel,
        grid=(steps,),
        in_specs=[
            pl.BlockSpec((length, width), lambda i: (0, 0)),
            pl.BlockSpec((width, wide), lambda i: (0, i)),
            pl.BlockSpec((width, narrow), lambda i: (0, i)),
            pl.BlockSpec((width, narrow), lambda i: (0, i)),
        ],
        out_specs=pl.BlockSpec((length, wide), lambda i: (0, i)),
        out_shape=jax.ShapeDtypeStruct((length, heads), jnp.bfloat16),
        cost_estimate=pl.CostEstimate(
            flops=2 * length * width * (heads + 2 * keys), bytes_accessed=2 * width * (length + heads + 2 * keys), transcendentals=0
        ),
    )(tokens, w_query, w_key, w_value)


def project_kernel(
    capacity, route_ref, own_ref, heads_ref, weight_ref, tokens_ref, parcel_ref, kept_ref, place_ref, flag_ref, order_ref, picked
):
    strips, strip = order_ref.shape[1], heads_ref.shape[1]
    half = strips * strip
    blocks = strips // 2
    certain = blocks - capacity
    own = own_ref[0]

    @pl.when(pl.program_id(0) == 0)
    def _():
        routes = [route_ref[index] for index in range(blocks)]
        loose_before = jnp.int32(0)
        marks = [jnp.int32(0) for _ in range(blocks - 2 * certain)]
        for index in range(blocks):
            slot = jnp.int32(0)
            for other in range(index):
                slot = slot + jnp.where(routes[other] == routes[index], 1, 0)
            for which, first in ((0, 1 - own), (1, own)):
                fixed = jnp.where(routes[index] == first, slot, capacity + slot)
                place = jnp.where(slot >= certain, certain + loose_before, fixed)
                behind = blocks + (place + blocks - certain) % blocks
                strip_at = index * 4 + first * 2
                order_ref[which, place] = strip_at
                order_ref[which, behind] = strip_at + 1
                if which == 1:
                    place_ref[0, index] = place
                    place_ref[1, index] = behind
            for mark in range(len(marks)):
                mine = (slot >= certain) & (loose_before == mark) & (routes[index] == own)
                marks[mark] = marks[mark] + jnp.where(mine, 1, 0)
            loose_before = loose_before + jnp.where(slot >= certain, 1, 0)
        for mark, found in enumerate(marks):
            flag_ref[mark * strip : (mark + 1) * strip] = jnp.full((strip, 128), found.astype(jnp.float32))
        for which in range(2):
            for index in range(strips):
                start = which * half + index * strip
                picked[start : start + strip] = heads_ref[order_ref[which, index]]

    value = jnp.dot(picked[...], weight_ref[...], preferred_element_type=jnp.float32)
    parcel_ref[...] = value[:half].astype(jnp.bfloat16)
    for index in range(strips):
        here = slice(index * strip, (index + 1) * strip)
        kept_ref[here] = value[half + index * strip : half + (index + 1) * strip] + tokens_ref[
            order_ref[1, index]
        ].astype(jnp.float32)


def projected(routes, own, heads_out, weight, tokens, strip, capacity):
    depth, width = weight.shape
    blocks = routes.shape[0]
    count = 2 * blocks * strip
    strips = heads_out.shape[0] // strip
    free = blocks - 2 * (blocks - capacity)
    tile = 1024
    piece = pl.BlockSpec((count, tile), lambda i, route, own: (0, i))
    return pl.pallas_call(
        functools.partial(project_kernel, capacity),
        grid_spec=pltpu.PrefetchScalarGridSpec(
            num_scalar_prefetch=2,
            grid=(width // tile,),
            in_specs=[
                pl.BlockSpec((strips, strip, depth), lambda i, route, own: (0, 0, 0)),
                pl.BlockSpec((depth, tile), lambda i, route, own: (0, i)),
                pl.BlockSpec((strips, strip, tile), lambda i, route, own: (0, 0, i)),
            ],
            out_specs=[
                piece,
                piece,
                pl.BlockSpec((2, blocks), lambda i, route, own: (0, 0), memory_space=pltpu.SMEM),
                pl.BlockSpec((free * strip, 128), lambda i, route, own: (0, 0)),
            ],
            scratch_shapes=[pltpu.SMEM((2, 2 * blocks), jnp.int32), pltpu.VMEM((2 * count, depth), jnp.bfloat16)],
        ),
        out_shape=(
            jax.ShapeDtypeStruct((count, width), jnp.bfloat16),
            jax.ShapeDtypeStruct((count, width), jnp.float32),
            jax.ShapeDtypeStruct((2, blocks), jnp.int32),
            jax.ShapeDtypeStruct((free * strip, 128), jnp.float32),
        ),
        cost_estimate=pl.CostEstimate(flops=4 * count * depth * width, bytes_accessed=2 * 10**7, transcendentals=0),
    )(routes, own.reshape(1), heads_out.reshape(strips, strip, depth), weight, tokens.reshape(strips, strip, width))


def finish_kernel(place_ref, route_ref, out_ref, old_ref, joined_ref, divergence_ref):
    blocks, strip = old_ref.shape[0], out_ref.shape[1]
    for block in range(blocks):
        fresh = jnp.where(route_ref[block] >= 1, 1.0, 0.0)
        for index in range(2):
            here = slice(index * strip, (index + 1) * strip)
            value = out_ref[place_ref[index, block]]
            joined_ref[block, here] = value
            gap = value.astype(jnp.float32) - old_ref[block, here].astype(jnp.float32)
            divergence_ref[block, here] = 0.5 * jnp.mean(gap * gap, axis=-1, keepdims=True) * fresh


def finished(place, routes, out, old_out, strip):
    blocks, piece, width = old_out.shape
    smem, vmem = pl.BlockSpec(memory_space=pltpu.SMEM), pl.BlockSpec(memory_space=pltpu.VMEM)
    return pl.pallas_call(
        finish_kernel,
        in_specs=[smem, smem, vmem, vmem],
        out_specs=[vmem, vmem],
        out_shape=(
            jax.ShapeDtypeStruct((blocks, piece, width), jnp.bfloat16),
            jax.ShapeDtypeStruct((blocks, piece, 1), jnp.float32),
        ),
    )(place, routes, out.reshape(-1, strip, width), old_out)


def two_experts(
    tokens, w_query, w_key, w_value, w_out, w_gate, w_up, w_down, route, old_out, cotangent
):
    own = lax.axis_index("expert")
    length, width = tokens.shape
    blocks = length // BLOCK
    piece = BLOCK // 2
    strip = piece // 2
    capacity = max(2, blocks // 2 + 1)
    certain = blocks - capacity
    free = blocks - 2 * certain
    sure, loose, rest = certain * strip, free * strip, capacity * strip
    side = blocks * strip
    routes = route[:, 0]
    outer, section = lax.axis_size("outer"), lax.axis_size("section")
    ring = []
    for line in range(outer):
        places = [line * section + place for place in range(section)]
        ring += places if line % 2 == 0 else places[::-1]
    count = len(ring)

    early = swap(w_gate[0][: w_gate.shape[1] // 2], "expert")
    heads_out = attended(tokens, w_query, w_key, w_value)
    parcel, kept, place, flag_rows = projected(routes, own, heads_out, w_out, tokens, strip, capacity)

    core = lax.axis_index("pair")
    span = width // (outer * 2)

    def part(number):
        pieces = [
            lax.dynamic_slice_in_dim(cotangent, (line * 2 + number) * span, span, axis=1) for line in range(outer)
        ]
        return jnp.concatenate(pieces, axis=1)

    left = jnp.concatenate([part(core), swap(part(1 - core), "pair")], axis=0)
    term = lax.dot_general(
        left, both(heads_out), (((0,), (0,)), ((), ())), preferred_element_type=jnp.float32
    ).astype(jnp.bfloat16)
    high, deep = width // (2 * count), term.shape[1]

    hidden_units = w_gate.shape[1]
    half = hidden_units // 2
    tiles = 4
    any_space = pl.BlockSpec(memory_space=pl.ANY)
    low = jnp.bfloat16
    dma = pltpu.SemaphoreType.DMA
    out, gradient, _, _ = pl.pallas_call(
        functools.partial(moe_kernel, sure, loose, half),
        out_shape=(
            jax.ShapeDtypeStruct((2 * side, width), low),
            jax.ShapeDtypeStruct((high, deep), jnp.float32),
            jax.ShapeDtypeStruct((3, 2, hidden_units, width), low),
            jax.ShapeDtypeStruct((2, count, high, deep // 2), low),
        ),
        in_specs=[any_space] * 8,
        out_specs=[any_space] * 4,
        scratch_shapes=[
            pltpu.VMEM((3, 2, hidden_units, width), low),
            pltpu.VMEM((count, 2 * side, width), low),
            pltpu.VMEM((count, 2 * sure, width), low),
            pltpu.VMEM((2, 2 * sure, width), low),
            pltpu.VMEM((2, 2 * rest, width), low),
            pltpu.VMEM((count, 2 * loose, width), low),
            pltpu.VMEM((count, tiles, 2 * rest, half), low),
            pltpu.VMEM((tiles, 2 * side, half), low),
            pltpu.VMEM((half, width), low),
            pltpu.VMEM((half, width), low),
            pltpu.VMEM((2, high, deep // 2), low),
            pltpu.VMEM((2, high, deep // 2), low),
            pltpu.VMEM((2, 2, high, deep // 2), low),
            pltpu.VMEM((high, deep), jnp.float32),
            pltpu.VMEM((2 * loose, width), jnp.float32),
            pltpu.VMEM((2, count, loose, 128), jnp.float32),
            dma((2, 2, count)), dma((2, 2, count)), dma((2, count)), dma((2, count)),
            dma((2, count)), dma((2, count)), dma((2, 2, count)), dma((2, 2, count)),
            dma((3,)), dma((3,)), dma((3,)), dma((3,)), dma((4,)), dma((4,)),
            dma((2, 2)), dma((2, 2)), dma((2, count)), dma((2, count)),
            dma((4,)), pltpu.SemaphoreType.REGULAR((2, 2)),
        ],
        compiler_params=pltpu.CompilerParams(
            collective_id=0, has_side_effects=True, vmem_limit_bytes=67043328
        ),
        cost_estimate=pl.CostEstimate(flops=10**11, bytes_accessed=10**8, transcendentals=0),
    )(
        parcel.reshape(-1, 2 * loose, width),
        kept.reshape(-1, 2 * loose, width),
        early,
        w_gate[0],
        w_up[0],
        w_down[0],
        term,
        flag_rows,
    )

    joined, divergence = finished(place, routes, out, old_out, strip)
    divergence = divergence.reshape(blocks, piece)
    return (joined, divergence, gradient)


def solution(mesh):
    sizes = mesh.shape
    pair = 2 if sizes["dp"] % 2 == 0 else 1
    replicas_in_ring = sizes["dp"] // pair * sizes["section"]
    body = two_experts if sizes["expert"] == 2 and pair == 2 and replicas_in_ring == 8 else per_device
    split = Mesh(
        mesh.devices.reshape(sizes["dp"] // pair, pair, sizes["section"], sizes["expert"]),
        ("outer", "pair", "section", "expert"),
    )
    replicas = ("outer", "pair", "section")
    return jax.shard_map(
        body,
        mesh=split,
        in_specs=(
            P(replicas, None),
            P(None, "expert"),
            P(None, "expert"),
            P(None, "expert"),
            P("expert", None),
            P("expert", replicas, None),
            P("expert", replicas, None),
            P("expert", replicas, None),
            P(replicas, None),
            P(replicas, "expert", None),
            P(replicas, None),
        ),
        out_specs=(
            P(replicas, "expert", None),
            P(replicas, "expert"),
            P(replicas, "expert"),
        ),
        check_vma=False,
    )
```

```python
import functools
import math

import jax
import jax.numpy as jnp
from jax import lax
from jax.experimental import pallas as pl
from jax.experimental.pallas import tpu as pltpu
from jax.sharding import Mesh
from jax.sharding import PartitionSpec as P


HEAD_DIM = 128
BLOCK = 64
GROUP = ("outer", "section")


def attend_local(tokens, w_query, w_key, w_value):
    length = tokens.shape[0]
    key_heads = w_key.shape[1] // HEAD_DIM
    group = w_query.shape[1] // w_key.shape[1]
    queries = jnp.dot(tokens, w_query, preferred_element_type=jnp.float32).astype(jnp.bfloat16)
    queries = queries.reshape(length, key_heads, group, HEAD_DIM)
    keys = jnp.dot(tokens, w_key, preferred_element_type=jnp.float32).astype(jnp.bfloat16)
    keys = keys.reshape(length, key_heads, HEAD_DIM)
    values = jnp.dot(tokens, w_value, preferred_element_type=jnp.float32).astype(jnp.bfloat16)
    values = values.reshape(length, key_heads, HEAD_DIM)
    scores = jnp.einsum("qkgd,skd->kgqs", queries, keys, preferred_element_type=jnp.float32)
    scores = scores * (1.0 / math.sqrt(HEAD_DIM))
    query_pos = lax.broadcasted_iota(jnp.int32, (length, length), 0)
    key_pos = lax.broadcasted_iota(jnp.int32, (length, length), 1)
    scores = jnp.where(query_pos >= key_pos, scores, -jnp.inf)
    top = jnp.max(scores, axis=-1, keepdims=True)
    weights = jnp.exp(scores - top)
    probs = (weights / jnp.sum(weights, axis=-1, keepdims=True)).astype(jnp.bfloat16)
    mixed = jnp.einsum("kgqs,skd->qkgd", probs, values, preferred_element_type=jnp.float32)
    return mixed.astype(jnp.bfloat16).reshape(length, key_heads * group * HEAD_DIM)


def routing_table(routes, experts, capacity):
    number = routes.shape[0]
    same = routes[:, None] == routes[None, :]
    earlier = lax.broadcasted_iota(jnp.int32, (number, number), 1) < lax.broadcasted_iota(
        jnp.int32, (number, number), 0
    )
    slot = jnp.sum((same & earlier).astype(jnp.int32), axis=1)
    expert_hit = routes[None, :] == lax.broadcasted_iota(jnp.int32, (experts, number), 0)
    slot_hit = slot[None, :] == lax.broadcasted_iota(jnp.int32, (capacity, number), 0)
    return (expert_hit[:, None, :] & slot_hit[None, :, :]).astype(jnp.bfloat16)


def swap(value, axis):
    return lax.ppermute(value, axis, [(0, 1), (1, 0)])


def both(value, axis=0):
    if lax.axis_size("pair") == 1:
        return value
    return jnp.concatenate([value, swap(value, "pair")], axis=axis)


def pick(blocks, table):
    rows = jnp.einsum("cb,brd->crd", table, blocks, preferred_element_type=jnp.float32)
    return rows.astype(jnp.bfloat16)


def wo_gradient(cotangent, heads_out):
    length, width = cotangent.shape
    outer, pair = lax.axis_size("outer"), lax.axis_size("pair")
    parts = cotangent.reshape(length, outer, pair, width // (outer * pair))
    mine = lax.axis_index("pair")

    def part(number):
        return lax.dynamic_index_in_dim(parts, number, 2, keepdims=False).reshape(length, width // pair)

    left = part(mine)
    if pair == 2:
        left = jnp.concatenate([left, swap(part(1 - mine), "pair")], axis=0)
    term = lax.dot_general(
        left, both(heads_out), (((0,), (0,)), ((), ())), preferred_element_type=jnp.float32
    ).astype(jnp.bfloat16)
    return lax.psum_scatter(term, GROUP, scatter_dimension=0, tiled=True).astype(jnp.float32)


def per_device(
    tokens, w_query, w_key, w_value, w_out, w_gate, w_up, w_down, route, old_out, cotangent
):
    experts = lax.axis_size("expert")
    own = lax.axis_index("expert")
    length, width = tokens.shape
    blocks = length // BLOCK
    piece_rows = BLOCK // experts
    capacity = max(2, blocks // experts + 1)
    old_count = experts - max(1, experts // 4)
    routes = route[:, 0]
    table = routing_table(routes, experts, capacity)
    own_table = lax.dynamic_index_in_dim(table, own, 0, keepdims=False)
    token_rows = pick(tokens.reshape(blocks, BLOCK, width), own_table)

    heads_out = attend_local(tokens, w_query, w_key, w_value)
    head_blocks = heads_out.reshape(blocks, BLOCK, heads_out.shape[1])

    def project(rows):
        return jnp.dot(
            rows.reshape(-1, rows.shape[-1]), w_out, preferred_element_type=jnp.float32
        ).reshape(rows.shape[:-1] + (width,))

    if experts == 2:
        half = capacity * BLOCK // 2
        peer_table = lax.dynamic_index_in_dim(table, 1 - own, 0, keepdims=False)
        outgoing = project(pick(head_blocks, peer_table)).astype(jnp.bfloat16).reshape(-1, width)
        kept = project(pick(head_blocks, own_table)).reshape(-1, width)
        kept = kept + token_rows.reshape(-1, width).astype(jnp.float32)
        first = (kept[:half] + swap(outgoing[:half], "expert").astype(jnp.float32)).astype(jnp.bfloat16)
        second = (kept[half:] + swap(outgoing[half:], "expert").astype(jnp.float32)).astype(jnp.bfloat16)
    else:
        half = capacity * BLOCK // 2
        rows = jnp.einsum("jcb,brd->jcrd", table, head_blocks, preferred_element_type=jnp.float32)
        outgoing = project(rows.astype(jnp.bfloat16)).astype(jnp.bfloat16)
        total = lax.psum_scatter(outgoing, "expert", scatter_dimension=0, tiled=True)[0]
        total = (token_rows.astype(jnp.float32) + total.astype(jnp.float32)).astype(jnp.bfloat16)
        total = total.reshape(-1, width)
        first, second = total[:half], total[half:]

    gradient = wo_gradient(cotangent, heads_out)
    gate_rows, up_rows, down_rows = both(w_gate[0]), both(w_up[0]), both(w_down[0])
    contract = (((1,), (1,)), ((), ()))

    def expert(top, bottom):
        rows = jnp.concatenate([top, bottom], axis=0)
        gate = lax.dot_general(rows, gate_rows, contract, preferred_element_type=jnp.float32)
        lifted = lax.dot_general(rows, up_rows, contract, preferred_element_type=jnp.float32)
        active = (jax.nn.silu(gate) * lifted).astype(jnp.bfloat16)
        return jnp.dot(active, down_rows, preferred_element_type=jnp.float32)

    outer, section = lax.axis_size("outer"), lax.axis_size("section")
    ring = []
    for line in range(outer):
        places = [line * section + place for place in range(section)]
        ring += places if line % 2 == 0 else places[::-1]
    count = len(ring)
    onward = [(ring[i], ring[(i + 1) % count]) for i in range(count)]
    backward = [(target, source) for source, target in onward]
    front, back = first, second
    sums = None
    for _ in range(count - 1):
        front = lax.ppermute(front, GROUP, onward)
        back = lax.ppermute(back, GROUP, backward)
        terms = expert(front, back)
        upper, lower = terms[:half], terms[half:]
        if sums is not None:
            upper = upper + lax.ppermute(sums[0], GROUP, onward).astype(jnp.float32)
            lower = lower + lax.ppermute(sums[1], GROUP, backward).astype(jnp.float32)
        sums = (upper.astype(jnp.bfloat16), lower.astype(jnp.bfloat16))
    terms = expert(first, second)
    upper = terms[:half] + lax.ppermute(sums[0], GROUP, onward).astype(jnp.float32)
    lower = terms[half:] + lax.ppermute(sums[1], GROUP, backward).astype(jnp.float32)
    expert_sum = jnp.concatenate([upper, lower], axis=0)
    hidden = jnp.concatenate([first, second], axis=0).astype(jnp.float32)
    whole = (hidden + expert_sum.astype(jnp.bfloat16).astype(jnp.float32)).astype(jnp.bfloat16)
    whole = whole.reshape(capacity, experts, piece_rows, width)
    if experts == 2:
        mine = lax.dynamic_index_in_dim(whole, own, 1, keepdims=False)
        theirs = swap(lax.dynamic_index_in_dim(whole, 1 - own, 1, keepdims=False), "expert")
        joined = jnp.einsum("cb,crd->brd", own_table, mine, preferred_element_type=jnp.float32)
        joined = joined + jnp.einsum("cb,crd->brd", peer_table, theirs, preferred_element_type=jnp.float32)
    else:
        returned = lax.all_to_all(
            whole.transpose(1, 0, 2, 3), "expert", split_axis=0, concat_axis=0, tiled=True
        )
        joined = jnp.einsum("jcb,jcrd->brd", table, returned, preferred_element_type=jnp.float32)
    joined = joined.astype(jnp.bfloat16)
    fresh = (routes >= old_count).astype(jnp.float32)
    gap = joined.astype(jnp.float32) - old_out.astype(jnp.float32)
    divergence = 0.5 * jnp.mean(gap * gap, axis=-1) * fresh[:, None]
    return (joined, divergence, gradient)


MESH_ID = pl.DeviceIdType.MESH
NT = (((1,), (1,)), ((), ()))


def moe_kernel(
    sure, loose, half,
    parcel_ref, kept_ref, early_ref, gate_ref, up_ref, down_ref, term_ref, flag_ref,
    out_ref, grad_ref, far_ref, slot_ref,
    near_w, rows, sums, stage, stage_rest, part, far_act, act, gate_tile, up_tile, grad_in, term_in, grad_out, total_grad,
    kept_in, flags,
    row_send, row_recv, sum_send, sum_recv, grad_send, grad_recv, rest_send, rest_recv,
    pair_send, pair_recv, far_send, far_recv, fwd_send, fwd_recv, got_send, got_recv, flag_send, flag_recv,
    local_sem, free_sem,
):
    outer, section = lax.axis_size("outer"), lax.axis_size("section")
    count = outer * section
    x, z = lax.axis_index("outer"), lax.axis_index("section")
    spot = x * (count - 1) + z * (1 - 2 * x)

    def at(place):
        line = place // section
        within = place % section
        return {"outer": line, "section": within * (1 - 2 * line) + (section - 1) * line}

    onward, backward = at((spot + 1) % count), at((spot + count - 1) % count)
    partner = {"pair": 1 - lax.axis_index("pair")}
    peer = {"expert": 1 - lax.axis_index("expert")}
    ways = (onward, backward)
    total_rows, width = rows.shape[1:]
    side = total_rows // 2
    block = part.shape[1]
    layers = side // block
    rest = side - sure
    edges = (0, rest // 32 * 16, rest)
    tile = half
    tiles = near_w.shape[1] * near_w.shape[2] // tile
    per = near_w.shape[2] // tile
    chunk = 512
    weights = (gate_ref, up_ref, down_ref)

    barrier = pltpu.get_barrier_semaphore()
    for target in (onward, backward, partner, peer):
        pl.semaphore_signal(barrier, inc=1, device_id=target, device_id_type=MESH_ID)
    pl.semaphore_wait(barrier, 4)

    def remote(source, target, send, recv, device):
        return pltpu.make_async_remote_copy(
            src_ref=source, dst_ref=target, send_sem=send, recv_sem=recv, device_id=device, device_id_type=MESH_ID
        )

    def row_copy(way, piece, step):
        here = pl.ds(way * side + piece * block, block)
        return remote(
            rows.at[step - 1, here], rows.at[step, here], row_send.at[way, piece, step], row_recv.at[way, piece, step], ways[way]
        )

    def flag_copy(way, step):
        return remote(
            flags.at[way, step - 1], flags.at[way, step], flag_send.at[way, step], flag_recv.at[way, step], ways[way]
        )

    def got_copy(way, piece):
        here = way * layers + piece
        return remote(parcel_ref.at[here], part.at[here], got_send.at[way, piece], got_recv.at[way, piece], peer)

    high, deep = grad_in.shape[1], grad_in.shape[2]

    def term_at(way, index):
        place = (spot + index) % count
        line = place // section
        within = place % section
        block = line * section + within * (1 - 2 * line) + (section - 1) * line
        return term_ref.at[pl.ds(pl.multiple_of(block * high, high), high), pl.ds(way * deep, deep)]

    def grad_copy(way, step, source):
        return remote(source, slot_ref.at[way, step], grad_send.at[way, step], grad_recv.at[way, step], ways[way])

    def sum_copy(way, step):
        here = pl.ds(way * sure, sure)
        return remote(stage.at[step % 2, here], sums.at[step, here], sum_send.at[way, step], sum_recv.at[way, step], ways[way])

    def rest_copy(way, half_index, step):
        first, size = edges[half_index], edges[half_index + 1] - edges[half_index]
        here = pl.ds(way * rest + first, size)
        there = pl.ds(sure + way * rest + first, size)
        return remote(
            stage_rest.at[step % 2, here],
            rows.at[step, there],
            rest_send.at[way, half_index, step],
            rest_recv.at[way, half_index, step],
            ways[way],
        )

    late = pl.ds(tile, near_w.shape[2] - tile)
    head = pl.ds(0, tile)

    def far_copy(which):
        source, target = weights[which], far_ref.at[which, 0]
        if which == 0:
            source, target = source.at[late], target.at[late]
        return remote(source, target, far_send.at[which], far_recv.at[which], peer)

    def forward_copy(which):
        source, target = far_ref.at[which, 0], far_ref.at[which, 1]
        if which == 0:
            source, target = source.at[late], target.at[late]
        return remote(source, target, fwd_send.at[which], fwd_recv.at[which], partner)

    def early_copy():
        return remote(early_ref, far_ref.at[0, 1, head], fwd_send.at[3], fwd_recv.at[3], partner)

    def pair_copy(which):
        return remote(weights[which], near_w.at[which, 1], pair_send.at[which], pair_recv.at[which], partner)

    def local(source, target, place):
        return pltpu.make_async_copy(source, target, local_sem.at[place])

    def gradient_step(step):
        pulls = []
        for way in range(2):
            grad_copy(way, step, slot_ref.at[way, step]).wait_recv()
            pulls.append(local(slot_ref.at[way, step], grad_in.at[way], way))
            index = (2 * count - 1 - step) % count if way == 0 else (1 + step) % count
            pulls.append(local(term_at(way, index), term_in.at[way], 2 + way))
        for pull in pulls:
            pull.start()
        for pull in pulls:
            pull.wait()
        for way in range(2):
            value = grad_in[way].astype(jnp.float32) + term_in[way].astype(jnp.float32)

            step = jnp.asarray(step, jnp.int32)

            @pl.when(step < count - 1)
            def _():
                @pl.when(step >= 3)
                def _():
                    grad_copy(way, step - 1, grad_out.at[way, step % 2]).wait_send()

                grad_out[way, step % 2] = value.astype(jnp.bfloat16)
                grad_copy(way, step + 1, grad_out.at[way, step % 2]).start()

            @pl.when(step == count - 1)
            def _():
                total_grad[:, pl.ds(way * value.shape[1], value.shape[1])] = value

    for piece in range(2):
        for way in range(2):
            got_copy(way, piece).start()
    for which in range(3):
        far_copy(which).start()
    grad_copy(0, 1, term_at(0, count - 1)).start()
    grad_copy(1, 1, term_at(1, 1)).start()
    marks = [local(flag_ref, flags.at[way, 0], way) for way in range(2)]
    for mark in marks:
        mark.start()
    for mark in marks:
        mark.wait()
    for way in range(2):
        flag_copy(way, 1).start()
    loads = [local(weights[which], near_w.at[which, 0], 1 + which) for which in range(3)]
    for load in loads:
        load.start()
    for which in range(3):
        pair_copy(which).start()
    early_copy().start()
    for load in loads:
        load.wait()

    def pass_on(way, piece):
        row_copy(way, piece, 1).wait_recv()
        row_copy(way, piece, 2).start()

    for number in range(4):
        piece, way = number // 2, number % 2
        layer = way * layers + piece
        pull = local(kept_ref.at[layer], kept_in, 0)
        pull.start()
        pull.wait()
        got_copy(way, piece).wait_recv()

        def join(index, _):
            columns = pl.ds(pl.multiple_of(index * chunk, chunk), chunk)
            value = kept_in[:, columns] + part[layer, :, columns].astype(jnp.float32)
            rows[0, way * side + piece * block : way * side + (piece + 1) * block, columns] = value.astype(jnp.bfloat16)
            return 0

        lax.fori_loop(0, width // chunk, join, 0)
        row_copy(way, piece, 1).start()
        if number > 0:
            pass_on((number - 1) % 2, (number - 1) // 2)
        if number < 3:
            gradient_step(number + 1)
    pass_on(1, 1)
    for which in range(3):
        pair_copy(which).wait_recv()

    def gated(value, gate, up):
        pre = lax.dot_general(value, gate, NT, preferred_element_type=jnp.float32)
        lifted = lax.dot_general(value, up, NT, preferred_element_type=jnp.float32)
        return pre * (1.0 / (1.0 + jnp.exp(-pre))) * lifted

    def near_step(step):
        slot = step

        def one(index, _):
            place = pl.ds(pl.multiple_of((index % per) * tile, tile), tile)
            value = gated(rows[slot], near_w[0, index // per, place], near_w[1, index // per, place])
            act[index] = value.astype(jnp.bfloat16)
            return 0

        lax.fori_loop(0, tiles, one, 0)

        @pl.when(step >= 2)
        def _():
            for way in range(2):
                sum_copy(way, step - 1).wait_recv()

        @pl.when(step >= 3)
        def _():
            for way in range(2):
                sum_copy(way, step - 2).wait_send()

        def two(index, _):
            columns = pl.ds(pl.multiple_of(index * chunk, chunk), chunk)
            total = None
            for number in range(tiles):
                place = pl.ds((number % per) * tile, tile)
                term = jnp.dot(
                    act[number], near_w[2, number // per, place, columns], preferred_element_type=jnp.float32
                )
                total = term if total is None else total + term
            before = sums[jnp.maximum(step - 1, 0), :, columns].astype(jnp.float32)
            before = jnp.where(step >= 2, before, 0.0)
            stage[step % 2, 0:sure, columns] = (total[0:sure] + before[0:sure]).astype(jnp.bfloat16)
            stage[step % 2, sure : 2 * sure, columns] = (total[total_rows - sure :] + before[sure:]).astype(jnp.bfloat16)
            part[slot, 0:loose, columns] = jnp.where(
                flags[0, slot][:, 0:1] > 0, total[sure : sure + loose], 0.0
            ).astype(jnp.bfloat16)
            part[slot, loose : 2 * loose, columns] = jnp.where(
                flags[1, slot][:, 0:1] > 0, total[side : side + loose], 0.0
            ).astype(jnp.bfloat16)
            return 0

        lax.fori_loop(0, width // chunk, two, 0)

    def far_step(low, high):
        def one(index, _):
            place = pl.ds(pl.multiple_of((index % per) * tile, tile), tile)
            gate_fetch = local(far_ref.at[0, index // per, place], gate_tile, 0)
            up_fetch = local(far_ref.at[1, index // per, place], up_tile, 1)

            @pl.when(index == 0)
            def _():
                fetch = local(early_ref, gate_tile, 0)
                fetch.start()
                fetch.wait()

            up_fetch.start()

            @pl.when(index > 0)
            def _():
                gate_fetch.start()
                gate_fetch.wait()

            up_fetch.wait()

            def two(step, _):
                slot = step % count
                value = gated(rows[slot, sure : sure + 2 * rest], gate_tile[...], up_tile[...])
                for way in range(2):
                    base = way * rest
                    far_act[slot, index, base : base + loose] = jnp.where(
                        flags[way, slot][:, 0:1] > 0, 0.0, value[base : base + loose]
                    ).astype(jnp.bfloat16)
                    far_act[slot, index, base + loose : base + rest] = value[base + loose : base + rest].astype(
                        jnp.bfloat16
                    )
                return 0

            lax.fori_loop(low, high, two, 0)
            return 0

        lax.fori_loop(0, tiles, one, 0)

    def ring_step(step, _):
        @pl.when(step >= 2)
        def _():
            for piece in range(2):
                for way in range(2):
                    row_copy(way, piece, step).wait_recv()

                    @pl.when(step < count - 1)
                    def _():
                        row_copy(way, piece, step + 1).start()

        @pl.when(step >= 1)
        def _():
            for way in range(2):
                flag_copy(way, step).wait_recv()

                @pl.when(step < count - 1)
                def _():
                    flag_copy(way, step + 1).start()

        @pl.when((step >= 1) & (step < count - 3))
        def _():
            gradient_step(step + 3)

        near_step(step)

        @pl.when(step >= 1)
        def _():
            for way in range(2):
                sum_copy(way, step).start()

        @pl.when(step == 0)
        def _():
            sums[0] = stage[0]

        for which, when in ((0, count // 2 - 1), (1, count - 3), (2, count - 1)):
            @pl.when(step == when)
            def _():
                far_copy(which).wait_recv()
                forward_copy(which).start()

        @pl.when(step == count - 3)
        def _():
            early_copy().wait_recv()
            for which in range(2):
                forward_copy(which).wait_recv()

        @pl.when((step >= count - 3) & (step < count - 1))
        def _():
            low = 3 * (step - (count - 3))
            far_step(low, low + 3)

        return 0

    lax.fori_loop(0, count, ring_step, 0)

    for way in range(2):
        for step in range(1, count):
            flag_copy(way, step).wait_send()
            for piece in range(2):
                row_copy(way, piece, step).wait_send()

    def grant(turn):
        pl.semaphore_signal(free_sem.at[0, turn], inc=1, device_id=backward, device_id_type=MESH_ID)
        pl.semaphore_signal(free_sem.at[1, turn], inc=1, device_id=onward, device_id_type=MESH_ID)

    grant(0)
    pulls = [local(far_ref.at[2, 0], near_w.at[0, 0], 0), local(far_ref.at[2, 1], near_w.at[0, 1], 1)]
    pulls[0].start()
    forward_copy(2).wait_recv()
    pulls[1].start()
    for pull in pulls:
        pull.wait()

    def rest_step(step, _):
        slot = step % count

        def two(index, _):
            columns = pl.ds(pl.multiple_of(index * chunk, chunk), chunk)
            total = None
            for number in range(tiles):
                place = pl.ds((number % per) * tile, tile)
                term = jnp.dot(
                    far_act[slot, number], near_w[0, number // per, place, columns], preferred_element_type=jnp.float32
                )
                total = term if total is None else total + term
            piece = part[slot, :, columns].astype(jnp.float32)
            for way in range(2):
                base = way * rest
                near_w[1, 0, base : base + loose, columns] = (
                    total[base : base + loose] + piece[way * loose : (way + 1) * loose]
                ).astype(jnp.bfloat16)
                near_w[1, 0, base + loose : base + rest, columns] = total[base + loose : base + rest].astype(jnp.bfloat16)
            return 0

        lax.fori_loop(0, width // chunk, two, 0)

        for turn, when in ((0, 1), (1, count - 2)):
            @pl.when(step == when)
            def _():
                for way in range(2):
                    pl.semaphore_wait(free_sem.at[way, turn], 1)

        for half_index in range(2):
            for way in range(2):
                here = slice(way * rest + edges[half_index], way * rest + edges[half_index + 1])
                there = slice(sure + here.start, sure + here.stop)

                @pl.when(step >= 3)
                def _():
                    rest_copy(way, half_index, step - 2).wait_send()

                @pl.when(step >= 2)
                def _():
                    rest_copy(way, half_index, step - 1).wait_recv()
                    stage_rest[step % 2, here] = (
                        near_w[1, 0, here].astype(jnp.float32) + rows[step - 1, there].astype(jnp.float32)
                    ).astype(jnp.bfloat16)

                @pl.when(step < 2)
                def _():
                    stage_rest[step % 2, here] = near_w[1, 0, here]

                @pl.when(step < count)
                def _():
                    rest_copy(way, half_index, step).start()

        @pl.when(step == 1)
        def _():
            far_step(count - 2, count)
            grant(1)

        return 0

    lax.fori_loop(1, count + 1, rest_step, 0)
    for way in range(2):
        sum_copy(way, count - 1).wait_recv()

    def last(index, _):
        columns = pl.ds(pl.multiple_of(index * chunk, chunk), chunk)
        base = rows[0, :, columns].astype(jnp.float32)
        certain = sums[0, :, columns].astype(jnp.float32) + sums[count - 1, :, columns].astype(jnp.float32)
        certain = certain.astype(jnp.bfloat16).astype(jnp.float32)
        others = stage_rest[count % 2, :, columns].astype(jnp.float32)
        rows[0, 0:sure, columns] = (base[0:sure] + certain[0:sure]).astype(jnp.bfloat16)
        rows[0, sure : sure + 2 * rest, columns] = (base[sure : sure + 2 * rest] + others).astype(jnp.bfloat16)
        rows[0, total_rows - sure :, columns] = (base[total_rows - sure :] + certain[sure:]).astype(jnp.bfloat16)
        return 0

    lax.fori_loop(0, width // chunk, last, 0)
    pushes = [local(rows.at[0], out_ref, 0), local(total_grad, grad_ref, 1)]
    for push in pushes:
        push.start()
    for push in pushes:
        push.wait()
    for way in range(2):
        sum_copy(way, count - 2).wait_send()
        sum_copy(way, count - 1).wait_send()
        for half_index in range(2):
            rest_copy(way, half_index, count - 1).wait_send()
        grad_copy(way, 1, term_at(way, 0)).wait_send()
        for step in range(max(2, count - 2), count):
            grad_copy(way, step, grad_out.at[way, step % 2]).wait_send()
        for piece in range(2):
            got_copy(way, piece).wait_send()
    early_copy().wait_send()
    for which in range(3):
        pair_copy(which).wait_send()
        far_copy(which).wait_send()
        forward_copy(which).wait_send()


def attend_kernel(tokens_ref, query_ref, key_ref, value_ref, out_ref):
    tokens = tokens_ref[...]
    length = tokens.shape[0]
    low = jnp.bfloat16
    queries = jnp.dot(tokens, query_ref[...], preferred_element_type=jnp.float32).astype(low)
    keys = jnp.dot(tokens, key_ref[...], preferred_element_type=jnp.float32).astype(low)
    values = jnp.dot(tokens, value_ref[...], preferred_element_type=jnp.float32).astype(low)
    group = queries.shape[1] // keys.shape[1]
    step = 128 if length % 128 == 0 else length
    for head in range(queries.shape[1] // HEAD_DIM):
        across = slice(head * HEAD_DIM, (head + 1) * HEAD_DIM)
        shared = slice(head // group * HEAD_DIM, (head // group + 1) * HEAD_DIM)
        for start in range(0, length, step):
            end = start + step
            scores = lax.dot_general(
                queries[start:end, across], keys[:end, shared], NT, preferred_element_type=jnp.float32
            )
            scores = scores * (1.0 / math.sqrt(HEAD_DIM))
            query_pos = lax.broadcasted_iota(jnp.int32, scores.shape, 0) + start
            key_pos = lax.broadcasted_iota(jnp.int32, scores.shape, 1)
            scores = jnp.where(query_pos >= key_pos, scores, -jnp.inf)
            top = jnp.max(scores, axis=-1, keepdims=True)
            parts = jnp.exp(scores - top)
            probs = (parts / jnp.sum(parts, axis=-1, keepdims=True)).astype(low)
            mixed = jnp.dot(probs, values[:end, shared], preferred_element_type=jnp.float32)
            out_ref[start:end, across] = mixed.astype(low)


def attended(tokens, w_query, w_key, w_value):
    length, width = tokens.shape
    heads, keys = w_query.shape[1], w_key.shape[1]
    steps = 2 if keys // HEAD_DIM % 2 == 0 else 1
    wide, narrow = heads // steps, keys // steps
    return pl.pallas_call(
        attend_kernel,
        grid=(steps,),
        in_specs=[
            pl.BlockSpec((length, width), lambda i: (0, 0)),
            pl.BlockSpec((width, wide), lambda i: (0, i)),
            pl.BlockSpec((width, narrow), lambda i: (0, i)),
            pl.BlockSpec((width, narrow), lambda i: (0, i)),
        ],
        out_specs=pl.BlockSpec((length, wide), lambda i: (0, i)),
        out_shape=jax.ShapeDtypeStruct((length, heads), jnp.bfloat16),
        cost_estimate=pl.CostEstimate(
            flops=2 * length * width * (heads + 2 * keys), bytes_accessed=2 * width * (length + heads + 2 * keys), transcendentals=0
        ),
    )(tokens, w_query, w_key, w_value)


def project_kernel(
    capacity, route_ref, own_ref, heads_ref, weight_ref, tokens_ref, parcel_ref, kept_ref, place_ref, flag_ref, order_ref, picked
):
    strips, strip = order_ref.shape[1], heads_ref.shape[1]
    half = strips * strip
    blocks = strips // 2
    certain = blocks - capacity
    own = own_ref[0]

    @pl.when(pl.program_id(0) == 0)
    def _():
        routes = [route_ref[index] for index in range(blocks)]
        loose_before = jnp.int32(0)
        marks = [jnp.int32(0) for _ in range(blocks - 2 * certain)]
        for index in range(blocks):
            slot = jnp.int32(0)
            for other in range(index):
                slot = slot + jnp.where(routes[other] == routes[index], 1, 0)
            for which, first in ((0, 1 - own), (1, own)):
                fixed = jnp.where(routes[index] == first, slot, capacity + slot)
                place = jnp.where(slot >= certain, certain + loose_before, fixed)
                behind = blocks + (place + blocks - certain) % blocks
                strip_at = index * 4 + first * 2
                order_ref[which, place] = strip_at
                order_ref[which, behind] = strip_at + 1
                if which == 1:
                    place_ref[0, index] = place
                    place_ref[1, index] = behind
            for mark in range(len(marks)):
                mine = (slot >= certain) & (loose_before == mark) & (routes[index] == own)
                marks[mark] = marks[mark] + jnp.where(mine, 1, 0)
            loose_before = loose_before + jnp.where(slot >= certain, 1, 0)
        for mark, found in enumerate(marks):
            flag_ref[mark * strip : (mark + 1) * strip] = jnp.full((strip, 128), found.astype(jnp.float32))
        for which in range(2):
            for index in range(strips):
                start = which * half + index * strip
                picked[start : start + strip] = heads_ref[order_ref[which, index]]

    value = jnp.dot(picked[...], weight_ref[...], preferred_element_type=jnp.float32)
    parcel_ref[...] = value[:half].astype(jnp.bfloat16)
    for index in range(strips):
        here = slice(index * strip, (index + 1) * strip)
        kept_ref[here] = value[half + index * strip : half + (index + 1) * strip] + tokens_ref[
            order_ref[1, index]
        ].astype(jnp.float32)


def projected(routes, own, heads_out, weight, tokens, strip, capacity):
    depth, width = weight.shape
    blocks = routes.shape[0]
    count = 2 * blocks * strip
    strips = heads_out.shape[0] // strip
    free = blocks - 2 * (blocks - capacity)
    tile = 1024
    piece = pl.BlockSpec((count, tile), lambda i, route, own: (0, i))
    return pl.pallas_call(
        functools.partial(project_kernel, capacity),
        grid_spec=pltpu.PrefetchScalarGridSpec(
            num_scalar_prefetch=2,
            grid=(width // tile,),
            in_specs=[
                pl.BlockSpec((strips, strip, depth), lambda i, route, own: (0, 0, 0)),
                pl.BlockSpec((depth, tile), lambda i, route, own: (0, i)),
                pl.BlockSpec((strips, strip, tile), lambda i, route, own: (0, 0, i)),
            ],
            out_specs=[
                piece,
                piece,
                pl.BlockSpec((2, blocks), lambda i, route, own: (0, 0), memory_space=pltpu.SMEM),
                pl.BlockSpec((free * strip, 128), lambda i, route, own: (0, 0)),
            ],
            scratch_shapes=[pltpu.SMEM((2, 2 * blocks), jnp.int32), pltpu.VMEM((2 * count, depth), jnp.bfloat16)],
        ),
        out_shape=(
            jax.ShapeDtypeStruct((count, width), jnp.bfloat16),
            jax.ShapeDtypeStruct((count, width), jnp.float32),
            jax.ShapeDtypeStruct((2, blocks), jnp.int32),
            jax.ShapeDtypeStruct((free * strip, 128), jnp.float32),
        ),
        cost_estimate=pl.CostEstimate(flops=4 * count * depth * width, bytes_accessed=2 * 10**7, transcendentals=0),
    )(routes, own.reshape(1), heads_out.reshape(strips, strip, depth), weight, tokens.reshape(strips, strip, width))


def finish_kernel(place_ref, route_ref, out_ref, old_ref, joined_ref, divergence_ref):
    blocks, strip = old_ref.shape[0], out_ref.shape[1]
    for block in range(blocks):
        fresh = jnp.where(route_ref[block] >= 1, 1.0, 0.0)
        for index in range(2):
            here = slice(index * strip, (index + 1) * strip)
            value = out_ref[place_ref[index, block]]
            joined_ref[block, here] = value
            gap = value.astype(jnp.float32) - old_ref[block, here].astype(jnp.float32)
            divergence_ref[block, here] = 0.5 * jnp.mean(gap * gap, axis=-1, keepdims=True) * fresh


def finished(place, routes, out, old_out, strip):
    blocks, piece, width = old_out.shape
    smem, vmem = pl.BlockSpec(memory_space=pltpu.SMEM), pl.BlockSpec(memory_space=pltpu.VMEM)
    return pl.pallas_call(
        finish_kernel,
        in_specs=[smem, smem, vmem, vmem],
        out_specs=[vmem, vmem],
        out_shape=(
            jax.ShapeDtypeStruct((blocks, piece, width), jnp.bfloat16),
            jax.ShapeDtypeStruct((blocks, piece, 1), jnp.float32),
        ),
    )(place, routes, out.reshape(-1, strip, width), old_out)


def two_experts(
    tokens, w_query, w_key, w_value, w_out, w_gate, w_up, w_down, route, old_out, cotangent
):
    own = lax.axis_index("expert")
    length, width = tokens.shape
    blocks = length // BLOCK
    piece = BLOCK // 2
    strip = piece // 2
    capacity = max(2, blocks // 2 + 1)
    certain = blocks - capacity
    free = blocks - 2 * certain
    sure, loose, rest = certain * strip, free * strip, capacity * strip
    side = blocks * strip
    routes = route[:, 0]
    outer, section = lax.axis_size("outer"), lax.axis_size("section")
    ring = []
    for line in range(outer):
        places = [line * section + place for place in range(section)]
        ring += places if line % 2 == 0 else places[::-1]
    count = len(ring)

    early = swap(w_gate[0][: w_gate.shape[1] // 2], "expert")
    heads_out = attended(tokens, w_query, w_key, w_value)
    parcel, kept, place, flag_rows = projected(routes, own, heads_out, w_out, tokens, strip, capacity)

    core = lax.axis_index("pair")
    span = width // (outer * 2)

    def part(number):
        pieces = [
            lax.dynamic_slice_in_dim(cotangent, (line * 2 + number) * span, span, axis=1) for line in range(outer)
        ]
        return jnp.concatenate(pieces, axis=1)

    left = jnp.concatenate([part(core), swap(part(1 - core), "pair")], axis=0)
    term = lax.dot_general(
        left, both(heads_out), (((0,), (0,)), ((), ())), preferred_element_type=jnp.float32
    ).astype(jnp.bfloat16)
    high, deep = width // (2 * count), term.shape[1]

    hidden_units = w_gate.shape[1]
    half = hidden_units // 2
    tiles = 4
    any_space = pl.BlockSpec(memory_space=pl.ANY)
    low = jnp.bfloat16
    dma = pltpu.SemaphoreType.DMA
    out, gradient, _, _ = pl.pallas_call(
        functools.partial(moe_kernel, sure, loose, half),
        out_shape=(
            jax.ShapeDtypeStruct((2 * side, width), low),
            jax.ShapeDtypeStruct((high, deep), jnp.float32),
            jax.ShapeDtypeStruct((3, 2, hidden_units, width), low),
            jax.ShapeDtypeStruct((2, count, high, deep // 2), low),
        ),
        in_specs=[any_space] * 8,
        out_specs=[any_space] * 4,
        scratch_shapes=[
            pltpu.VMEM((3, 2, hidden_units, width), low),
            pltpu.VMEM((count, 2 * side, width), low),
            pltpu.VMEM((count, 2 * sure, width), low),
            pltpu.VMEM((2, 2 * sure, width), low),
            pltpu.VMEM((2, 2 * rest, width), low),
            pltpu.VMEM((count, 2 * loose, width), low),
            pltpu.VMEM((count, tiles, 2 * rest, half), low),
            pltpu.VMEM((tiles, 2 * side, half), low),
            pltpu.VMEM((half, width), low),
            pltpu.VMEM((half, width), low),
            pltpu.VMEM((2, high, deep // 2), low),
            pltpu.VMEM((2, high, deep // 2), low),
            pltpu.VMEM((2, 2, high, deep // 2), low),
            pltpu.VMEM((high, deep), jnp.float32),
            pltpu.VMEM((2 * loose, width), jnp.float32),
            pltpu.VMEM((2, count, loose, 128), jnp.float32),
            dma((2, 2, count)), dma((2, 2, count)), dma((2, count)), dma((2, count)),
            dma((2, count)), dma((2, count)), dma((2, 2, count)), dma((2, 2, count)),
            dma((3,)), dma((3,)), dma((3,)), dma((3,)), dma((4,)), dma((4,)),
            dma((2, 2)), dma((2, 2)), dma((2, count)), dma((2, count)),
            dma((4,)), pltpu.SemaphoreType.REGULAR((2, 2)),
        ],
        compiler_params=pltpu.CompilerParams(
            collective_id=0, has_side_effects=True, vmem_limit_bytes=67043328
        ),
        cost_estimate=pl.CostEstimate(flops=10**11, bytes_accessed=10**8, transcendentals=0),
    )(
        parcel.reshape(-1, 2 * loose, width),
        kept.reshape(-1, 2 * loose, width),
        early,
        w_gate[0],
        w_up[0],
        w_down[0],
        term,
        flag_rows,
    )

    joined, divergence = finished(place, routes, out, old_out, strip)
    divergence = divergence.reshape(blocks, piece)
    return (joined, divergence, gradient)


def solution(mesh):
    sizes = mesh.shape
    pair = 2 if sizes["dp"] % 2 == 0 else 1
    replicas_in_ring = sizes["dp"] // pair * sizes["section"]
    body = two_experts if sizes["expert"] == 2 and pair == 2 and replicas_in_ring == 8 else per_device
    split = Mesh(
        mesh.devices.reshape(sizes["dp"] // pair, pair, sizes["section"], sizes["expert"]),
        ("outer", "pair", "section", "expert"),
    )
    replicas = ("outer", "pair", "section")
    return jax.shard_map(
        body,
        mesh=split,
        in_specs=(
            P(replicas, None),
            P(None, "expert"),
            P(None, "expert"),
            P(None, "expert"),
            P("expert", None),
            P("expert", replicas, None),
            P("expert", replicas, None),
            P("expert", replicas, None),
            P(replicas, None),
            P(replicas, "expert", None),
            P(replicas, None),
        ),
        out_specs=(
            P(replicas, "expert", None),
            P(replicas, "expert"),
            P(replicas, "expert"),
        ),
        check_vma=False,
    )
```
